32 devices in a mesh: slab: 8 (over z, y), sub: 4 (over x, core).
Axes of the slice: x: 2, y: 2, z: 4, core: 2. Of those that a mesh axis runs over, the one named last changes fastest.
Arguments:
- fine_blocks: float32 [64, 64, 64, 64], P('slab', 'sub')
- prolong: float32 [64, 64, 64], P('slab')
- smoother: float32 [64, 64, 64], P('slab')
- right_side: float32 [64, 64, 512], P('slab'), may hold values from -6 to 6
- agg_of: int32 [64], replicated, may hold values from 0 to 3, as said below
- col_slot: int32 [64, 64], P('slab', 'sub'), may hold values from 0 to 23, as said below
- send_rows: int32 [8, 4, 2, 8], replicated, may hold values from 0 to 7, as said below
- send_count: int32 [8, 4, 2], replicated, may hold values from 0 to 8, as said below
Outputs:
- coarse_op: float32 [32, 12, 64, 64], P('slab', 'sub')
- solution: float32 [64, 64, 512], P('slab', None, 'sub')
The draws below stay inside these ranges and needn't reach their ends.
Inputs may be any that keep to these rules, and one draw needn't show every extreme that they name: `agg_of`: each entry is an aggregate of the block row's own slab, numbered within the slab; every aggregate of every slab holds at least one block row. `send_rows`: each list (slab s, sub index k, direction d) holds distinct block rows of slab s numbered within the slab; direction 0 goes to slab s - 1, direction 1 to slab s + 1; only the first send_count entries are live. `send_count`: the first slab sends nothing down and the last nothing up; some list is 8 long. `col_slot`: every slot named is live; block 0 of each row names the row's own block row; some block names the last slot from each neighbour.
All inputs are finite; a program needn't handle non-finite values.
Results may differ from the reference program's by a relative error of at most 0.0003.
Values sent between devices are 32-bit elements; how exact they have to be, the bound alone decides.
No kernel may reach another device: no remote copies, remote signals or barrier semaphores. Data moves between devices by JAX's collectives and lax.ppermute only.
A program may use at most 128 MiB of HBM per device.

```python
import math
import jax
import jax.numpy as jnp
from jax import lax

DOF = 64
NNZ = 64
ROWS = 8
NRHS = 512
COARSE_SWEEPS = 3
NE = 64
NB_SUB = 16
GMAX = 8
AGG = 4
NA = 32
BAND = 12
N_SLAB = 8
N_SUB = 4


def permute_rows(one_key):
    return jax.random.permutation(one_key, ROWS).astype(jnp.int32)


def settle_groups(ids_row, order_row):
    return ids_row.at[order_row[:AGG]].set(jnp.arange(AGG, dtype=jnp.int32))


def layout(key):
    base_key = jax.random.fold_in(key, 11)
    key_first, key_second, key_perm, key_region, key_ghost, key_own, key_group, key_order = jax.random.split(base_key, 8)
    counts = jnp.minimum(jax.random.randint(key_first, (N_SLAB, N_SUB, 2), 1, GMAX + 1), jax.random.randint(key_second, (N_SLAB, N_SUB, 2), 1, GMAX + 1)).astype(jnp.int32)
    counts = counts.at[0, 0, 1].set(GMAX).at[N_SLAB - 1, 0, 0].set(GMAX)
    counts = counts.at[0, :, 0].set(0).at[N_SLAB - 1, :, 1].set(0)
    perm_keys = jax.random.split(key_perm, N_SLAB * N_SUB * 2)
    lists = jax.vmap(permute_rows)(perm_keys)[:, :GMAX].reshape(N_SLAB, N_SUB, 2, GMAX)
    slab_of = (jnp.arange(NE, dtype=jnp.int32) // ROWS)[:, None]
    element_of = (jnp.arange(NE, dtype=jnp.int32) % ROWS)[:, None]
    sub_of = (jnp.arange(NNZ, dtype=jnp.int32) // NB_SUB)[None, :]
    block_of = (jnp.arange(NNZ, dtype=jnp.int32) % NB_SUB)[None, :]
    slab_below = jnp.maximum(slab_of - 1, 0)
    slab_above = jnp.minimum(slab_of + 1, N_SLAB - 1)
    lower_count = jnp.where(slab_of > 0, counts[slab_below, sub_of, 1], 0)
    upper_count = jnp.where(slab_of < N_SLAB - 1, counts[slab_above, sub_of, 0], 0)
    region = jax.random.randint(key_region, (NE, NNZ), 0, 4)
    ghost_draw = jax.random.randint(key_ghost, (NE, NNZ), 0, 1 << 20)
    own_draw = jax.random.randint(key_own, (NE, NNZ), 0, ROWS)
    lower_slot = ROWS + ghost_draw % jnp.maximum(lower_count, 1)
    upper_slot = ROWS + GMAX + ghost_draw % jnp.maximum(upper_count, 1)
    slot_ids = jnp.where((region == 2) & (lower_count > 0), lower_slot, own_draw)
    slot_ids = jnp.where((region == 3) & (upper_count > 0), upper_slot, slot_ids)
    slot_ids = jnp.where((sub_of == 0) & (block_of == 0), element_of, slot_ids)
    slot_ids = slot_ids.at[ROWS, 1].set(ROWS + GMAX - 1)
    slot_ids = slot_ids.at[(N_SLAB - 1) * ROWS - 1, 1].set(ROWS + 2 * GMAX - 1)
    group_ids = jax.random.randint(key_group, (N_SLAB, ROWS), 0, AGG).astype(jnp.int32)
    orders = jax.vmap(permute_rows)(jax.random.split(key_order, N_SLAB))
    groups = jax.vmap(settle_groups)(group_ids, orders).reshape(NE)
    return (counts, lists, slot_ids.astype(jnp.int32), groups)


def draw_send_count(key, part):
    return layout(key)[0]


def draw_send_rows(key, part):
    return layout(key)[1]


def draw_col_slot(key, part):
    return layout(key)[2]


def draw_agg_of(key, part):
    return layout(key)[3]


def noise_draw(key, shape):
    return jax.random.normal(key, shape, jnp.float32)


def draw_fine_blocks(key, part):
    shape = (NE, NNZ, DOF, DOF)
    noise = noise_draw(key, shape)
    row_iota = lax.broadcasted_iota(jnp.int32, shape, 2)
    col_iota = lax.broadcasted_iota(jnp.int32, shape, 3)
    block_iota = lax.broadcasted_iota(jnp.int32, shape, 1)
    diagonal = ((row_iota == col_iota) & (block_iota == 0)).astype(jnp.float32)
    return 4.0 * diagonal + noise * (0.25 / math.sqrt(DOF))


def draw_prolong(key, part):
    shape = (NE, DOF, DOF)
    noise = noise_draw(key, shape)
    diagonal = (lax.broadcasted_iota(jnp.int32, shape, 1) == lax.broadcasted_iota(jnp.int32, shape, 2)).astype(jnp.float32)
    return diagonal + noise * (0.32 / math.sqrt(DOF))


def draw_smoother(key, part):
    shape = (NE, DOF, DOF)
    noise = noise_draw(key, shape)
    diagonal = (lax.broadcasted_iota(jnp.int32, shape, 1) == lax.broadcasted_iota(jnp.int32, shape, 2)).astype(jnp.float32)
    return 0.25 * diagonal + noise * (0.08 / math.sqrt(DOF))


def shard_levels(stream_key, shape, cuts, low, top_value):
    level, own = 1.0, jax.random.fold_in(stream_key, 6)
    for position, parts in cuts:
        steps = jnp.exp(jax.random.uniform(jax.random.fold_in(own, position), (parts,), jnp.float32, low / len(cuts), top_value / len(cuts)))
        level = level * jnp.repeat(steps, shape[position] // parts).reshape([-1 if axis == position else 1 for axis in range(len(shape))])
    return level


def gaussian(stream_key, shape, deviation, bound, cuts=(), kind=jnp.bfloat16):
    loudness = shard_levels(stream_key, shape, cuts, -0.22, 0.18) if cuts else 1.0
    array = jax.random.normal(stream_key, shape, jnp.float32) * deviation * loudness
    return jnp.minimum(jnp.maximum(array, -bound), bound).astype(kind)


def setup_inputs(seed: int = 0) -> dict:
    seeds = jax.random.split(jax.random.key(seed), 9)
    fine_blocks = draw_fine_blocks(jax.random.fold_in(seeds[8], 71), 0)
    prolong = draw_prolong(jax.random.fold_in(seeds[8], 71), 0)
    smoother = draw_smoother(jax.random.fold_in(seeds[8], 71), 0)
    right_side = gaussian(seeds[3], (NE, DOF, NRHS), 1.0, 6.0, ((0, 8),), jnp.float32)
    agg_of = draw_agg_of(jax.random.fold_in(seeds[8], 71), 0)
    col_slot = draw_col_slot(jax.random.fold_in(seeds[8], 71), 0)
    send_rows = draw_send_rows(jax.random.fold_in(seeds[8], 71), 0)
    send_count = draw_send_count(jax.random.fold_in(seeds[8], 71), 0)
    return dict(fine_blocks=fine_blocks, prolong=prolong, smoother=smoother, right_side=right_side, agg_of=agg_of, col_slot=col_slot, send_rows=send_rows, send_count=send_count)


highest = lax.Precision.HIGHEST
coarse_weight = 0.25


def slot_tables(agg_of, send_rows, send_count):
    slab_ids = jnp.arange(N_SLAB, dtype=jnp.int32)
    slab_below = jnp.maximum(slab_ids - 1, 0)
    slab_above = jnp.minimum(slab_ids + 1, N_SLAB - 1)
    own_rows = slab_ids[:, None, None] * ROWS + jnp.zeros((1, N_SUB, 1), jnp.int32) + jnp.arange(ROWS, dtype=jnp.int32)[None, None, :]
    lower_rows = slab_below[:, None, None] * ROWS + send_rows[slab_below][:, :, 1, :]
    upper_rows = slab_above[:, None, None] * ROWS + send_rows[slab_above][:, :, 0, :]
    places = jnp.arange(GMAX, dtype=jnp.int32)[None, None, :]
    lower_live = (places < send_count[slab_below][:, :, 1][:, :, None]) & (slab_ids > 0)[:, None, None]
    upper_live = (places < send_count[slab_above][:, :, 0][:, :, None]) & (slab_ids < N_SLAB - 1)[:, None, None]
    element_table = jnp.concatenate([own_rows, lower_rows, upper_rows], axis=2)
    band_table = jnp.concatenate([agg_of[own_rows] + AGG, agg_of[lower_rows], agg_of[upper_rows] + 2 * AGG], axis=2)
    live_table = jnp.concatenate([own_rows >= 0, lower_live, upper_live], axis=2)
    return element_table, band_table, live_table


def column_maps(agg_of, col_slot, send_rows, send_count):
    element_table, band_table, live_table = slot_tables(agg_of, send_rows, send_count)
    slot_width = ROWS + 2 * GMAX
    slab_of = (jnp.arange(NE, dtype=jnp.int32) // ROWS)[:, None]
    sub_of = (jnp.arange(NNZ, dtype=jnp.int32) // NB_SUB)[None, :]
    flat_index = (slab_of * N_SUB + sub_of) * slot_width + col_slot
    col_element = element_table.reshape(-1)[flat_index]
    col_band = band_table.reshape(-1)[flat_index]
    col_live = live_table.reshape(-1)[flat_index].astype(jnp.float32)
    return col_element, col_band, col_live


def coarse_rows(fine_blocks, prolong, agg_of, col_element, col_band, col_live):
    group_ids = jnp.arange(AGG, dtype=jnp.int32)
    band_ids = jnp.arange(BAND, dtype=jnp.int32)

    def one_slab(pieces):
        blocks_here, prolong_here, groups_here, element_here, band_here, live_here = pieces
        picked = prolong[element_here] * live_here[:, :, None, None]
        products = jnp.einsum("ejab,ejbc->ejac", blocks_here, picked, precision=highest)
        term_blocks = jnp.einsum("eba,ejbc->ejac", prolong_here, products, precision=highest)
        row_hot = (groups_here[:, None] == group_ids[None, :]).astype(jnp.float32)
        col_hot = (band_here[:, :, None] == band_ids[None, None, :]).astype(jnp.float32)
        return jnp.einsum("ea,ejq,ejxy->aqxy", row_hot, col_hot, term_blocks, precision=highest)

    stacked = lax.map(one_slab, (fine_blocks.reshape(N_SLAB, ROWS, NNZ, DOF, DOF), prolong.reshape(N_SLAB, ROWS, DOF, DOF), agg_of.reshape(N_SLAB, ROWS), col_element.reshape(N_SLAB, ROWS, NNZ), col_band.reshape(N_SLAB, ROWS, NNZ), col_live.reshape(N_SLAB, ROWS, NNZ)))
    return stacked.reshape(NA, BAND, DOF, DOF)


def apply_operator(fine_blocks, field_rows, col_element, col_live):
    def one_slab(pieces):
        blocks_here, element_here, live_here = pieces
        picked = field_rows[element_here] * live_here[:, :, None, None]
        return jnp.einsum("ejab,ejbn->ean", blocks_here, picked, precision=highest)

    stacked = lax.map(one_slab, (fine_blocks.reshape(N_SLAB, ROWS, NNZ, DOF, DOF), col_element.reshape(N_SLAB, ROWS, NNZ), col_live.reshape(N_SLAB, ROWS, NNZ)))
    return stacked.reshape(NE, DOF, NRHS)


def coarse_apply(coarse_op, vector):
    vector_blocks = vector.reshape(N_SLAB, AGG, DOF, NRHS)
    zero_rows = jnp.zeros((1, AGG, DOF, NRHS), vector.dtype)
    padded = jnp.concatenate([zero_rows, vector_blocks, zero_rows], axis=0)
    widened = jnp.concatenate([padded[:-2], padded[1:-1], padded[2:]], axis=1)
    result = jnp.einsum("saqxy,sqyn->saxn", coarse_op.reshape(N_SLAB, AGG, BAND, DOF, DOF), widened, precision=highest)
    return result.reshape(NA, DOF, NRHS)


def reference(fine_blocks, prolong, smoother, right_side, agg_of, col_slot, send_rows, send_count):
    col_element, col_band, col_live = column_maps(agg_of, col_slot, send_rows, send_count)
    coarse_op = coarse_rows(fine_blocks, prolong, agg_of, col_element, col_band, col_live)
    row_hot = (agg_of.reshape(N_SLAB, ROWS)[:, :, None] == jnp.arange(AGG, dtype=jnp.int32)[None, None, :]).astype(jnp.float32)
    weight = (coarse_weight / jnp.sum(row_hot, axis=1)).reshape(NA, 1, 1)
    prolong_slabs = prolong.reshape(N_SLAB, ROWS, DOF, DOF)
    x_first = jnp.einsum("eab,ebn->ean", smoother, right_side, precision=highest)
    residual = right_side - apply_operator(fine_blocks, x_first, col_element, col_live)
    coarse_rhs = jnp.einsum("sea,sedc,sedn->sacn", row_hot, prolong_slabs, residual.reshape(N_SLAB, ROWS, DOF, NRHS), precision=highest).reshape(NA, DOF, NRHS)
    correction = weight * coarse_rhs
    for sweep_index in range(COARSE_SWEEPS - 1):
        correction = correction + weight * (coarse_rhs - coarse_apply(coarse_op, correction))
    lifted = jnp.einsum("sea,sedc,sacn->sedn", row_hot, prolong_slabs, correction.reshape(N_SLAB, AGG, DOF, NRHS), precision=highest)
    x_second = x_first + lifted.reshape(NE, DOF, NRHS)
    image_next = apply_operator(fine_blocks, x_second, col_element, col_live)
    solution = x_second + jnp.einsum("eab,ebn->ean", smoother, right_side - image_next, precision=highest)
    return coarse_op, solution
```

```python
import functools
import jax
import jax.numpy as jnp
from jax import lax
from jax.experimental import pallas as pl
from jax.experimental.pallas import tpu as pltpu
from jax.sharding import PartitionSpec as P

COARSE_SWEEPS = 3
COARSE_WEIGHT = 0.25
F32 = jnp.float32
BF16 = jnp.bfloat16
VMEM = pl.BlockSpec(memory_space=pltpu.VMEM)
SMEM = pl.BlockSpec(memory_space=pltpu.SMEM)
ROWS = 8
GHOSTS = 8
SLOTS = ROWS + 2 * GHOSTS
GROUPS = 4
BANDS = 3 * GROUPS
DOF = 64
COLS = 128

AT_SUB = 0
AT_COL = 8
AT_LIVE = AT_COL + SLOTS
AT_AGG = AT_LIVE + SLOTS


def params(limit=48):
    return pltpu.CompilerParams(vmem_limit_bytes=limit << 20)


def halves(value):
    high = value.astype(BF16)
    return high, (value - high.astype(F32)).astype(BF16)


def mm(a, b):
    return jnp.dot(a, b, preferred_element_type=F32)


def product(left, right):
    left_high, left_low = left
    right_high, right_low = right
    return mm(left_high, right_high) + (mm(left_high, right_low) + mm(left_low, right_high))


def rows_of(index, size=DOF):
    return slice(index * size, (index + 1) * size)


def first_kernel(meta, smoother, right_own, right_other, prolong, x_ref, packed_ref):
    for e in range(ROWS):
        right = jnp.concatenate([right_own[e], right_other[e]], axis=1)
        x_ref[rows_of(e), :] = product(halves(smoother[e]), halves(right))
    for e in range(ROWS // 2):
        packed_ref[rows_of(e), :] = jnp.concatenate([prolong[e], prolong[e + ROWS // 2]], axis=1)


def first_step(meta, smoother, right_side, prolong):
    whole = lambda shape: pl.BlockSpec(shape, lambda i, meta: (0,) * len(shape))
    chunk = (ROWS, DOF, COLS)
    return pl.pallas_call(
        first_kernel,
        grid_spec=pltpu.PrefetchScalarGridSpec(
            num_scalar_prefetch=1,
            grid=(1,),
            in_specs=[
                whole(smoother.shape),
                pl.BlockSpec(chunk, lambda i, meta: (0, 0, meta[AT_SUB])),
                pl.BlockSpec(chunk, lambda i, meta: (0, 0, meta[AT_SUB + 1])),
                whole(prolong.shape),
            ],
            out_specs=[whole((ROWS * DOF, 2 * COLS)), whole((ROWS * DOF // 2, 2 * DOF))],
        ),
        out_shape=[
            jax.ShapeDtypeStruct((ROWS * DOF, 2 * COLS), F32),
            jax.ShapeDtypeStruct((ROWS * DOF // 2, 2 * DOF), F32),
        ],
        compiler_params=params(),
        name="first_step",
    )(meta, smoother, right_side, right_side, prolong)


def build_kernel(meta, col_slot, blocks, d_ref):
    row = pl.program_id(0)
    d_ref[...] = jnp.zeros_like(d_ref)
    upper = lax.broadcasted_iota(jnp.int32, (DOF, 2 * DOF), 1) >= DOF
    for j in range(blocks.shape[1]):
        slot = col_slot[row, j]
        column = meta[AT_COL + slot]
        live = meta[AT_LIVE + slot].astype(F32)
        block = blocks[0, j]
        doubled = jnp.concatenate([block, block], axis=1)
        odd = lax.rem(column, 2)
        lower_scale = jnp.where(odd == 0, live, 0.0)
        upper_scale = jnp.where(odd == 1, live, 0.0)
        placed = doubled * jnp.where(upper, upper_scale, lower_scale)
        lanes = pl.ds(pl.multiple_of(lax.div(column, 2) * 2 * DOF, 2 * DOF), 2 * DOF)
        d_ref[:, lanes] += placed


def build(meta, col_slot, blocks):
    per_row = blocks.shape[1]
    return pl.pallas_call(
        build_kernel,
        grid=(ROWS,),
        in_specs=[SMEM, SMEM, pl.BlockSpec((1, per_row, DOF, DOF), lambda e: (e, 0, 0, 0))],
        out_specs=pl.BlockSpec((DOF, SLOTS * DOF), lambda e: (e, 0)),
        out_shape=jax.ShapeDtypeStruct((ROWS * DOF, SLOTS * DOF), F32),
        compiler_params=params(),
        name="build",
    )(meta, col_slot, blocks)


def galerkin_kernel(
    meta, d_own, d_other, prolong, below, above, high_ref, low_ref, half_ref, rt_high, rt_low, q_high, q_low
):
    step = pl.program_id(0)
    band_start = meta[AT_SUB + 2] * (BANDS // 2)
    upper = lax.broadcasted_iota(jnp.int32, (DOF, 2 * DOF), 1) >= DOF

    @pl.when(step == 0)
    def _():
        for c in range(SLOTS):
            if c < ROWS:
                piece = jnp.concatenate([prolong[c], prolong[c]], axis=1)
            else:
                packed = below if c < 2 * ROWS else above
                r = c % ROWS
                both = packed[rows_of(r % (ROWS // 2)), :]
                piece = both[:, :DOF] if r < ROWS // 2 else both[:, DOF:]
                piece = jnp.concatenate([piece, piece], axis=1)
            region = (GROUPS, 0, 2 * GROUPS)[c // ROWS]
            band = meta[AT_AGG + c] + region - band_start
            for t in range(BANDS // 4):
                lower_scale = jnp.where(band == 2 * t, 1.0, 0.0)
                upper_scale = jnp.where(band == 2 * t + 1, 1.0, 0.0)
                high, low = halves(piece * jnp.where(upper, upper_scale, lower_scale))
                q_high[rows_of(c), rows_of(t, 2 * DOF)] = high
                q_low[rows_of(c), rows_of(t, 2 * DOF)] = low
        restrict_rows = []
        for e in range(ROWS):
            piece = jnp.concatenate([prolong[e], prolong[e]], axis=1)
            group = meta[AT_AGG + e]
            parts = []
            for t in range(GROUPS // 2):
                lower_scale = jnp.where(group == 2 * t, 1.0, 0.0)
                upper_scale = jnp.where(group == 2 * t + 1, 1.0, 0.0)
                parts.append(piece * jnp.where(upper, upper_scale, lower_scale))
            restrict_rows.append(jnp.concatenate(parts, axis=1))
        high, low = halves(jnp.concatenate(restrict_rows, axis=0).T)
        rt_high[...] = high
        rt_low[...] = low

    high, low = halves(d_own[...] + d_other[...])
    high_ref[...] = high
    low_ref[...] = low
    half_ref[...] = product((high, low), (q_high[...], q_low[...]))


def galerkin(meta, d_own, d_other, prolong, below, above):
    rows, wide = d_own.shape
    steps = 2
    half = BANDS // 2 * DOF
    whole = lambda array: pl.BlockSpec(array.shape, lambda i: (0,) * array.ndim)
    part = lambda width: pl.BlockSpec((rows // steps, width), lambda i: (i, 0))
    restrict_shape = (GROUPS * DOF, rows)
    restrict = pl.BlockSpec(restrict_shape, lambda i: (0, 0))
    return pl.pallas_call(
        galerkin_kernel,
        grid=(steps,),
        in_specs=[SMEM, part(wide), part(wide), whole(prolong), whole(below), whole(above)],
        out_specs=[part(wide), part(wide), part(half), restrict, restrict],
        out_shape=[
            jax.ShapeDtypeStruct((rows, wide), BF16),
            jax.ShapeDtypeStruct((rows, wide), BF16),
            jax.ShapeDtypeStruct((rows, half), F32),
            jax.ShapeDtypeStruct(restrict_shape, BF16),
            jax.ShapeDtypeStruct(restrict_shape, BF16),
        ],
        scratch_shapes=[pltpu.VMEM((wide, half), BF16), pltpu.VMEM((wide, half), BF16)],
        compiler_params=params(),
        name="galerkin",
    )(meta, d_own, d_other, prolong, below, above)


def image_kernel(d_high, d_low, own, below, above, keep_ref, send_ref):
    total = None
    for region, field in enumerate((own, below, above)):
        lanes = rows_of(region, ROWS * DOF)
        part = product((d_high[:, lanes], d_low[:, lanes]), halves(field[...]))
        total = part if total is None else total + part
    keep_ref[...] = total[:, :COLS]
    send_ref[...] = total[:, COLS:]


def image(d_high, d_low, own, below, above):
    shape = jax.ShapeDtypeStruct((d_high.shape[0], COLS), F32)
    return pl.pallas_call(
        image_kernel,
        in_specs=[VMEM] * 5,
        out_specs=[VMEM] * 2,
        out_shape=[shape, shape],
        compiler_params=params(),
        name="image",
    )(d_high, d_low, own, below, above)


def scaled_by_weight(meta, value):
    pieces = []
    for a in range(GROUPS):
        members = jnp.zeros((), jnp.int32)
        for e in range(ROWS):
            members += jnp.where(meta[AT_AGG + e] == a, 1, 0)
        piece = value[rows_of(a), :]
        pieces.append(piece * (COARSE_WEIGHT / jnp.full(piece.shape, members.astype(F32))))
    return jnp.concatenate(pieces, axis=0)


def coarse_kernel(meta, rt_high, rt_low, mine, other, g_high, g_low, m_high, m_low, op_ref):
    core = meta[AT_SUB + 2]
    sub = meta[AT_SUB]
    half = mine.shape[1]
    own_value, other_value = mine[...], other[...]
    is_first = core == 0
    left = jnp.where(is_first, own_value, other_value)
    right = jnp.where(is_first, other_value, own_value)
    for position, value in enumerate((left, right)):
        lanes = rows_of(position, half)
        high, low = halves(value)
        g_high[:, lanes] = high
        g_low[:, lanes] = low
        coarse = product((rt_high[...], rt_low[...]), (high, low))
        high, low = halves(scaled_by_weight(meta, coarse))
        m_high[:, lanes] = high
        m_low[:, lanes] = low
        per_half = op_ref.shape[1]
        for place in range(2):

            @pl.when(sub == 2 * position + place)
            def _():
                for a in range(GROUPS):
                    for q in range(per_half):
                        op_ref[a, q] = coarse[rows_of(a), rows_of(place * per_half + q)]


def coarse_operator(meta, rt_high, rt_low, mine, other):
    rows, half = mine.shape
    field = lambda n, t: jax.ShapeDtypeStruct((n, 2 * half), t)
    return pl.pallas_call(
        coarse_kernel,
        in_specs=[SMEM] + [VMEM] * 4,
        out_specs=[VMEM] * 5,
        out_shape=[
            field(rows, BF16),
            field(rows, BF16),
            field(GROUPS * DOF, BF16),
            field(GROUPS * DOF, BF16),
            jax.ShapeDtypeStruct((GROUPS, BANDS // 4, DOF, DOF), F32),
        ],
        compiler_params=params(),
        name="coarse_operator",
    )(meta, rt_high, rt_low, mine, other)


def residual_kernel(meta, right, keep, received, rt_high, rt_low, residual_ref, first_ref):
    residual = right[...].reshape(keep.shape) - (keep[...] + received[...])
    residual_ref[...] = residual
    coarse_rhs = product((rt_high[...], rt_low[...]), halves(residual))
    first_ref[...] = scaled_by_weight(meta, coarse_rhs)


def residual_step(meta, right_side, keep, received, rt_high, rt_low):
    whole = lambda shape: pl.BlockSpec(shape, lambda i, meta: (0,) * len(shape))
    coarse_shape = (rt_high.shape[0], COLS)
    return pl.pallas_call(
        residual_kernel,
        grid_spec=pltpu.PrefetchScalarGridSpec(
            num_scalar_prefetch=1,
            grid=(1,),
            in_specs=[
                pl.BlockSpec((ROWS, DOF, COLS), lambda i, meta: (0, 0, meta[AT_SUB])),
                whole(keep.shape),
                whole(keep.shape),
                whole(rt_high.shape),
                whole(rt_high.shape),
            ],
            out_specs=[whole(keep.shape), whole(coarse_shape)],
        ),
        out_shape=[jax.ShapeDtypeStruct(keep.shape, F32), jax.ShapeDtypeStruct(coarse_shape, F32)],
        compiler_params=params(),
        name="residual_step",
    )(meta, right_side, keep, received, rt_high, rt_low)


def applied(op_high, op_low, below, own, above):
    total = None
    for region, field in enumerate((below, own, above)):
        lanes = rows_of(region, GROUPS * DOF)
        part = product((op_high[:, lanes], op_low[:, lanes]), halves(field[...]))
        total = part if total is None else total + part
    return total


def sweep_kernel(m_high, m_low, first, below, own, above, next_ref):
    next_ref[...] = own[...] + first[...] - applied(m_high, m_low, below, own, above)


def sweep(m_high, m_low, first, below, own, above):
    return pl.pallas_call(
        sweep_kernel,
        in_specs=[VMEM] * 6,
        out_specs=VMEM,
        out_shape=jax.ShapeDtypeStruct(own.shape, F32),
        compiler_params=params(),
        name="sweep",
    )(m_high, m_low, first, below, own, above)


def last_kernel(meta, g_high, g_low, prolong, smoother, x_first, residual, below, own, above, out_ref):
    remaining = residual[...] - applied(g_high, g_low, below, own, above)
    for e in range(ROWS):
        group = meta[AT_AGG + e]
        correction = own[pl.ds(pl.multiple_of(group * DOF, DOF), DOF), :]
        out_ref[e] = (
            x_first[rows_of(e), :COLS]
            + product(halves(prolong[e]), halves(correction))
            + product(halves(smoother[e]), halves(remaining[rows_of(e), :]))
        )


def last_step(meta, g_high, g_low, prolong, smoother, x_first, residual, below, own, above):
    return pl.pallas_call(
        last_kernel,
        in_specs=[SMEM] + [VMEM] * 9,
        out_specs=VMEM,
        out_shape=jax.ShapeDtypeStruct((ROWS, DOF, COLS), F32),
        compiler_params=params(),
        name="last_step",
    )(meta, g_high, g_low, prolong, smoother, x_first, residual, below, own, above)


def from_neighbours(value):
    size = lax.axis_size("slab")
    up = [(i, i + 1) for i in range(size - 1)]
    down = [(i + 1, i) for i in range(size - 1)]
    return lax.ppermute(value, "slab", up), lax.ppermute(value, "slab", down)


def swapped(value, bit):
    size = lax.axis_size("sub")
    return lax.ppermute(value, "sub", [(i, i ^ bit) for i in range(size)])


def scalars(agg_of, send_rows, send_count):
    slab = lax.axis_index("slab")
    sub = lax.axis_index("sub")
    size = lax.axis_size("slab")
    below = jnp.maximum(slab - 1, 0)
    above = jnp.minimum(slab + 1, size - 1)
    own = jnp.arange(ROWS, dtype=jnp.int32)
    places = jnp.arange(GHOSTS, dtype=jnp.int32)
    lower_live = (places < send_count[below, sub, 1]) & (slab > 0)
    upper_live = (places < send_count[above, sub, 0]) & (slab < size - 1)
    rows_at = lambda which: lax.dynamic_slice_in_dim(agg_of, which * ROWS, ROWS)
    head = jnp.stack([sub, sub ^ 2, sub & 1, slab, slab, slab, slab, slab]).astype(jnp.int32)
    return jnp.concatenate(
        [
            head,
            own,
            ROWS + send_rows[below, sub, 1],
            2 * ROWS + send_rows[above, sub, 0],
            jnp.ones((ROWS,), jnp.int32),
            lower_live.astype(jnp.int32),
            upper_live.astype(jnp.int32),
            rows_at(slab),
            rows_at(below),
            rows_at(above),
        ]
    )


def per_device(fine_blocks, prolong, smoother, right_side, agg_of, col_slot, send_rows, send_count):
    meta = scalars(agg_of, send_rows, send_count)
    x_first, packed = first_step(meta, smoother, right_side, prolong)
    packed_below, packed_above = from_neighbours(packed)
    x_below, x_above = from_neighbours(x_first)
    d_own = build(meta, col_slot, fine_blocks)
    d_other = swapped(d_own, 1)
    d_high, d_low, half, rt_high, rt_low = galerkin(meta, d_own, d_other, prolong, packed_below, packed_above)
    half = half + swapped(half, 2)
    g_high, g_low, m_high, m_low, coarse_op = coarse_operator(meta, rt_high, rt_low, half, swapped(half, 1))
    keep, send = image(d_high, d_low, x_first, x_below, x_above)
    residual, first = residual_step(meta, right_side, keep, swapped(send, 2), rt_high, rt_low)
    correction = first
    for _ in range(COARSE_SWEEPS - 1):
        below, above = from_neighbours(correction)
        correction = sweep(m_high, m_low, first, below, correction, above)
    below, above = from_neighbours(correction)
    solution = last_step(meta, g_high, g_low, prolong, smoother, x_first, residual, below, correction, above)
    return coarse_op, solution


def solution(mesh):
    placed = (
        P("slab", "sub", None, None),
        P("slab", None, None),
        P("slab", None, None),
        P("slab", None, None),
        P(),
        P("slab", "sub"),
        P(),
        P(),
    )
    return jax.shard_map(
        per_device,
        mesh=mesh,
        in_specs=placed,
        out_specs=(P("slab", "sub", None, None), P("slab", None, "sub")),
        check_vma=False,
    )
```

```python
import functools
import jax
import jax.numpy as jnp
from jax import lax
from jax.experimental import pallas as pl
from jax.experimental.pallas import tpu as pltpu
from jax.sharding import PartitionSpec as P

COARSE_SWEEPS = 3
COARSE_WEIGHT = 0.25
F32 = jnp.float32
BF16 = jnp.bfloat16
VMEM = pl.BlockSpec(memory_space=pltpu.VMEM)
SMEM = pl.BlockSpec(memory_space=pltpu.SMEM)
ANY = pl.BlockSpec(memory_space=pl.ANY)
ROWS = 8
GHOSTS = 8
SLOTS = ROWS + 2 * GHOSTS
GROUPS = 4
BANDS = 3 * GROUPS
DOF = 64
COLS = 128
SUBS = 4


def params(limit=48):
    return pltpu.CompilerParams(vmem_limit_bytes=limit << 20)


def halves(value):
    high = value.astype(BF16)
    return high, (value - high.astype(F32)).astype(BF16)


def mm(a, b):
    return jnp.dot(a, b, preferred_element_type=F32)


def product(left, right):
    left_high, left_low = left
    right_high, right_low = right
    return mm(left_high, right_high) + (mm(left_high, right_low) + mm(left_low, right_high))


def rows_of(index, size=DOF):
    return slice(index * size, (index + 1) * size)


def place_of(slab, size):
    odd = slab & 1
    near = jnp.minimum(slab ^ 1, size - 1)
    far = jnp.where(odd == 1, jnp.minimum(slab + 1, size - 1), jnp.maximum(slab - 1, 0))
    return odd, near, far


def here():
    slab = lax.axis_index("slab")
    return slab, lax.axis_size("slab"), lax.axis_index("sub")


def start_kernel(
    col_slot, rows_hbm, counts_hbm, blocks, smoother, right_side, prolong,
    d_ref, x_ref, packed_ref, rows, counts, sems, *parts
):
    step = pl.program_id(0)
    slab, size, sub = here()
    below = jnp.maximum(slab - 1, 0)
    above = jnp.minimum(slab + 1, size - 1)

    @pl.when(step == 0)
    def _():
        copies = [
            pltpu.make_async_copy(rows_hbm.at[below, sub], rows.at[0], sems.at[0]),
            pltpu.make_async_copy(rows_hbm.at[above, sub], rows.at[1], sems.at[1]),
            pltpu.make_async_copy(counts_hbm.at[below], counts.at[0], sems.at[2]),
            pltpu.make_async_copy(counts_hbm.at[above], counts.at[1], sems.at[3]),
        ]
        for copy in copies:
            copy.start()
        start = (sub & 1) * (ROWS // 2)
        packed_ref[...] = jnp.concatenate([prolong[start + i] for i in range(ROWS // 2)], axis=1)
        for copy in copies:
            copy.wait()

    own = pl.ds(pl.multiple_of(sub * COLS, COLS), COLS)
    other = pl.ds(pl.multiple_of((sub ^ 2) * COLS, COLS), COLS)
    for e in range(len(parts)):
        right = jnp.concatenate([right_side[e, :, own], right_side[e, :, other]], axis=1)
        x_ref[rows_of(e), :] = product(halves(smoother[e]), halves(right))
    lower_count = jnp.where(slab > 0, counts[0, sub, 1], 0)
    upper_count = jnp.where(slab < size - 1, counts[1, sub, 0], 0)
    odd = slab & 1
    lower_start = (2 - odd) * ROWS
    upper_start = (1 + odd) * ROWS
    upper_lanes = lax.broadcasted_iota(jnp.int32, (DOF, 2 * DOF), 1) >= DOF
    for part in parts:
        part[...] = jnp.zeros_like(part)
    for j in range(blocks.shape[1]):
        for position, part in enumerate(parts):
            slot = col_slot[step * len(parts) + position, j]
            ghost = jnp.maximum(slot - ROWS, 0)
            is_own = slot < ROWS
            is_upper = slot >= ROWS + GHOSTS
            side = jnp.where(is_upper, 1, 0)
            at = jnp.where(is_upper, ghost - GHOSTS, ghost)
            at = jnp.where(is_own, 0, at)
            listed = rows[side, 1 - side, at] + jnp.where(is_upper, upper_start, lower_start)
            column = jnp.where(is_own, slot, listed)
            count = jnp.where(is_upper, upper_count, lower_count)
            live = jnp.where(is_own | (at < count), 1.0, 0.0)
            block = blocks[position, j]
            doubled = jnp.concatenate([block, block], axis=1)
            odd_column = column & 1
            lower_scale = jnp.where(odd_column == 0, live, 0.0)
            upper_scale = jnp.where(odd_column == 1, live, 0.0)
            placed = doubled * jnp.where(upper_lanes, upper_scale, lower_scale)
            lanes = pl.ds(pl.multiple_of((column >> 1) * 2 * DOF, 2 * DOF), 2 * DOF)
            part[:, lanes] += placed
    for position, part in enumerate(parts):
        d_ref[rows_of(position), :] = part[...]


def start_step(col_slot, send_rows, send_count, blocks, smoother, right_side, prolong):
    per_row, columns = blocks.shape[1], right_side.shape[2]
    at_once = 4
    by_rows = lambda *shape: pl.BlockSpec((at_once,) + shape, lambda e: (e,) + (0,) * len(shape))
    return pl.pallas_call(
        start_kernel,
        grid=(ROWS // at_once,),
        in_specs=[
            SMEM,
            ANY,
            ANY,
            by_rows(per_row, DOF, DOF),
            by_rows(DOF, DOF),
            by_rows(DOF, columns),
            pl.BlockSpec(prolong.shape, lambda e: (0, 0, 0)),
        ],
        out_specs=[
            pl.BlockSpec((at_once * DOF, SLOTS * DOF), lambda e: (e, 0)),
            pl.BlockSpec((at_once * DOF, 2 * COLS), lambda e: (e, 0)),
            pl.BlockSpec((DOF, 2 * COLS), lambda e: (0, 0)),
        ],
        out_shape=[
            jax.ShapeDtypeStruct((ROWS * DOF, SLOTS * DOF), F32),
            jax.ShapeDtypeStruct((ROWS * DOF, 2 * COLS), F32),
            jax.ShapeDtypeStruct((DOF, 2 * COLS), F32),
        ],
        scratch_shapes=[
            pltpu.SMEM((2, 2, GHOSTS), jnp.int32),
            pltpu.SMEM((2, SUBS, 2), jnp.int32),
            pltpu.SemaphoreType.DMA((4,)),
        ]
        + [pltpu.VMEM((DOF, SLOTS * DOF), F32)] * at_once,
        compiler_params=params(),
        name="start_step",
    )(col_slot, send_rows, send_count, blocks, smoother, right_side, prolong)


def placed_pairs(piece, index, count):
    upper = lax.broadcasted_iota(jnp.int32, (DOF, 2 * DOF), 1) >= DOF
    doubled = jnp.concatenate([piece, piece], axis=1)
    for t in range(count):
        lower_scale = jnp.where(index == 2 * t, 1.0, 0.0)
        upper_scale = jnp.where(index == 2 * t + 1, 1.0, 0.0)
        yield t, doubled * jnp.where(upper, upper_scale, lower_scale)


def own_kernel(
    agg_of, d_own, d_other, prolong, own, high_ref, low_ref, half_ref, image_ref, rt_high, rt_low, q_high, q_low
):
    step = pl.program_id(0)
    slab, size, sub = here()
    band_start = (sub & 1) * (BANDS // 2)

    @pl.when(step == 0)
    def _():
        restrict_rows = []
        for e in range(ROWS):
            group = agg_of[slab * ROWS + e]
            for t, value in placed_pairs(prolong[e], group + GROUPS - band_start, BANDS // 4):
                high, low = halves(value)
                q_high[rows_of(e), rows_of(t, 2 * DOF)] = high
                q_low[rows_of(e), rows_of(t, 2 * DOF)] = low
            parts = [value for _, value in placed_pairs(prolong[e], group, GROUPS // 2)]
            restrict_rows.append(jnp.concatenate(parts, axis=1))
        high, low = halves(jnp.concatenate(restrict_rows, axis=0).T)
        rt_high[...] = high
        rt_low[...] = low

    high, low = halves(d_own[...] + d_other[...])
    high_ref[...] = high
    low_ref[...] = low
    width = ROWS * DOF
    pair = (high[:, :width], low[:, :width])
    half_ref[...] = product(pair, (q_high[...], q_low[...]))
    image_ref[...] = product(pair, halves(own[...]))


def own_step(agg_of, d_own, d_other, prolong, x_message):
    rows, wide = d_own.shape
    steps = 2
    half = BANDS // 2 * DOF
    whole = lambda shape: pl.BlockSpec(shape, lambda i: (0,) * len(shape))
    part = lambda width: pl.BlockSpec((rows // steps, width), lambda i: (i, 0))
    restrict_shape = (GROUPS * DOF, rows)
    return pl.pallas_call(
        own_kernel,
        grid=(steps,),
        in_specs=[SMEM, part(wide), part(wide), whole(prolong.shape), whole((rows, 2 * COLS))],
        out_specs=[part(wide), part(wide), part(half), part(2 * COLS)] + [whole(restrict_shape)] * 2,
        out_shape=[
            jax.ShapeDtypeStruct((rows, wide), BF16),
            jax.ShapeDtypeStruct((rows, wide), BF16),
            jax.ShapeDtypeStruct((rows, half), F32),
            jax.ShapeDtypeStruct((rows, 2 * COLS), F32),
            jax.ShapeDtypeStruct(restrict_shape, BF16),
            jax.ShapeDtypeStruct(restrict_shape, BF16),
        ],
        scratch_shapes=[pltpu.VMEM((rows, half), BF16), pltpu.VMEM((rows, half), BF16)],
        compiler_params=params(),
        name="own_step",
    )(agg_of, d_own, d_other, prolong, x_message)


def ghost_lanes(side):
    return rows_of(1 + side, ROWS * DOF)


def image_kernel(d_high, d_low, own_image, near, far, keep_ref, send_ref):
    rows = own_image.shape[0]
    for place, target in ((1, send_ref), (0, keep_ref)):
        columns = rows_of(place, COLS)
        total = own_image[:, columns]
        for side, message in enumerate((near, far)):
            lanes = ghost_lanes(side)
            total += product((d_high[:, lanes], d_low[:, lanes]), halves(message[:rows, columns]))
        target[...] = total


def image(d_high, d_low, own_image, near, far):
    shape = jax.ShapeDtypeStruct((d_high.shape[0], COLS), F32)
    return pl.pallas_call(
        image_kernel,
        in_specs=[VMEM] * 5,
        out_specs=[VMEM] * 2,
        out_shape=[shape, shape],
        compiler_params=params(),
        name="image",
    )(d_high, d_low, own_image, near, far)


def ghost_kernel(agg_of, d_high, d_low, own_half, mine, other, rt_high, rt_low, half_ref, coarse_ref, q_high, q_low):
    slab, size, sub = here()
    core = sub & 1
    odd, near, far = place_of(slab, size)
    band_start = core * (BANDS // 2)
    for side, (which, region) in enumerate(((near, (1 - odd) * 2 * GROUPS), (far, odd * 2 * GROUPS))):
        for r in range(ROWS):
            columns = rows_of(r % (ROWS // 2))
            piece = jnp.where(core == r // (ROWS // 2), mine[side, :, columns], other[side, :, columns])
            band = agg_of[which * ROWS + r] + region - band_start
            for t, value in placed_pairs(piece, band, BANDS // 4):
                high, low = halves(value)
                q_high[rows_of(side * ROWS + r), rows_of(t, 2 * DOF)] = high
                q_low[rows_of(side * ROWS + r), rows_of(t, 2 * DOF)] = low
    lanes = slice(ROWS * DOF, SLOTS * DOF)
    half = own_half[...] + product((d_high[:, lanes], d_low[:, lanes]), (q_high[...], q_low[...]))
    half_ref[...] = half
    coarse_ref[...] = product((rt_high[...], rt_low[...]), halves(half))


def ghost_step(agg_of, d_high, d_low, own_half, mine, other, rt_high, rt_low):
    rows, half = own_half.shape
    return pl.pallas_call(
        ghost_kernel,
        in_specs=[SMEM] + [VMEM] * 7,
        out_specs=[VMEM] * 2,
        out_shape=[
            jax.ShapeDtypeStruct((rows, half), F32),
            jax.ShapeDtypeStruct((GROUPS * DOF, half), F32),
        ],
        scratch_shapes=[pltpu.VMEM((2 * ROWS * DOF, half), BF16)] * 2,
        compiler_params=params(),
        name="ghost_step",
    )(agg_of, d_high, d_low, own_half, mine, other, rt_high, rt_low)


def scaled_by_weight(agg_of, value):
    start = lax.axis_index("slab") * ROWS
    pieces = []
    for a in range(GROUPS):
        members = jnp.zeros((), jnp.int32)
        for e in range(ROWS):
            members += jnp.where(agg_of[start + e] == a, 1, 0)
        piece = value[rows_of(a), :]
        pieces.append(piece * (COARSE_WEIGHT / jnp.full(piece.shape, members.astype(F32))))
    return jnp.concatenate(pieces, axis=0)


def region_lanes(width):
    odd = lax.axis_index("slab") & 1
    near = pl.ds(pl.multiple_of((1 - odd) * 2 * width, width), width)
    far = pl.ds(pl.multiple_of(odd * 2 * width, width), width)
    return near, slice(width, 2 * width), far


def coarse_kernel(agg_of, mine, other, m_high, m_low, op_ref, natural):
    sub = lax.axis_index("sub")
    half = mine.shape[1]
    is_first = (sub & 1) == 0
    left = jnp.where(is_first, mine[...], other[...])
    right = jnp.where(is_first, other[...], mine[...])
    per_share = op_ref.shape[1]
    for position, value in enumerate((left, right)):
        natural[:, rows_of(position, half)] = scaled_by_weight(agg_of, value)
        for place in range(2):

            @pl.when(sub == 2 * position + place)
            def _():
                for a in range(GROUPS):
                    for q in range(per_share):
                        op_ref[a, q] = value[rows_of(a), rows_of(place * per_share + q)]

    width = GROUPS * DOF
    for region, lanes in enumerate(region_lanes(width)):
        high, low = halves(natural[:, lanes])
        m_high[:, rows_of(region, width)] = high
        m_low[:, rows_of(region, width)] = low


def coarse_operator(agg_of, mine, other):
    rows, half = mine.shape
    field = jax.ShapeDtypeStruct((rows, 2 * half), BF16)
    return pl.pallas_call(
        coarse_kernel,
        in_specs=[SMEM] + [VMEM] * 2,
        out_specs=[VMEM] * 3,
        out_shape=[field, field, jax.ShapeDtypeStruct((GROUPS, BANDS // 4, DOF, DOF), F32)],
        scratch_shapes=[pltpu.VMEM((rows, 2 * half), F32)],
        compiler_params=params(),
        name="coarse_operator",
    )(agg_of, mine, other)


def lift_kernel(agg_of, mine, other, smoother, prolong, w_high, w_low, natural):
    half = mine.shape[1]
    width = GROUPS * DOF
    slab, size, sub = here()
    is_first = (sub & 1) == 0
    for e in range(ROWS):
        own_value, other_value = mine[rows_of(e), :], other[rows_of(e), :]
        left = jnp.where(is_first, own_value, other_value)
        right = jnp.where(is_first, other_value, own_value)
        smooth = halves(smoother[e])
        natural[rows_of(e), :half] = -product(smooth, halves(left))
        natural[rows_of(e), half:] = -product(smooth, halves(right))
        for t, value in placed_pairs(prolong[e], agg_of[slab * ROWS + e], GROUPS // 2):
            lanes = slice(width + t * 2 * DOF, width + (t + 1) * 2 * DOF)
            natural[rows_of(e), lanes] += value
    for region, lanes in enumerate(region_lanes(width)):
        high, low = halves(natural[:, lanes])
        w_high[:, rows_of(region, width)] = high
        w_low[:, rows_of(region, width)] = low


def lift_operator(agg_of, mine, other, smoother, prolong):
    rows, half = mine.shape
    field = jax.ShapeDtypeStruct((rows, 2 * half), BF16)
    return pl.pallas_call(
        lift_kernel,
        in_specs=[SMEM] + [VMEM] * 4,
        out_specs=[VMEM] * 2,
        out_shape=[field, field],
        scratch_shapes=[pltpu.VMEM((rows, 2 * half), F32)],
        compiler_params=params(),
        name="lift_operator",
    )(agg_of, mine, other, smoother, prolong)


def residual_kernel(agg_of, right_side, keep, received, rt_high, rt_low, residual_ref, first_ref):
    own = pl.ds(pl.multiple_of(lax.axis_index("sub") * COLS, COLS), COLS)
    residual = right_side[:, :, own].reshape(keep.shape) - (keep[...] + received[...])
    residual_ref[...] = residual
    coarse_rhs = product((rt_high[...], rt_low[...]), halves(residual))
    first_ref[...] = scaled_by_weight(agg_of, coarse_rhs)


def residual_step(agg_of, right_side, keep, received, rt_high, rt_low):
    return pl.pallas_call(
        residual_kernel,
        in_specs=[SMEM] + [VMEM] * 5,
        out_specs=[VMEM] * 2,
        out_shape=[
            jax.ShapeDtypeStruct(keep.shape, F32),
            jax.ShapeDtypeStruct((rt_high.shape[0], COLS), F32),
        ],
        compiler_params=params(),
        name="residual_step",
    )(agg_of, right_side, keep, received, rt_high, rt_low)


def base_kernel(smoother, x_first, residual, base_ref):
    for e in range(ROWS):
        smoothed = product(halves(smoother[e]), halves(residual[rows_of(e), :]))
        base_ref[rows_of(e), :] = x_first[rows_of(e), :COLS] + smoothed


def base_step(smoother, x_first, residual):
    return pl.pallas_call(
        base_kernel,
        in_specs=[VMEM] * 3,
        out_specs=VMEM,
        out_shape=jax.ShapeDtypeStruct(residual.shape, F32),
        compiler_params=params(),
        name="base_step",
    )(smoother, x_first, residual)


def applied(op_high, op_low, near, own, far):
    total = None
    for region, field in enumerate((near, own, far)):
        lanes = rows_of(region, GROUPS * DOF)
        part = product((op_high[:, lanes], op_low[:, lanes]), halves(field[...]))
        total = part if total is None else total + part
    return total


def sweep_kernel(m_high, m_low, first, near, own, far, next_ref):
    next_ref[...] = own[...] + first[...] - applied(m_high, m_low, near, own, far)


def sweep(m_high, m_low, first, near, own, far):
    return pl.pallas_call(
        sweep_kernel,
        in_specs=[VMEM] * 6,
        out_specs=VMEM,
        out_shape=jax.ShapeDtypeStruct(own.shape, F32),
        compiler_params=params(),
        name="sweep",
    )(m_high, m_low, first, near, own, far)


def last_kernel(w_high, w_low, base, near, own, far, out_ref):
    out_ref[...] = base[...] + applied(w_high, w_low, near, own, far)


def last_step(w_high, w_low, base, near, own, far):
    return pl.pallas_call(
        last_kernel,
        in_specs=[VMEM] * 6,
        out_specs=VMEM,
        out_shape=jax.ShapeDtypeStruct(base.shape, F32),
        compiler_params=params(),
        name="last_step",
    )(w_high, w_low, base, near, own, far)


def swaps(size, start):
    pairs = [(i, i + 1) for i in range(start, size - 1, 2)]
    return pairs + [(j, i) for i, j in pairs]


def from_neighbours(value):
    size = lax.axis_size("slab")
    far = lax.ppermute(value, "slab", swaps(size, 1))
    near = lax.ppermute(value, "slab", swaps(size, 0))
    return near, far


def swapped(value, bit):
    size = lax.axis_size("sub")
    return lax.ppermute(value, "sub", [(i, i ^ bit) for i in range(size)])


def per_device(fine_blocks, prolong, smoother, right_side, agg_of, col_slot, send_rows, send_count):
    d_own, x_first, packed = start_step(
        col_slot, send_rows, send_count, fine_blocks, smoother, right_side, prolong
    )
    x_message = jnp.concatenate([x_first, packed], axis=0)
    near_message, far_message = from_neighbours(x_message)
    d_other = swapped(d_own, 1)
    d_high, d_low, half, own_image, rt_high, rt_low = own_step(agg_of, d_own, d_other, prolong, x_first)
    near_message, far_message, own_image = lax.optimization_barrier((near_message, far_message, own_image))
    keep, send = image(d_high, d_low, own_image, near_message, far_message)
    received = swapped(send, 2)
    ghosts = jnp.stack([near_message[ROWS * DOF :], far_message[ROWS * DOF :]])
    half, coarse = ghost_step(agg_of, d_high, d_low, half, ghosts, swapped(ghosts, 1), rt_high, rt_low)
    coarse_other = swapped(coarse, 2)
    residual, first = residual_step(agg_of, right_side, keep, received, rt_high, rt_low)
    base = base_step(smoother, x_first, residual)
    near, far = from_neighbours(first)
    near, far, coarse_other = lax.optimization_barrier((near, far, coarse_other))
    coarse = coarse + coarse_other
    half, coarse = lax.optimization_barrier((half, coarse))
    half_other = swapped(half, 2)
    m_high, m_low, coarse_op = coarse_operator(agg_of, coarse, swapped(coarse, 1))
    correction = first
    for index in range(COARSE_SWEEPS - 1):
        if index > 0:
            near, far = from_neighbours(correction)
        correction = sweep(m_high, m_low, first, near, correction, far)
    half_other, correction = lax.optimization_barrier((half_other, correction))
    half = half + half_other
    w_high, w_low = lift_operator(agg_of, half, swapped(half, 1), smoother, prolong)
    near, far = from_neighbours(correction)
    solution = last_step(w_high, w_low, base, near, correction, far)
    return coarse_op, solution.reshape(ROWS, DOF, COLS)


def solution(mesh):
    placed = (
        P("slab", "sub", None, None),
        P("slab", None, None),
        P("slab", None, None),
        P("slab", None, None),
        P(),
        P("slab", "sub"),
        P(),
        P(),
    )
    return jax.shard_map(
        per_device,
        mesh=mesh,
        in_specs=placed,
        out_specs=(P("slab", "sub", None, None), P("slab", None, "sub")),
        check_vma=False,
    )
```

```python
import jax
import jax.numpy as jnp
from jax import lax
from jax.experimental import pallas as pl
from jax.experimental.pallas import tpu as pltpu
from jax.sharding import PartitionSpec as P

COARSE_SWEEPS = 3
COARSE_WEIGHT = 0.25
F32 = jnp.float32
BF16 = jnp.bfloat16
VMEM = pl.BlockSpec(memory_space=pltpu.VMEM)
SMEM = pl.BlockSpec(memory_space=pltpu.SMEM)
HBM = pl.BlockSpec(memory_space=pltpu.HBM)
ROWS = 8
GHOSTS = 8
SLOTS = ROWS + 2 * GHOSTS
GROUPS = 4
BANDS = 3 * GROUPS
DOF = 64
COLS = 128
SUBS = 4
HALF_ROWS = ROWS // 2
WIDE = ROWS * DOF
PAIR = 2 * DOF
COARSE = GROUPS * DOF


def params(limit=24):
    return pltpu.CompilerParams(vmem_limit_bytes=limit << 20)


def shape(*dims, dtype=F32):
    return jax.ShapeDtypeStruct(dims, dtype)


def halves(value):
    high = value.astype(BF16)
    return high, (value - high.astype(F32)).astype(BF16)


def mm(a, b):
    return jnp.dot(a, b, preferred_element_type=F32)


def product(left, right):
    left_high, left_low = left
    right_high, right_low = right
    return mm(left_high, right_high) + (mm(left_high, right_low) + mm(left_low, right_high))


def narrow_product(left, value):
    left_high, left_low = left
    high, low = halves(value)
    width = value.shape[1]
    both = mm(left_high, jnp.concatenate([high, low], axis=1))
    return both[:, :width] + (both[:, width:] + mm(left_low, high))


def span(index, size=DOF):
    return slice(index * size, (index + 1) * size)


def aligned(index, size):
    return pl.ds(pl.multiple_of(index * size, size), size)


def neighbours():
    slab, size = lax.axis_index("slab"), lax.axis_size("slab")
    odd = slab & 1
    near = jnp.minimum(slab ^ 1, size - 1)
    far = jnp.where(odd == 1, jnp.minimum(slab + 1, size - 1), jnp.maximum(slab - 1, 0))
    return slab, near, far


def start_kernel(
    col_hbm, rows_hbm, counts_hbm, blocks_hbm, smoother_hbm, right_hbm, prolong_hbm,
    pair_ref, mine_ref, theirs_ref, message_ref, right_ref,
    col_slot, rows, counts, blocks, smoother, right, prolong, sems, block_sems, *parts
):
    slab, size, sub = lax.axis_index("slab"), lax.axis_size("slab"), lax.axis_index("sub")
    below = jnp.maximum(slab - 1, 0)
    above = jnp.minimum(slab + 1, size - 1)
    core = sub & 1
    chip = (sub >> 1) & 1
    sources = [
        (smoother_hbm, smoother),
        (right_hbm.at[:, :, aligned(sub, COLS)], right.at[0]),
        (right_hbm.at[:, :, aligned(sub ^ 2, COLS)], right.at[1]),
        (prolong_hbm.at[pl.ds(core * HALF_ROWS, HALF_ROWS)], prolong),
        (col_hbm, col_slot),
        (rows_hbm.at[below, sub], rows.at[0]),
        (rows_hbm.at[above, sub], rows.at[1]),
        (counts_hbm.at[sub], counts),
    ]
    copies = [pltpu.make_async_copy(s, d, sems.at[i]) for i, (s, d) in enumerate(sources)]
    block_copies = [
        pltpu.make_async_copy(blocks_hbm.at[e], blocks.at[e], block_sems.at[e]) for e in range(ROWS)
    ]
    for copy in copies + block_copies:
        copy.start()
    for copy in copies:
        copy.wait()

    for e in range(ROWS):
        right_ref[span(e), :] = right[0, e]
        wide = jnp.concatenate([right[0, e], right[1, e]], axis=1)
        message_ref[span(e), :] = product(halves(smoother[e]), halves(wide))
    message_ref[span(ROWS), :] = jnp.concatenate([prolong[i] for i in range(HALF_ROWS)], axis=1)

    lower_count = jnp.where(slab > 0, counts[1, below], 0)
    upper_count = jnp.where(slab < size - 1, counts[0, above], 0)
    lower_region = 1 + (1 - (slab & 1) ^ chip)
    lower_start = lower_region * ROWS
    upper_start = (3 - lower_region) * ROWS
    upper_lanes = lax.broadcasted_iota(jnp.int32, (DOF, PAIR), 1) >= DOF
    for group in range(ROWS // HALF_ROWS):
        for position, part in enumerate(parts):
            part[...] = jnp.zeros_like(part)
            block_copies[group * HALF_ROWS + position].wait()
        for j in range(blocks.shape[1]):
            for position, part in enumerate(parts):
                e = group * HALF_ROWS + position
                slot = col_slot[e, j]
                is_own = slot < ROWS
                is_upper = slot >= ROWS + GHOSTS
                side = jnp.where(is_upper, 1, 0)
                place = jnp.where(is_own, 0, slot - ROWS - side * GHOSTS)
                listed = rows[side, 1 - side, place] + jnp.where(is_upper, upper_start, lower_start)
                column = jnp.where(is_own, slot, listed)
                count = jnp.where(is_upper, upper_count, lower_count)
                live = jnp.where(is_own | (place < count), 1.0, 0.0)
                odd_column = column & 1
                lower_scale = jnp.where(odd_column == 0, live, 0.0)
                upper_scale = jnp.where(odd_column == 1, live, 0.0)
                block = blocks[e, j]
                doubled = jnp.concatenate([block, block], axis=1)
                part[:, aligned(column >> 1, PAIR)] += doubled * jnp.where(upper_lanes, upper_scale, lower_scale)
        for position, part in enumerate(parts):
            pair_ref[span(group * HALF_ROWS + position), :] = part[:, : 2 * WIDE]

        @pl.when(core == group)
        def _():
            for position, part in enumerate(parts):
                mine_ref[span(position), :] = part[:, 2 * WIDE :]

        @pl.when(core != group)
        def _():
            for position, part in enumerate(parts):
                theirs_ref[span(position), :] = part[:, 2 * WIDE :]


def start_step(col_slot, send_rows, send_count, blocks, smoother, right_side, prolong):
    counts = jnp.transpose(send_count, (1, 2, 0))
    arrays = (col_slot, send_rows, counts, blocks, smoother, right_side, prolong)
    return pl.pallas_call(
        start_kernel,
        in_specs=[HBM] * 7,
        out_specs=[VMEM] * 5,
        out_shape=[
            shape(WIDE, 2 * WIDE),
            shape(WIDE // 2, WIDE),
            shape(WIDE // 2, WIDE),
            shape(WIDE + DOF, 2 * COLS),
            shape(WIDE, COLS),
        ],
        scratch_shapes=[
            pltpu.SMEM(col_slot.shape, jnp.int32),
            pltpu.SMEM((2, 2, GHOSTS), jnp.int32),
            pltpu.SMEM((2, send_count.shape[0]), jnp.int32),
            pltpu.VMEM(blocks.shape, F32),
            pltpu.VMEM(smoother.shape, F32),
            pltpu.VMEM((2, ROWS, DOF, COLS), F32),
            pltpu.VMEM((HALF_ROWS, DOF, DOF), F32),
            pltpu.SemaphoreType.DMA((8,)),
            pltpu.SemaphoreType.DMA((ROWS,)),
        ]
        + [pltpu.VMEM((DOF, 3 * WIDE), F32)] * HALF_ROWS,
        compiler_params=params(),
        name="start_step",
    )(*(pltpu.with_memory_space_constraint(a, pltpu.HBM) for a in arrays))


def placed(piece, index):
    upper = lax.broadcasted_iota(jnp.int32, (DOF, PAIR), 1) >= DOF
    doubled = jnp.concatenate([piece, piece], axis=1)
    lower_scale = jnp.where(index == 0, 1.0, 0.0)
    upper_scale = jnp.where(index == 1, 1.0, 0.0)
    return doubled * jnp.where(upper, upper_scale, lower_scale)


def own_kernel(
    agg_of, prolong, field, right, pair, pair_other, side_ref, half_ref, image_ref, rt_high, rt_low, q_high, q_low
):
    start = lax.axis_index("slab") * ROWS
    core = lax.axis_index("sub") & 1

    @pl.when(pl.program_id(0) == 0)
    def _():
        restrict_rows = []
        for e in range(ROWS):
            group = agg_of[start + e]
            high, low = halves(placed(prolong[e], group - 2 * core))
            q_high[span(e), :] = high
            q_low[span(e), :] = low
            parts = [placed(prolong[e], group - 2 * t) for t in range(GROUPS // 2)]
            restrict_rows.append(jnp.concatenate(parts, axis=1))
        high, low = halves(jnp.concatenate(restrict_rows, axis=0).T)
        rt_high[...] = high
        rt_low[...] = low

    side_ref[...] = pair[:, WIDE:] + pair_other[:, WIDE:]
    own = halves(pair[:, :WIDE] + pair_other[:, :WIDE])
    half_ref[...] = product(own, (q_high[...], q_low[...]))
    total = product(own, halves(field[...]))
    image_ref[:, :COLS] = total[:, :COLS] - right[...]
    image_ref[:, COLS:] = total[:, COLS:]


def own_step(agg_of, prolong, message, right, pair, pair_other):
    steps = 2
    whole = lambda *dims: pl.BlockSpec(dims, lambda i: (0,) * len(dims))
    part = lambda width: pl.BlockSpec((WIDE // steps, width), lambda i: (i, 0))
    return pl.pallas_call(
        own_kernel,
        grid=(steps,),
        in_specs=[SMEM, whole(*prolong.shape), whole(WIDE, 2 * COLS), part(COLS)] + [part(2 * WIDE)] * 2,
        out_specs=[part(WIDE), part(PAIR), part(2 * COLS)] + [whole(COARSE, WIDE)] * 2,
        out_shape=[
            shape(WIDE, WIDE),
            shape(WIDE, PAIR),
            shape(WIDE, 2 * COLS),
            shape(COARSE, WIDE, dtype=BF16),
            shape(COARSE, WIDE, dtype=BF16),
        ],
        scratch_shapes=[pltpu.VMEM((WIDE, PAIR), BF16)] * 2,
        compiler_params=params(),
        name="own_step",
    )(agg_of, prolong, message, right, pair, pair_other)


def image_kernel(own_image, side, received, received_other, message, keep_ref, send_ref, high_ref, low_ref):
    core = lax.axis_index("sub") & 1
    field = halves(message[:WIDE, :])
    rows = WIDE // 2
    for group in range(2):
        part = span(group, rows)
        extra = jnp.where(core == group, received[...], received_other[...])
        high, low = halves(side[part, :] + extra)
        high_ref[part, :] = high
        low_ref[part, :] = low
        total = own_image[part, :] + product((high, low), field)
        keep_ref[part, :] = total[:, :COLS]
        send_ref[part, :] = total[:, COLS:]


def image(own_image, side, received, received_other, message):
    return pl.pallas_call(
        image_kernel,
        in_specs=[VMEM] * 5,
        out_specs=[VMEM] * 4,
        out_shape=[shape(WIDE, COLS)] * 2 + [shape(WIDE, WIDE, dtype=BF16)] * 2,
        compiler_params=params(),
        name="image",
    )(own_image, side, received, received_other, message)


def ghost_kernel(agg_of, d_high, d_low, own_half, mine, other, rt_high, rt_low, half_ref, coarse_ref, q_high, q_low):
    _, near, far = neighbours()
    sub = lax.axis_index("sub")
    core = sub & 1
    start = jnp.where(((sub >> 1) & 1) == 0, near, far) * ROWS
    for r in range(ROWS):
        columns = span(r % HALF_ROWS)
        piece = jnp.where(core == r // HALF_ROWS, mine[:, columns], other[:, columns])
        high, low = halves(placed(piece, agg_of[start + r] - 2 * core))
        q_high[span(r), :] = high
        q_low[span(r), :] = low
    half_ref[:, :PAIR] = own_half[...]
    half_ref[:, PAIR:] = product((d_high[...], d_low[...]), (q_high[...], q_low[...]))
    coarse_ref[...] = product((rt_high[...], rt_low[...]), halves(half_ref[...]))


def ghost_step(agg_of, d_high, d_low, own_half, mine, other, rt_high, rt_low):
    return pl.pallas_call(
        ghost_kernel,
        in_specs=[SMEM] + [VMEM] * 7,
        out_specs=[VMEM] * 2,
        out_shape=[shape(WIDE, 2 * PAIR), shape(COARSE, 2 * PAIR)],
        scratch_shapes=[pltpu.VMEM((WIDE, PAIR), BF16)] * 2,
        compiler_params=params(),
        name="ghost_step",
    )(agg_of, d_high, d_low, own_half, mine, other, rt_high, rt_low)


def scaled_by_weight(agg_of, value):
    start = lax.axis_index("slab") * ROWS
    pieces = []
    for a in range(GROUPS):
        members = jnp.zeros((), jnp.int32)
        for e in range(ROWS):
            members += jnp.where(agg_of[start + e] == a, 1, 0)
        piece = value[span(a), :]
        pieces.append(piece * (COARSE_WEIGHT / jnp.full(piece.shape, members.astype(F32))))
    return jnp.concatenate(pieces, axis=0)


def coarse_kernel(agg_of, mine, other, m_high, m_low, op_ref, natural):
    sub = lax.axis_index("sub")
    odd = lax.axis_index("slab") & 1
    is_first = (sub & 1) == 0
    first = jnp.where(is_first, mine[...], other[...])
    second = jnp.where(is_first, other[...], mine[...])
    places = (2 * (1 - odd), 1, 2 * odd)
    for region, place in enumerate(places):
        value = jnp.concatenate([first[:, span(region, PAIR)], second[:, span(region, PAIR)]], axis=1)
        natural[:, aligned(place, COARSE)] = value
        high, low = halves(scaled_by_weight(agg_of, value))
        m_high[:, span(region, COARSE)] = high
        m_low[:, span(region, COARSE)] = low
    share = op_ref.shape[1]
    for k in range(BANDS // share):

        @pl.when(sub == k)
        def _():
            for a in range(GROUPS):
                for q in range(share):
                    op_ref[a, q] = natural[span(a), span(k * share + q)]


def coarse_operator(agg_of, mine, other):
    return pl.pallas_call(
        coarse_kernel,
        in_specs=[SMEM] + [VMEM] * 2,
        out_specs=[VMEM] * 3,
        out_shape=[shape(COARSE, 3 * COARSE, dtype=BF16)] * 2 + [shape(GROUPS, BANDS // SUBS, DOF, DOF)],
        scratch_shapes=[pltpu.VMEM((COARSE, 3 * COARSE), F32)],
        compiler_params=params(),
        name="coarse_operator",
    )(agg_of, mine, other)


def lift_kernel(agg_of, mine, other, smoother, prolong, w_high, w_low):
    start = lax.axis_index("slab") * ROWS
    is_first = (lax.axis_index("sub") & 1) == 0
    for e in range(ROWS):
        smooth = halves(smoother[e])
        from_mine = product(smooth, halves(mine[span(e), :]))
        from_other = product(smooth, halves(other[span(e), :]))
        first = jnp.where(is_first, from_mine, from_other)
        second = jnp.where(is_first, from_other, from_mine)
        for region in range(3):
            for t, value in enumerate((first, second)):
                value = -value[:, span(region, PAIR)]
                if region == 1:
                    value += placed(prolong[e], agg_of[start + e] - 2 * t)
                high, low = halves(value)
                w_high[span(e), span(2 * region + t, PAIR)] = high
                w_low[span(e), span(2 * region + t, PAIR)] = low


def lift_operator(agg_of, mine, other, smoother, prolong):
    return pl.pallas_call(
        lift_kernel,
        in_specs=[SMEM] + [VMEM] * 4,
        out_specs=[VMEM] * 2,
        out_shape=[shape(WIDE, 3 * COARSE, dtype=BF16)] * 2,
        compiler_params=params(),
        name="lift_operator",
    )(agg_of, mine, other, smoother, prolong)


def residual_kernel(agg_of, keep, received, rt_high, rt_low, residual_ref, first_ref):
    residual = -(keep[...] + received[...])
    residual_ref[...] = residual
    first_ref[...] = scaled_by_weight(agg_of, narrow_product((rt_high[...], rt_low[...]), residual))


def residual_step(agg_of, keep, received, rt_high, rt_low):
    return pl.pallas_call(
        residual_kernel,
        in_specs=[SMEM] + [VMEM] * 4,
        out_specs=[VMEM] * 2,
        out_shape=[shape(WIDE, COLS), shape(COARSE, COLS)],
        compiler_params=params(),
        name="residual_step",
    )(agg_of, keep, received, rt_high, rt_low)


def base_kernel(smoother, message, residual, base_ref):
    for e in range(ROWS):
        smoothed = narrow_product(halves(smoother[e]), residual[span(e), :])
        base_ref[span(e), :] = message[span(e), :COLS] + smoothed


def base_step(smoother, message, residual):
    return pl.pallas_call(
        base_kernel,
        in_specs=[VMEM] * 3,
        out_specs=VMEM,
        out_shape=shape(WIDE, COLS),
        compiler_params=params(),
        name="base_step",
    )(smoother, message, residual)


def applied(op_high, op_low, fields):
    total = None
    for region, field in fields:
        lanes = span(region, COARSE)
        part = narrow_product((op_high[:, lanes], op_low[:, lanes]), field[...])
        total = part if total is None else total + part
    return total


def sweep_kernel(m_high, m_low, first, near, own, far, next_ref):
    fields = ((0, near), (1, own), (2, far))
    next_ref[...] = own[...] + first[...] - applied(m_high, m_low, fields)


def sweep(m_high, m_low, first, near, own, far):
    return pl.pallas_call(
        sweep_kernel,
        in_specs=[VMEM] * 6,
        out_specs=VMEM,
        out_shape=shape(COARSE, COLS),
        compiler_params=params(),
        name="sweep",
    )(m_high, m_low, first, near, own, far)


def lifted_kernel(w_high, w_low, base, own, out_ref):
    out_ref[...] = base[...] + applied(w_high, w_low, ((1, own),))


def lifted(w_high, w_low, base, own):
    return pl.pallas_call(
        lifted_kernel,
        in_specs=[VMEM] * 4,
        out_specs=VMEM,
        out_shape=shape(WIDE, COLS),
        compiler_params=params(),
        name="lifted",
    )(w_high, w_low, base, own)


def last_kernel(w_high, w_low, base, near, far, out_ref):
    out_ref[...] = base[...] + applied(w_high, w_low, ((0, near), (2, far)))


def last_step(w_high, w_low, base, near, far):
    return pl.pallas_call(
        last_kernel,
        in_specs=[VMEM] * 5,
        out_specs=VMEM,
        out_shape=shape(WIDE, COLS),
        compiler_params=params(),
        name="last_step",
    )(w_high, w_low, base, near, far)


def swaps(size, start):
    pairs = [(i, i + 1) for i in range(start, size - 1, 2)]
    return pairs + [(j, i) for i, j in pairs]


def from_neighbours(value):
    size = lax.axis_size("slab")
    far = lax.ppermute(value, "slab", swaps(size, 1))
    near = lax.ppermute(value, "slab", swaps(size, 0))
    return near, far


def from_side(value):
    size, subs = lax.axis_size("slab"), lax.axis_size("sub")
    pairs = [
        (i * subs + k, j * subs + k) for k in range(subs) for i, j in swaps(size, (k >> 1) & 1)
    ]
    return lax.ppermute(value, ("slab", "sub"), pairs)


def swapped(value, bit):
    size = lax.axis_size("sub")
    return lax.ppermute(value, "sub", [(i, i ^ bit) for i in range(size)])


def summed_regions(mine, received):
    is_near = ((lax.axis_index("sub") >> 1) & 1) == 0
    own = mine[:, :PAIR] + received[:, :PAIR]
    near = jnp.where(is_near, mine[:, PAIR:], received[:, PAIR:])
    far = jnp.where(is_near, received[:, PAIR:], mine[:, PAIR:])
    return jnp.concatenate([near, own, far], axis=1)


def per_device(fine_blocks, prolong, smoother, right_side, agg_of, col_slot, send_rows, send_count):
    pair, mine, theirs, message, right = start_step(
        col_slot, send_rows, send_count, fine_blocks, smoother, right_side, prolong
    )
    side_message = from_side(message)
    received = swapped(mine + swapped(theirs, 1), 2)
    received_other = swapped(received, 1)
    side, half, own_image, rt_high, rt_low = own_step(agg_of, prolong, message, right, pair, swapped(pair, 1))
    keep, send, d_high, d_low = image(own_image, side, received, received_other, side_message)
    image_received = swapped(send, 2)
    ghosts = side_message[WIDE:]
    half, coarse = ghost_step(agg_of, d_high, d_low, half, ghosts, swapped(ghosts, 1), rt_high, rt_low)
    coarse_received = swapped(coarse, 2)
    residual, first = residual_step(agg_of, keep, image_received, rt_high, rt_low)
    base = base_step(smoother, message, residual)
    half, first = lax.optimization_barrier((half, first))
    half_received = swapped(half, 2)
    near, far = from_neighbours(first)
    near, far, coarse_received = lax.optimization_barrier((near, far, coarse_received))
    coarse = summed_regions(coarse, coarse_received)
    m_high, m_low, coarse_op = coarse_operator(agg_of, coarse, swapped(coarse, 1))
    correction = first
    for index in range(COARSE_SWEEPS - 1):
        if index > 0:
            near, far = from_neighbours(correction)
        correction = sweep(m_high, m_low, first, near, correction, far)
    half_received, correction = lax.optimization_barrier((half_received, correction))
    half = summed_regions(half, half_received)
    w_high, w_low = lift_operator(agg_of, half, swapped(half, 1), smoother, prolong)
    near, far = from_neighbours(correction)
    base = lifted(w_high, w_low, base, correction)
    solution = last_step(w_high, w_low, base, near, far)
    return coarse_op, solution.reshape(ROWS, DOF, COLS)


def solution(mesh):
    placed_args = (
        P("slab", "sub", None, None),
        P("slab", None, None),
        P("slab", None, None),
        P("slab", None, None),
        P(),
        P("slab", "sub"),
        P(),
        P(),
    )
    return jax.shard_map(
        per_device,
        mesh=mesh,
        in_specs=placed_args,
        out_specs=(P("slab", "sub", None, None), P("slab", None, "sub")),
        check_vma=False,
    )
```

```python
import jax
import jax.numpy as jnp
from jax import lax
from jax.experimental import pallas as pl
from jax.experimental.pallas import tpu as pltpu
from jax.sharding import PartitionSpec as P

COARSE_SWEEPS = 3
COARSE_WEIGHT = 0.25
F32 = jnp.float32
BF16 = jnp.bfloat16
VMEM = pl.BlockSpec(memory_space=pltpu.VMEM)
SMEM = pl.BlockSpec(memory_space=pltpu.SMEM)
HBM = pl.BlockSpec(memory_space=pltpu.HBM)
ROWS = 8
GHOSTS = 8
SLOTS = ROWS + 2 * GHOSTS
GROUPS = 4
BANDS = 3 * GROUPS
DOF = 64
COLS = 128
SUBS = 4
HALF_ROWS = ROWS // 2
WIDE = ROWS * DOF
PAIR = 2 * DOF
COARSE = GROUPS * DOF


def params(limit=24):
    return pltpu.CompilerParams(vmem_limit_bytes=limit << 20)


def shape(*dims, dtype=F32):
    return jax.ShapeDtypeStruct(dims, dtype)


def halves(value):
    high = value.astype(BF16)
    return high, (value - high.astype(F32)).astype(BF16)


def mm(a, b):
    return jnp.dot(a, b, preferred_element_type=F32)


def product(left, right):
    left_high, left_low = left
    right_high, right_low = right
    return mm(left_high, right_high) + (mm(left_high, right_low) + mm(left_low, right_high))


def narrow_product(left, value):
    left_high, left_low = left
    high, low = halves(value)
    width = value.shape[1]
    both = mm(left_high, jnp.concatenate([high, low], axis=1))
    return both[:, :width] + (both[:, width:] + mm(left_low, high))


def span(index, size=DOF):
    return slice(index * size, (index + 1) * size)


def aligned(index, size):
    return pl.ds(pl.multiple_of(index * size, size), size)


def neighbours():
    slab, size = lax.axis_index("slab"), lax.axis_size("slab")
    odd = slab & 1
    near = jnp.minimum(slab ^ 1, size - 1)
    far = jnp.where(odd == 1, jnp.minimum(slab + 1, size - 1), jnp.maximum(slab - 1, 0))
    return slab, near, far


def start_kernel(
    col_hbm, rows_hbm, counts_hbm, blocks_hbm, smoother_hbm, right_hbm, prolong_hbm,
    pair_ref, mine_ref, theirs_ref, message_ref, right_ref,
    col_slot, rows, counts, blocks, smoother, right, prolong, sems, block_sems, *parts
):
    slab, size, sub = lax.axis_index("slab"), lax.axis_size("slab"), lax.axis_index("sub")
    below = jnp.maximum(slab - 1, 0)
    above = jnp.minimum(slab + 1, size - 1)
    core = sub & 1
    chip = (sub >> 1) & 1
    sources = [
        (smoother_hbm, smoother),
        (right_hbm.at[:, :, aligned(sub, COLS)], right.at[0]),
        (right_hbm.at[:, :, aligned(sub ^ 2, COLS)], right.at[1]),
        (prolong_hbm.at[pl.ds(core * HALF_ROWS, HALF_ROWS)], prolong),
        (col_hbm, col_slot),
        (rows_hbm.at[below, sub], rows.at[0]),
        (rows_hbm.at[above, sub], rows.at[1]),
        (counts_hbm.at[sub], counts),
    ]
    copies = [pltpu.make_async_copy(s, d, sems.at[i]) for i, (s, d) in enumerate(sources)]
    block_copies = [
        pltpu.make_async_copy(blocks_hbm.at[e], blocks.at[e], block_sems.at[e]) for e in range(ROWS)
    ]
    for copy in copies + block_copies:
        copy.start()
    for copy in copies:
        copy.wait()

    for e in range(ROWS):
        right_ref[span(e), :] = right[0, e]
        wide = jnp.concatenate([right[0, e], right[1, e]], axis=1)
        message_ref[span(e), :] = product(halves(smoother[e]), halves(wide))
    message_ref[span(ROWS), :] = jnp.concatenate([prolong[i] for i in range(HALF_ROWS)], axis=1)

    lower_count = jnp.where(slab > 0, counts[1, below], 0)
    upper_count = jnp.where(slab < size - 1, counts[0, above], 0)
    lower_region = 1 + (1 - (slab & 1) ^ chip)
    lower_start = lower_region * ROWS
    upper_start = (3 - lower_region) * ROWS
    upper_lanes = lax.broadcasted_iota(jnp.int32, (DOF, PAIR), 1) >= DOF
    for group in range(ROWS // HALF_ROWS):
        for position, part in enumerate(parts):
            part[...] = jnp.zeros_like(part)
            block_copies[group * HALF_ROWS + position].wait()
        for j in range(blocks.shape[1]):
            for position, part in enumerate(parts):
                e = group * HALF_ROWS + position
                slot = col_slot[e, j]
                is_own = slot < ROWS
                is_upper = slot >= ROWS + GHOSTS
                side = jnp.where(is_upper, 1, 0)
                place = jnp.where(is_own, 0, slot - ROWS - side * GHOSTS)
                listed = rows[side, 1 - side, place] + jnp.where(is_upper, upper_start, lower_start)
                column = jnp.where(is_own, slot, listed)
                count = jnp.where(is_upper, upper_count, lower_count)
                live = jnp.where(is_own | (place < count), 1.0, 0.0)
                odd_column = column & 1
                lower_scale = jnp.where(odd_column == 0, live, 0.0)
                upper_scale = jnp.where(odd_column == 1, live, 0.0)
                block = blocks[e, j]
                doubled = jnp.concatenate([block, block], axis=1)
                part[:, aligned(column >> 1, PAIR)] += doubled * jnp.where(upper_lanes, upper_scale, lower_scale)
        for position, part in enumerate(parts):
            pair_ref[span(group * HALF_ROWS + position), :] = part[:, : 2 * WIDE]

        @pl.when(core == group)
        def _():
            for position, part in enumerate(parts):
                mine_ref[span(position), :] = part[:, 2 * WIDE :]

        @pl.when(core != group)
        def _():
            for position, part in enumerate(parts):
                theirs_ref[span(position), :] = part[:, 2 * WIDE :]


def start_step(col_slot, send_rows, send_count, blocks, smoother, right_side, prolong):
    counts = jnp.transpose(send_count, (1, 2, 0))
    arrays = (col_slot, send_rows, counts, blocks, smoother, right_side, prolong)
    return pl.pallas_call(
        start_kernel,
        in_specs=[HBM] * 7,
        out_specs=[VMEM] * 5,
        out_shape=[
            shape(WIDE, 2 * WIDE),
            shape(WIDE // 2, WIDE),
            shape(WIDE // 2, WIDE),
            shape(WIDE + DOF, 2 * COLS),
            shape(WIDE, COLS),
        ],
        scratch_shapes=[
            pltpu.SMEM(col_slot.shape, jnp.int32),
            pltpu.SMEM((2, 2, GHOSTS), jnp.int32),
            pltpu.SMEM((2, send_count.shape[0]), jnp.int32),
            pltpu.VMEM(blocks.shape, F32),
            pltpu.VMEM(smoother.shape, F32),
            pltpu.VMEM((2, ROWS, DOF, COLS), F32),
            pltpu.VMEM((HALF_ROWS, DOF, DOF), F32),
            pltpu.SemaphoreType.DMA((8,)),
            pltpu.SemaphoreType.DMA((ROWS,)),
        ]
        + [pltpu.VMEM((DOF, 3 * WIDE), F32)] * HALF_ROWS,
        compiler_params=params(),
        name="start_step",
    )(*(pltpu.with_memory_space_constraint(a, pltpu.HBM) for a in arrays))


def placed(piece, index):
    upper = lax.broadcasted_iota(jnp.int32, (DOF, PAIR), 1) >= DOF
    doubled = jnp.concatenate([piece, piece], axis=1)
    lower_scale = jnp.where(index == 0, 1.0, 0.0)
    upper_scale = jnp.where(index == 1, 1.0, 0.0)
    return doubled * jnp.where(upper, upper_scale, lower_scale)


def own_kernel(
    agg_of, prolong, field, right, pair, pair_other, side_ref, half_ref, image_ref, rt_high, rt_low, q_high, q_low
):
    start = lax.axis_index("slab") * ROWS
    core = lax.axis_index("sub") & 1

    @pl.when(pl.program_id(0) == 0)
    def _():
        restrict_rows = []
        for e in range(ROWS):
            group = agg_of[start + e]
            high, low = halves(placed(prolong[e], group - 2 * core))
            q_high[span(e), :] = high
            q_low[span(e), :] = low
            parts = [placed(prolong[e], group - 2 * t) for t in range(GROUPS // 2)]
            restrict_rows.append(jnp.concatenate(parts, axis=1))
        high, low = halves(jnp.concatenate(restrict_rows, axis=0).T)
        rt_high[...] = high
        rt_low[...] = low

    side_ref[...] = pair[:, WIDE:] + pair_other[:, WIDE:]
    own = halves(pair[:, :WIDE] + pair_other[:, :WIDE])
    half_ref[...] = product(own, (q_high[...], q_low[...]))
    total = product(own, halves(field[...]))
    image_ref[:, :COLS] = total[:, :COLS] - right[...]
    image_ref[:, COLS:] = total[:, COLS:]


def own_step(agg_of, prolong, message, right, pair, pair_other):
    steps = 2
    whole = lambda *dims: pl.BlockSpec(dims, lambda i: (0,) * len(dims))
    part = lambda width: pl.BlockSpec((WIDE // steps, width), lambda i: (i, 0))
    return pl.pallas_call(
        own_kernel,
        grid=(steps,),
        in_specs=[SMEM, whole(*prolong.shape), whole(WIDE, 2 * COLS), part(COLS)] + [part(2 * WIDE)] * 2,
        out_specs=[part(WIDE), part(PAIR), part(2 * COLS)] + [whole(COARSE, WIDE)] * 2,
        out_shape=[
            shape(WIDE, WIDE),
            shape(WIDE, PAIR),
            shape(WIDE, 2 * COLS),
            shape(COARSE, WIDE, dtype=BF16),
            shape(COARSE, WIDE, dtype=BF16),
        ],
        scratch_shapes=[pltpu.VMEM((WIDE, PAIR), BF16)] * 2,
        compiler_params=params(),
        name="own_step",
    )(agg_of, prolong, message, right, pair, pair_other)


def image_kernel(own_image, side, received, received_other, message, keep_ref, send_ref, high_ref, low_ref):
    core = lax.axis_index("sub") & 1
    field = halves(message[:WIDE, :])
    rows = WIDE // 2
    for group in range(2):
        part = span(group, rows)
        extra = jnp.where(core == group, received[...], received_other[...])
        high, low = halves(side[part, :] + extra)
        high_ref[part, :] = high
        low_ref[part, :] = low
        total = own_image[part, :] + product((high, low), field)
        keep_ref[part, :] = total[:, :COLS]
        send_ref[part, :] = total[:, COLS:]


def image(own_image, side, received, received_other, message):
    return pl.pallas_call(
        image_kernel,
        in_specs=[VMEM] * 5,
        out_specs=[VMEM] * 4,
        out_shape=[shape(WIDE, COLS)] * 2 + [shape(WIDE, WIDE, dtype=BF16)] * 2,
        compiler_params=params(),
        name="image",
    )(own_image, side, received, received_other, message)


def ghost_kernel(agg_of, d_high, d_low, mine, other, half_ref, q_high, q_low):
    _, near, far = neighbours()
    sub = lax.axis_index("sub")
    core = sub & 1
    start = jnp.where(((sub >> 1) & 1) == 0, near, far) * ROWS
    for r in range(ROWS):
        columns = span(r % HALF_ROWS)
        piece = jnp.where(core == r // HALF_ROWS, mine[:, columns], other[:, columns])
        high, low = halves(placed(piece, agg_of[start + r] - 2 * core))
        q_high[span(r), :] = high
        q_low[span(r), :] = low
    half_ref[...] = product((d_high[...], d_low[...]), (q_high[...], q_low[...]))


def ghost_step(agg_of, d_high, d_low, mine, other):
    return pl.pallas_call(
        ghost_kernel,
        in_specs=[SMEM] + [VMEM] * 4,
        out_specs=VMEM,
        out_shape=shape(WIDE, PAIR),
        scratch_shapes=[pltpu.VMEM((WIDE, PAIR), BF16)] * 2,
        compiler_params=params(),
        name="ghost_step",
    )(agg_of, d_high, d_low, mine, other)


def scaled_by_weight(agg_of, value):
    start = lax.axis_index("slab") * ROWS
    pieces = []
    for a in range(GROUPS):
        members = jnp.zeros((), jnp.int32)
        for e in range(ROWS):
            members += jnp.where(agg_of[start + e] == a, 1, 0)
        piece = value[span(a), :]
        pieces.append(piece * (COARSE_WEIGHT / jnp.full(piece.shape, members.astype(F32))))
    return jnp.concatenate(pieces, axis=0)


def coarse_kernel(own, own_received, side, side_received, rt_high, rt_low, g_ref, coarse_ref):
    is_near = ((lax.axis_index("sub") >> 1) & 1) == 0
    g_ref[:, span(0, PAIR)] = jnp.where(is_near, side[...], side_received[...])
    g_ref[:, span(1, PAIR)] = own[...] + own_received[...]
    g_ref[:, span(2, PAIR)] = jnp.where(is_near, side_received[...], side[...])
    coarse_ref[...] = product((rt_high[...], rt_low[...]), halves(g_ref[...]))


def coarse_half(own, own_received, side, side_received, rt_high, rt_low):
    return pl.pallas_call(
        coarse_kernel,
        in_specs=[VMEM] * 6,
        out_specs=[VMEM] * 2,
        out_shape=[shape(WIDE, 3 * PAIR), shape(COARSE, 3 * PAIR)],
        compiler_params=params(),
        name="coarse_half",
    )(own, own_received, side, side_received, rt_high, rt_low)


def share_kernel(mine, other, op_ref, natural):
    sub = lax.axis_index("sub")
    odd = lax.axis_index("slab") & 1
    is_first = (sub & 1) == 0
    first = jnp.where(is_first, mine[...], other[...])
    second = jnp.where(is_first, other[...], mine[...])
    places = (2 * (1 - odd), 1, 2 * odd)
    for region, place in enumerate(places):
        value = jnp.concatenate([first[:, span(region, PAIR)], second[:, span(region, PAIR)]], axis=1)
        natural[:, aligned(place, COARSE)] = value
    share = op_ref.shape[1]
    for k in range(BANDS // share):

        @pl.when(sub == k)
        def _():
            for a in range(GROUPS):
                for q in range(share):
                    op_ref[a, q] = natural[span(a), span(k * share + q)]


def coarse_share(mine, other):
    return pl.pallas_call(
        share_kernel,
        in_specs=[VMEM] * 2,
        out_specs=VMEM,
        out_shape=shape(GROUPS, BANDS // SUBS, DOF, DOF),
        scratch_shapes=[pltpu.VMEM((COARSE, 3 * COARSE), F32)],
        compiler_params=params(),
        name="coarse_share",
    )(mine, other)


def lift_kernel(agg_of, g_half, smoother, prolong, w_ref):
    start = lax.axis_index("slab") * ROWS
    core = lax.axis_index("sub") & 1
    for e in range(ROWS):
        w_ref[span(e), :] = -product(halves(smoother[e]), halves(g_half[span(e), :]))
        w_ref[span(e), span(1, PAIR)] += placed(prolong[e], agg_of[start + e] - 2 * core)


def lift_half(agg_of, g_half, smoother, prolong):
    return pl.pallas_call(
        lift_kernel,
        in_specs=[SMEM] + [VMEM] * 3,
        out_specs=VMEM,
        out_shape=shape(WIDE, 3 * PAIR),
        compiler_params=params(),
        name="lift_half",
    )(agg_of, g_half, smoother, prolong)


def residual_kernel(agg_of, keep, received, rt_high, rt_low, residual_ref, first_ref):
    residual = -(keep[...] + received[...])
    residual_ref[...] = residual
    first_ref[...] = scaled_by_weight(agg_of, narrow_product((rt_high[...], rt_low[...]), residual))


def residual_step(agg_of, keep, received, rt_high, rt_low):
    return pl.pallas_call(
        residual_kernel,
        in_specs=[SMEM] + [VMEM] * 4,
        out_specs=[VMEM] * 2,
        out_shape=[shape(WIDE, COLS), shape(COARSE, COLS)],
        compiler_params=params(),
        name="residual_step",
    )(agg_of, keep, received, rt_high, rt_low)


def base_kernel(smoother, message, residual, base_ref):
    for e in range(ROWS):
        smoothed = narrow_product(halves(smoother[e]), residual[span(e), :])
        base_ref[span(e), :] = message[span(e), :COLS] + smoothed


def base_step(smoother, message, residual):
    return pl.pallas_call(
        base_kernel,
        in_specs=[VMEM] * 3,
        out_specs=VMEM,
        out_shape=shape(WIDE, COLS),
        compiler_params=params(),
        name="base_step",
    )(smoother, message, residual)


def core_parts(*fields):
    core = lax.axis_index("sub") & 1
    for which in (core, 1 - core):
        yield jnp.concatenate([field[aligned(which, PAIR), :] for field in fields], axis=0)


def sweep_kernel(agg_of, mine, other, first, near, own, far, next_ref):
    total = None
    for operator, field in zip((mine, other), core_parts(near, own, far)):
        part = narrow_product(halves(operator[...]), field)
        total = part if total is None else total + part
    next_ref[...] = own[...] + first[...] - scaled_by_weight(agg_of, total)


def sweep(agg_of, mine, other, first, near, own, far):
    return pl.pallas_call(
        sweep_kernel,
        in_specs=[SMEM] + [VMEM] * 6,
        out_specs=VMEM,
        out_shape=shape(COARSE, COLS),
        compiler_params=params(),
        name="sweep",
    )(agg_of, mine, other, first, near, own, far)


def lifted_kernel(mine, other, base, own, base_ref, high_ref, low_ref):
    total = base[...]
    for place, (operator, field) in enumerate(zip((mine, other), core_parts(own))):
        total += narrow_product(halves(operator[:, span(1, PAIR)]), field)
        for t, region in enumerate((0, 2)):
            high, low = halves(operator[:, span(region, PAIR)])
            high_ref[:, span(2 * place + t, PAIR)] = high
            low_ref[:, span(2 * place + t, PAIR)] = low
    base_ref[...] = total


def lifted(mine, other, base, own):
    return pl.pallas_call(
        lifted_kernel,
        in_specs=[VMEM] * 4,
        out_specs=[VMEM] * 3,
        out_shape=[shape(WIDE, COLS)] + [shape(WIDE, 2 * COARSE, dtype=BF16)] * 2,
        compiler_params=params(),
        name="lifted",
    )(mine, other, base, own)


def last_kernel(w_high, w_low, base, near, far, out_ref):
    field = jnp.concatenate(list(core_parts(near, far)), axis=0)
    out_ref[...] = base[...] + narrow_product((w_high[...], w_low[...]), field)


def last_step(w_high, w_low, base, near, far):
    return pl.pallas_call(
        last_kernel,
        in_specs=[VMEM] * 5,
        out_specs=VMEM,
        out_shape=shape(WIDE, COLS),
        compiler_params=params(),
        name="last_step",
    )(w_high, w_low, base, near, far)


def swaps(size, start):
    pairs = [(i, i + 1) for i in range(start, size - 1, 2)]
    return pairs + [(j, i) for i, j in pairs]


def from_neighbours(value):
    size = lax.axis_size("slab")
    far = lax.ppermute(value, "slab", swaps(size, 1))
    near = lax.ppermute(value, "slab", swaps(size, 0))
    return near, far


def from_side(value):
    size, subs = lax.axis_size("slab"), lax.axis_size("sub")
    pairs = [
        (i * subs + k, j * subs + k) for k in range(subs) for i, j in swaps(size, (k >> 1) & 1)
    ]
    return lax.ppermute(value, ("slab", "sub"), pairs)


def swapped(value, bit):
    size = lax.axis_size("sub")
    return lax.ppermute(value, "sub", [(i, i ^ bit) for i in range(size)])


def per_device(fine_blocks, prolong, smoother, right_side, agg_of, col_slot, send_rows, send_count):
    pair, mine, theirs, message, right = start_step(
        col_slot, send_rows, send_count, fine_blocks, smoother, right_side, prolong
    )
    side_message = from_side(message)
    theirs = swapped(theirs, 1)
    received = swapped(mine + theirs, 2)
    pair, theirs = lax.optimization_barrier((pair, theirs))
    side, own_half, own_image, rt_high, rt_low = own_step(agg_of, prolong, message, right, pair, swapped(pair, 1))
    received, side, side_message, own_half = lax.optimization_barrier((received, side, side_message, own_half))
    own_received = swapped(own_half, 2)
    keep, send, d_high, d_low = image(own_image, side, received, swapped(received, 1), side_message)
    image_received = swapped(send, 2)
    ghosts = side_message[WIDE:]
    side_half = ghost_step(agg_of, d_high, d_low, ghosts, swapped(ghosts, 1))
    side_received = swapped(side_half, 2)
    residual, first = residual_step(agg_of, keep, image_received, rt_high, rt_low)
    base = base_step(smoother, message, residual)
    near, far = from_neighbours(first)
    near, far, side_received = lax.optimization_barrier((near, far, side_received))
    g_half, coarse = coarse_half(own_half, own_received, side_half, side_received, rt_high, rt_low)
    coarse_other = swapped(coarse, 1)
    coarse_op = coarse_share(coarse, coarse_other)
    correction = first
    for index in range(COARSE_SWEEPS - 1):
        if index > 0:
            near, far = from_neighbours(correction)
        if index == 1:
            lift_other, near, far = lax.optimization_barrier((lift_other, near, far))
        correction = sweep(agg_of, coarse, coarse_other, first, near, correction, far)
        if index == 0:
            g_half, correction = lax.optimization_barrier((g_half, correction))
            lift = lift_half(agg_of, g_half, smoother, prolong)
            lift_other = swapped(lift, 1)
    near, far = from_neighbours(correction)
    base, w_high, w_low = lifted(lift, lift_other, base, correction)
    solution = last_step(w_high, w_low, base, near, far)
    return coarse_op, solution.reshape(ROWS, DOF, COLS)


def solution(mesh):
    placed_args = (
        P("slab", "sub", None, None),
        P("slab", None, None),
        P("slab", None, None),
        P("slab", None, None),
        P(),
        P("slab", "sub"),
        P(),
        P(),
    )
    return jax.shard_map(
        per_device,
        mesh=mesh,
        in_specs=placed_args,
        out_specs=(P("slab", "sub", None, None), P("slab", None, "sub")),
        check_vma=False,
    )
```

```python
import jax
import jax.numpy as jnp
from jax import lax
from jax.experimental import pallas as pl
from jax.experimental.pallas import tpu as pltpu
from jax.sharding import PartitionSpec as P

COARSE_SWEEPS = 3
COARSE_WEIGHT = 0.25
F32 = jnp.float32
BF16 = jnp.bfloat16
VMEM = pl.BlockSpec(memory_space=pltpu.VMEM)
SMEM = pl.BlockSpec(memory_space=pltpu.SMEM)
HBM = pl.BlockSpec(memory_space=pltpu.HBM)
ROWS = 8
GHOSTS = 8
SLOTS = ROWS + 2 * GHOSTS
GROUPS = 4
BANDS = 3 * GROUPS
DOF = 64
COLS = 128
SUBS = 4
HALF_ROWS = ROWS // 2
WIDE = ROWS * DOF
PAIR = 2 * DOF
COARSE = GROUPS * DOF


def params(limit=24):
    return pltpu.CompilerParams(vmem_limit_bytes=limit << 20)


def shape(*dims, dtype=F32):
    return jax.ShapeDtypeStruct(dims, dtype)


def halves(value):
    high = value.astype(BF16)
    return high, (value - high.astype(F32)).astype(BF16)


def mm(a, b):
    return jnp.dot(a, b, preferred_element_type=F32)


def product(left, right):
    left_high, left_low = left
    right_high, right_low = right
    return mm(left_high, right_high) + (mm(left_high, right_low) + mm(left_low, right_high))


def narrow_product(left, value):
    left_high, left_low = left
    high, low = halves(value)
    width = value.shape[1]
    both = mm(left_high, jnp.concatenate([high, low], axis=1))
    return both[:, :width] + (both[:, width:] + mm(left_low, high))


def span(index, size=DOF):
    return slice(index * size, (index + 1) * size)


def aligned(index, size):
    return pl.ds(pl.multiple_of(index * size, size), size)


def neighbours():
    slab, size = lax.axis_index("slab"), lax.axis_size("slab")
    odd = slab & 1
    near = jnp.minimum(slab ^ 1, size - 1)
    far = jnp.where(odd == 1, jnp.minimum(slab + 1, size - 1), jnp.maximum(slab - 1, 0))
    return slab, near, far


def start_kernel(
    col_hbm, rows_hbm, counts_hbm, blocks_hbm, smoother_hbm, right_hbm, prolong_hbm,
    pair_ref, mine_ref, theirs_ref, message_ref, right_ref,
    col_slot, rows, counts, blocks, smoother, right, prolong, sems, block_sems, *parts
):
    slab, size, sub = lax.axis_index("slab"), lax.axis_size("slab"), lax.axis_index("sub")
    below = jnp.maximum(slab - 1, 0)
    above = jnp.minimum(slab + 1, size - 1)
    core = sub & 1
    chip = (sub >> 1) & 1
    sources = [
        (smoother_hbm, smoother),
        (right_hbm.at[:, :, aligned(sub, COLS)], right.at[0]),
        (right_hbm.at[:, :, aligned(sub ^ 2, COLS)], right.at[1]),
        (prolong_hbm.at[pl.ds(core * HALF_ROWS, HALF_ROWS)], prolong),
        (col_hbm, col_slot),
        (rows_hbm.at[below, sub], rows.at[0]),
        (rows_hbm.at[above, sub], rows.at[1]),
        (counts_hbm.at[sub], counts),
    ]
    copies = [pltpu.make_async_copy(s, d, sems.at[i]) for i, (s, d) in enumerate(sources)]
    block_copies = [
        pltpu.make_async_copy(blocks_hbm.at[e], blocks.at[e], block_sems.at[e]) for e in range(ROWS)
    ]
    for copy in copies + block_copies:
        copy.start()
    for copy in copies:
        copy.wait()

    for e in range(ROWS):
        right_ref[span(e), :] = right[0, e]
        wide = jnp.concatenate([right[0, e], right[1, e]], axis=1)
        message_ref[span(e), :] = product(halves(smoother[e]), halves(wide))
    message_ref[span(ROWS), :] = jnp.concatenate([prolong[i] for i in range(HALF_ROWS)], axis=1)

    lower_count = jnp.where(slab > 0, counts[1, below], 0)
    upper_count = jnp.where(slab < size - 1, counts[0, above], 0)
    lower_region = 1 + (1 - (slab & 1) ^ chip)
    lower_start = lower_region * ROWS
    upper_start = (3 - lower_region) * ROWS
    upper_lanes = lax.broadcasted_iota(jnp.int32, (DOF, PAIR), 1) >= DOF
    for group in range(ROWS // HALF_ROWS):
        for position, part in enumerate(parts):
            part[...] = jnp.zeros_like(part)
            block_copies[group * HALF_ROWS + position].wait()
        for j in range(blocks.shape[1]):
            for position, part in enumerate(parts):
                e = group * HALF_ROWS + position
                slot = col_slot[e, j]
                is_own = slot < ROWS
                is_upper = slot >= ROWS + GHOSTS
                side = jnp.where(is_upper, 1, 0)
                place = jnp.where(is_own, 0, slot - ROWS - side * GHOSTS)
                listed = rows[side, 1 - side, place] + jnp.where(is_upper, upper_start, lower_start)
                column = jnp.where(is_own, slot, listed)
                count = jnp.where(is_upper, upper_count, lower_count)
                live = jnp.where(is_own | (place < count), 1.0, 0.0)
                odd_column = column & 1
                lower_scale = jnp.where(odd_column == 0, live, 0.0)
                upper_scale = jnp.where(odd_column == 1, live, 0.0)
                block = blocks[e, j]
                doubled = jnp.concatenate([block, block], axis=1)
                part[:, aligned(column >> 1, PAIR)] += doubled * jnp.where(upper_lanes, upper_scale, lower_scale)
        for position, part in enumerate(parts):
            pair_ref[span(group * HALF_ROWS + position), :] = part[:, : 2 * WIDE]

        @pl.when(core == group)
        def _():
            for position, part in enumerate(parts):
                mine_ref[span(position), :] = part[:, 2 * WIDE :]

        @pl.when(core != group)
        def _():
            for position, part in enumerate(parts):
                theirs_ref[span(position), :] = part[:, 2 * WIDE :]


def start_step(col_slot, send_rows, send_count, blocks, smoother, right_side, prolong):
    counts = jnp.transpose(send_count, (1, 2, 0))
    arrays = (col_slot, send_rows, counts, blocks, smoother, right_side, prolong)
    return pl.pallas_call(
        start_kernel,
        in_specs=[HBM] * 7,
        out_specs=[VMEM] * 5,
        out_shape=[
            shape(WIDE, 2 * WIDE),
            shape(WIDE // 2, WIDE),
            shape(WIDE // 2, WIDE),
            shape(WIDE + DOF, 2 * COLS),
            shape(WIDE, COLS),
        ],
        scratch_shapes=[
            pltpu.SMEM(col_slot.shape, jnp.int32),
            pltpu.SMEM((2, 2, GHOSTS), jnp.int32),
            pltpu.SMEM((2, send_count.shape[0]), jnp.int32),
            pltpu.VMEM(blocks.shape, F32),
            pltpu.VMEM(smoother.shape, F32),
            pltpu.VMEM((2, ROWS, DOF, COLS), F32),
            pltpu.VMEM((HALF_ROWS, DOF, DOF), F32),
            pltpu.SemaphoreType.DMA((8,)),
            pltpu.SemaphoreType.DMA((ROWS,)),
        ]
        + [pltpu.VMEM((DOF, 3 * WIDE), F32)] * HALF_ROWS,
        compiler_params=params(),
        name="start_step",
    )(*(pltpu.with_memory_space_constraint(a, pltpu.HBM) for a in arrays))


def placed(piece, index):
    upper = lax.broadcasted_iota(jnp.int32, (DOF, PAIR), 1) >= DOF
    doubled = jnp.concatenate([piece, piece], axis=1)
    lower_scale = jnp.where(index == 0, 1.0, 0.0)
    upper_scale = jnp.where(index == 1, 1.0, 0.0)
    return doubled * jnp.where(upper, upper_scale, lower_scale)


def own_kernel(
    agg_of, prolong, field, right, pair, pair_other, side_ref, half_ref, image_ref, rt_high, rt_low, q_high, q_low
):
    start = lax.axis_index("slab") * ROWS
    core = lax.axis_index("sub") & 1

    @pl.when(pl.program_id(0) == 0)
    def _():
        restrict_rows = []
        for e in range(ROWS):
            group = agg_of[start + e]
            high, low = halves(placed(prolong[e], group - 2 * core))
            q_high[span(e), :] = high
            q_low[span(e), :] = low
            parts = [placed(prolong[e], group - 2 * t) for t in range(GROUPS // 2)]
            restrict_rows.append(jnp.concatenate(parts, axis=1))
        high, low = halves(jnp.concatenate(restrict_rows, axis=0).T)
        rt_high[...] = high
        rt_low[...] = low

    side_ref[...] = pair[:, WIDE:] + pair_other[:, WIDE:]
    own = halves(pair[:, :WIDE] + pair_other[:, :WIDE])
    half_ref[...] = product(own, (q_high[...], q_low[...]))
    total = product(own, halves(field[...]))
    image_ref[:, :COLS] = total[:, :COLS] - right[...]
    image_ref[:, COLS:] = total[:, COLS:]


def own_step(agg_of, prolong, message, right, pair, pair_other):
    steps = 2
    whole = lambda *dims: pl.BlockSpec(dims, lambda i: (0,) * len(dims))
    part = lambda width: pl.BlockSpec((WIDE // steps, width), lambda i: (i, 0))
    return pl.pallas_call(
        own_kernel,
        grid=(steps,),
        in_specs=[SMEM, whole(*prolong.shape), whole(WIDE, 2 * COLS), part(COLS)] + [part(2 * WIDE)] * 2,
        out_specs=[part(WIDE), part(PAIR), part(2 * COLS)] + [whole(COARSE, WIDE)] * 2,
        out_shape=[
            shape(WIDE, WIDE),
            shape(WIDE, PAIR),
            shape(WIDE, 2 * COLS),
            shape(COARSE, WIDE, dtype=BF16),
            shape(COARSE, WIDE, dtype=BF16),
        ],
        scratch_shapes=[pltpu.VMEM((WIDE, PAIR), BF16)] * 2,
        compiler_params=params(),
        name="own_step",
    )(agg_of, prolong, message, right, pair, pair_other)


def image_kernel(own_image, side, received, received_other, message, keep_ref, send_ref, high_ref, low_ref):
    core = lax.axis_index("sub") & 1
    field = halves(message[:WIDE, :])
    rows = WIDE // 2
    for group in range(2):
        part = span(group, rows)
        extra = jnp.where(core == group, received[...], received_other[...])
        high, low = halves(side[part, :] + extra)
        high_ref[part, :] = high
        low_ref[part, :] = low
        total = own_image[part, :] + product((high, low), field)
        keep_ref[part, :] = total[:, :COLS]
        send_ref[part, :] = total[:, COLS:]


def image(own_image, side, received, received_other, message):
    return pl.pallas_call(
        image_kernel,
        in_specs=[VMEM] * 5,
        out_specs=[VMEM] * 4,
        out_shape=[shape(WIDE, COLS)] * 2 + [shape(WIDE, WIDE, dtype=BF16)] * 2,
        compiler_params=params(),
        name="image",
    )(own_image, side, received, received_other, message)


def ghost_kernel(agg_of, d_high, d_low, mine, other, half_ref, q_high, q_low):
    _, near, far = neighbours()
    sub = lax.axis_index("sub")
    core = sub & 1
    start = jnp.where(((sub >> 1) & 1) == 0, near, far) * ROWS
    for r in range(ROWS):
        columns = span(r % HALF_ROWS)
        piece = jnp.where(core == r // HALF_ROWS, mine[:, columns], other[:, columns])
        high, low = halves(placed(piece, agg_of[start + r] - 2 * core))
        q_high[span(r), :] = high
        q_low[span(r), :] = low
    half_ref[...] = product((d_high[...], d_low[...]), (q_high[...], q_low[...]))


def ghost_step(agg_of, d_high, d_low, mine, other):
    return pl.pallas_call(
        ghost_kernel,
        in_specs=[SMEM] + [VMEM] * 4,
        out_specs=VMEM,
        out_shape=shape(WIDE, PAIR),
        scratch_shapes=[pltpu.VMEM((WIDE, PAIR), BF16)] * 2,
        compiler_params=params(),
        name="ghost_step",
    )(agg_of, d_high, d_low, mine, other)


def scaled_by_weight(agg_of, value):
    start = lax.axis_index("slab") * ROWS
    pieces = []
    for a in range(GROUPS):
        members = jnp.zeros((), jnp.int32)
        for e in range(ROWS):
            members += jnp.where(agg_of[start + e] == a, 1, 0)
        piece = value[span(a), :]
        pieces.append(piece * (COARSE_WEIGHT / jnp.full(piece.shape, members.astype(F32))))
    return jnp.concatenate(pieces, axis=0)


def coarse_kernel(own, own_received, side, side_received, rt_high, rt_low, g_ref, coarse_ref):
    is_near = ((lax.axis_index("sub") >> 1) & 1) == 0
    g_ref[:, span(0, PAIR)] = jnp.where(is_near, side[...], side_received[...])
    g_ref[:, span(1, PAIR)] = own[...] + own_received[...]
    g_ref[:, span(2, PAIR)] = jnp.where(is_near, side_received[...], side[...])
    coarse_ref[...] = product((rt_high[...], rt_low[...]), halves(g_ref[...]))


def coarse_half(own, own_received, side, side_received, rt_high, rt_low):
    return pl.pallas_call(
        coarse_kernel,
        in_specs=[VMEM] * 6,
        out_specs=[VMEM] * 2,
        out_shape=[shape(WIDE, 3 * PAIR), shape(COARSE, 3 * PAIR)],
        compiler_params=params(),
        name="coarse_half",
    )(own, own_received, side, side_received, rt_high, rt_low)


def share_kernel(mine, other, op_ref, natural):
    sub = lax.axis_index("sub")
    odd = lax.axis_index("slab") & 1
    is_first = (sub & 1) == 0
    first = jnp.where(is_first, mine[...], other[...])
    second = jnp.where(is_first, other[...], mine[...])
    places = (2 * (1 - odd), 1, 2 * odd)
    for region, place in enumerate(places):
        value = jnp.concatenate([first[:, span(region, PAIR)], second[:, span(region, PAIR)]], axis=1)
        natural[:, aligned(place, COARSE)] = value
    share = op_ref.shape[1]
    for k in range(BANDS // share):

        @pl.when(sub == k)
        def _():
            for a in range(GROUPS):
                for q in range(share):
                    op_ref[a, q] = natural[span(a), span(k * share + q)]


def coarse_share(mine, other):
    return pl.pallas_call(
        share_kernel,
        in_specs=[VMEM] * 2,
        out_specs=VMEM,
        out_shape=shape(GROUPS, BANDS // SUBS, DOF, DOF),
        scratch_shapes=[pltpu.VMEM((COARSE, 3 * COARSE), F32)],
        compiler_params=params(),
        name="coarse_share",
    )(mine, other)


def lift_kernel(agg_of, g_half, smoother, prolong, w_ref):
    start = lax.axis_index("slab") * ROWS
    core = lax.axis_index("sub") & 1
    for e in range(ROWS):
        w_ref[span(e), :] = -product(halves(smoother[e]), halves(g_half[span(e), :]))
        w_ref[span(e), span(1, PAIR)] += placed(prolong[e], agg_of[start + e] - 2 * core)


def lift_half(agg_of, g_half, smoother, prolong):
    return pl.pallas_call(
        lift_kernel,
        in_specs=[SMEM] + [VMEM] * 3,
        out_specs=VMEM,
        out_shape=shape(WIDE, 3 * PAIR),
        compiler_params=params(),
        name="lift_half",
    )(agg_of, g_half, smoother, prolong)


def residual_kernel(agg_of, keep, received, rt_high, rt_low, residual_ref, first_ref):
    residual = -(keep[...] + received[...])
    residual_ref[...] = residual
    first_ref[...] = scaled_by_weight(agg_of, narrow_product((rt_high[...], rt_low[...]), residual))


def residual_step(agg_of, keep, received, rt_high, rt_low):
    return pl.pallas_call(
        residual_kernel,
        in_specs=[SMEM] + [VMEM] * 4,
        out_specs=[VMEM] * 2,
        out_shape=[shape(WIDE, COLS), shape(COARSE, COLS)],
        compiler_params=params(),
        name="residual_step",
    )(agg_of, keep, received, rt_high, rt_low)


def base_kernel(smoother, message, residual, base_ref):
    for e in range(ROWS):
        smoothed = narrow_product(halves(smoother[e]), residual[span(e), :])
        base_ref[span(e), :] = message[span(e), :COLS] + smoothed


def base_step(smoother, message, residual):
    return pl.pallas_call(
        base_kernel,
        in_specs=[VMEM] * 3,
        out_specs=VMEM,
        out_shape=shape(WIDE, COLS),
        compiler_params=params(),
        name="base_step",
    )(smoother, message, residual)


def core_parts(*fields):
    core = lax.axis_index("sub") & 1
    for which in (core, 1 - core):
        yield jnp.concatenate([field[aligned(which, PAIR), :] for field in fields], axis=0)


def sweep_kernel(agg_of, mine, other, first, near, own, far, next_ref):
    total = None
    for operator, field in zip((mine, other), core_parts(near, own, far)):
        part = narrow_product(halves(operator[...]), field)
        total = part if total is None else total + part
    next_ref[...] = own[...] + first[...] - scaled_by_weight(agg_of, total)


def sweep(agg_of, mine, other, first, near, own, far):
    return pl.pallas_call(
        sweep_kernel,
        in_specs=[SMEM] + [VMEM] * 6,
        out_specs=VMEM,
        out_shape=shape(COARSE, COLS),
        compiler_params=params(),
        name="sweep",
    )(agg_of, mine, other, first, near, own, far)


def lifted_kernel(mine, other, base, own, base_ref, high_ref, low_ref):
    total = base[...]
    for place, (operator, field) in enumerate(zip((mine, other), core_parts(own))):
        total += narrow_product(halves(operator[:, span(1, PAIR)]), field)
        for t, region in enumerate((0, 2)):
            high, low = halves(operator[:, span(region, PAIR)])
            high_ref[:, span(2 * place + t, PAIR)] = high
            low_ref[:, span(2 * place + t, PAIR)] = low
    base_ref[...] = total


def lifted(mine, other, base, own):
    return pl.pallas_call(
        lifted_kernel,
        in_specs=[VMEM] * 4,
        out_specs=[VMEM] * 3,
        out_shape=[shape(WIDE, COLS)] + [shape(WIDE, 2 * COARSE, dtype=BF16)] * 2,
        compiler_params=params(),
        name="lifted",
    )(mine, other, base, own)


def last_kernel(w_high, w_low, base, near, far, out_ref):
    field = jnp.concatenate(list(core_parts(near, far)), axis=0)
    out_ref[...] = base[...] + narrow_product((w_high[...], w_low[...]), field)


def last_step(w_high, w_low, base, near, far):
    return pl.pallas_call(
        last_kernel,
        in_specs=[VMEM] * 5,
        out_specs=VMEM,
        out_shape=shape(WIDE, COLS),
        compiler_params=params(),
        name="last_step",
    )(w_high, w_low, base, near, far)


def swaps(size, start):
    pairs = [(i, i + 1) for i in range(start, size - 1, 2)]
    return pairs + [(j, i) for i, j in pairs]


def from_neighbours(value):
    size = lax.axis_size("slab")
    near = lax.ppermute(value, "slab", swaps(size, 0))
    far = lax.ppermute(value, "slab", swaps(size, 1))
    return near, far


def from_side(value):
    size, subs = lax.axis_size("slab"), lax.axis_size("sub")
    pairs = [
        (i * subs + k, j * subs + k) for k in range(subs) for i, j in swaps(size, (k >> 1) & 1)
    ]
    return lax.ppermute(value, ("slab", "sub"), pairs)


def swapped(value, bit):
    size = lax.axis_size("sub")
    return lax.ppermute(value, "sub", [(i, i ^ bit) for i in range(size)])


def per_device(fine_blocks, prolong, smoother, right_side, agg_of, col_slot, send_rows, send_count):
    pair, mine, theirs, message, right = start_step(
        col_slot, send_rows, send_count, fine_blocks, smoother, right_side, prolong
    )
    side_message = from_side(message)
    theirs = swapped(theirs, 1)
    received = swapped(mine + theirs, 2)
    pair, theirs = lax.optimization_barrier((pair, theirs))
    side, own_half, own_image, rt_high, rt_low = own_step(agg_of, prolong, message, right, pair, swapped(pair, 1))
    received, side, own_half = lax.optimization_barrier((received, side, own_half))
    own_received = swapped(own_half, 2)
    keep, send, d_high, d_low = image(own_image, side, received, swapped(received, 1), side_message)
    send, own_received = lax.optimization_barrier((send, own_received))
    image_received = swapped(send, 2)
    ghosts = side_message[WIDE:]
    side_half = ghost_step(agg_of, d_high, d_low, ghosts, swapped(ghosts, 1))
    side_received = swapped(side_half, 2)
    residual, first = residual_step(agg_of, keep, image_received, rt_high, rt_low)
    base = base_step(smoother, message, residual)
    near, far = from_neighbours(first)
    g_half, coarse = coarse_half(own_half, own_received, side_half, side_received, rt_high, rt_low)
    near, far, coarse = lax.optimization_barrier((near, far, coarse))
    coarse_other = swapped(coarse, 1)
    coarse_op = coarse_share(coarse, coarse_other)
    lift = lift_half(agg_of, g_half, smoother, prolong)
    correction = first
    for index in range(COARSE_SWEEPS - 1):
        if index > 0:
            near, far = from_neighbours(correction)
            lift, near, far = lax.optimization_barrier((lift, near, far))
        correction = sweep(agg_of, coarse, coarse_other, first, near, correction, far)
    lift_other = swapped(lift, 1)
    near, far = from_neighbours(correction)
    base, w_high, w_low = lifted(lift, lift_other, base, correction)
    solution = last_step(w_high, w_low, base, near, far)
    return coarse_op, solution.reshape(ROWS, DOF, COLS)


def solution(mesh):
    placed_args = (
        P("slab", "sub", None, None),
        P("slab", None, None),
        P("slab", None, None),
        P("slab", None, None),
        P(),
        P("slab", "sub"),
        P(),
        P(),
    )
    return jax.shard_map(
        per_device,
        mesh=mesh,
        in_specs=placed_args,
        out_specs=(P("slab", "sub", None, None), P("slab", None, "sub")),
        check_vma=False,
    )
```

```python
import jax
import jax.numpy as jnp
from jax import lax
from jax.experimental import pallas as pl
from jax.experimental.pallas import tpu as pltpu
from jax.sharding import PartitionSpec as P

COARSE_SWEEPS = 3
COARSE_WEIGHT = 0.25
F32 = jnp.float32
BF16 = jnp.bfloat16
VMEM = pl.BlockSpec(memory_space=pltpu.VMEM)
SMEM = pl.BlockSpec(memory_space=pltpu.SMEM)
HBM = pl.BlockSpec(memory_space=pltpu.HBM)
ROWS = 8
GHOSTS = 8
SLOTS = ROWS + 2 * GHOSTS
GROUPS = 4
BANDS = 3 * GROUPS
DOF = 64
COLS = 128
SUBS = 4
HALF_ROWS = ROWS // 2
WIDE = ROWS * DOF
PAIR = 2 * DOF
COARSE = GROUPS * DOF


def params(limit=24):
    return pltpu.CompilerParams(vmem_limit_bytes=limit << 20)


def shape(*dims, dtype=F32):
    return jax.ShapeDtypeStruct(dims, dtype)


def halves(value):
    high = value.astype(BF16)
    return high, (value - high.astype(F32)).astype(BF16)


def mm(a, b):
    return jnp.dot(a, b, preferred_element_type=F32)


def product(left, right):
    left_high, left_low = left
    right_high, right_low = right
    return mm(left_high, right_high) + (mm(left_high, right_low) + mm(left_low, right_high))


def narrow_product(left, value):
    left_high, left_low = left
    high, low = halves(value)
    width = value.shape[1]
    both = mm(left_high, jnp.concatenate([high, low], axis=1))
    return both[:, :width] + (both[:, width:] + mm(left_low, high))


def span(index, size=DOF):
    return slice(index * size, (index + 1) * size)


def aligned(index, size):
    return pl.ds(pl.multiple_of(index * size, size), size)


def neighbours():
    slab, size = lax.axis_index("slab"), lax.axis_size("slab")
    odd = slab & 1
    near = jnp.minimum(slab ^ 1, size - 1)
    far = jnp.where(odd == 1, jnp.minimum(slab + 1, size - 1), jnp.maximum(slab - 1, 0))
    return slab, near, far


def start_kernel(
    col_hbm, rows_hbm, counts_hbm, blocks_hbm, smoother_hbm, right_hbm, prolong_hbm,
    pair_ref, mine_ref, theirs_ref, message_ref, right_ref,
    col_slot, rows, counts, blocks, smoother, right, prolong, sems, block_sems, *parts
):
    slab, size, sub = lax.axis_index("slab"), lax.axis_size("slab"), lax.axis_index("sub")
    below = jnp.maximum(slab - 1, 0)
    above = jnp.minimum(slab + 1, size - 1)
    core = sub & 1
    chip = (sub >> 1) & 1
    sources = [
        (smoother_hbm, smoother),
        (right_hbm.at[:, :, aligned(sub, COLS)], right.at[0]),
        (right_hbm.at[:, :, aligned(sub ^ 2, COLS)], right.at[1]),
        (prolong_hbm.at[pl.ds(core * HALF_ROWS, HALF_ROWS)], prolong),
        (col_hbm, col_slot),
        (rows_hbm.at[below, sub], rows.at[0]),
        (rows_hbm.at[above, sub], rows.at[1]),
        (counts_hbm.at[sub], counts),
    ]
    copies = [pltpu.make_async_copy(s, d, sems.at[i]) for i, (s, d) in enumerate(sources)]
    block_copies = [
        pltpu.make_async_copy(blocks_hbm.at[e], blocks.at[e], block_sems.at[e]) for e in range(ROWS)
    ]
    for copy in copies + block_copies:
        copy.start()
    for copy in copies:
        copy.wait()

    for e in range(ROWS):
        right_ref[span(e), :] = right[0, e]
        wide = jnp.concatenate([right[0, e], right[1, e]], axis=1)
        message_ref[span(e), :] = product(halves(smoother[e]), halves(wide))
    message_ref[span(ROWS), :] = jnp.concatenate([prolong[i] for i in range(HALF_ROWS)], axis=1)

    lower_count = jnp.where(slab > 0, counts[1, below], 0)
    upper_count = jnp.where(slab < size - 1, counts[0, above], 0)
    lower_region = 1 + (1 - (slab & 1) ^ chip)
    lower_start = lower_region * ROWS
    upper_start = (3 - lower_region) * ROWS
    upper_lanes = lax.broadcasted_iota(jnp.int32, (DOF, PAIR), 1) >= DOF
    for group in range(ROWS // HALF_ROWS):
        for position, part in enumerate(parts):
            part[...] = jnp.zeros_like(part)
            block_copies[group * HALF_ROWS + position].wait()
        for j in range(blocks.shape[1]):
            for position, part in enumerate(parts):
                e = group * HALF_ROWS + position
                slot = col_slot[e, j]
                is_own = slot < ROWS
                is_upper = slot >= ROWS + GHOSTS
                side = jnp.where(is_upper, 1, 0)
                place = jnp.where(is_own, 0, slot - ROWS - side * GHOSTS)
                listed = rows[side, 1 - side, place] + jnp.where(is_upper, upper_start, lower_start)
                column = jnp.where(is_own, slot, listed)
                count = jnp.where(is_upper, upper_count, lower_count)
                live = jnp.where(is_own | (place < count), 1.0, 0.0)
                odd_column = column & 1
                lower_scale = jnp.where(odd_column == 0, live, 0.0)
                upper_scale = jnp.where(odd_column == 1, live, 0.0)
                block = blocks[e, j]
                doubled = jnp.concatenate([block, block], axis=1)
                part[:, aligned(column >> 1, PAIR)] += doubled * jnp.where(upper_lanes, upper_scale, lower_scale)
        for position, part in enumerate(parts):
            pair_ref[span(group * HALF_ROWS + position), :] = part[:, : 2 * WIDE]

        @pl.when(core == group)
        def _():
            for position, part in enumerate(parts):
                mine_ref[span(position), :] = part[:, 2 * WIDE :]

        @pl.when(core != group)
        def _():
            for position, part in enumerate(parts):
                theirs_ref[span(position), :] = part[:, 2 * WIDE :]


def start_step(col_slot, send_rows, send_count, blocks, smoother, right_side, prolong):
    counts = jnp.transpose(send_count, (1, 2, 0))
    arrays = (col_slot, send_rows, counts, blocks, smoother, right_side, prolong)
    return pl.pallas_call(
        start_kernel,
        in_specs=[HBM] * 7,
        out_specs=[VMEM] * 5,
        out_shape=[
            shape(WIDE, 2 * WIDE),
            shape(WIDE // 2, WIDE),
            shape(WIDE // 2, WIDE),
            shape(WIDE + DOF, 2 * COLS),
            shape(WIDE, COLS),
        ],
        scratch_shapes=[
            pltpu.SMEM(col_slot.shape, jnp.int32),
            pltpu.SMEM((2, 2, GHOSTS), jnp.int32),
            pltpu.SMEM((2, send_count.shape[0]), jnp.int32),
            pltpu.VMEM(blocks.shape, F32),
            pltpu.VMEM(smoother.shape, F32),
            pltpu.VMEM((2, ROWS, DOF, COLS), F32),
            pltpu.VMEM((HALF_ROWS, DOF, DOF), F32),
            pltpu.SemaphoreType.DMA((8,)),
            pltpu.SemaphoreType.DMA((ROWS,)),
        ]
        + [pltpu.VMEM((DOF, 3 * WIDE), F32)] * HALF_ROWS,
        compiler_params=params(),
        name="start_step",
    )(*(pltpu.with_memory_space_constraint(a, pltpu.HBM) for a in arrays))


def placed(piece, index):
    upper = lax.broadcasted_iota(jnp.int32, (DOF, PAIR), 1) >= DOF
    doubled = jnp.concatenate([piece, piece], axis=1)
    lower_scale = jnp.where(index == 0, 1.0, 0.0)
    upper_scale = jnp.where(index == 1, 1.0, 0.0)
    return doubled * jnp.where(upper, upper_scale, lower_scale)


def own_kernel(
    agg_of, prolong, field, right, pair, pair_other, side_ref, half_ref, image_ref, rt_high, rt_low, q_high, q_low
):
    start = lax.axis_index("slab") * ROWS
    core = lax.axis_index("sub") & 1

    @pl.when(pl.program_id(0) == 0)
    def _():
        restrict_rows = []
        for e in range(ROWS):
            group = agg_of[start + e]
            high, low = halves(placed(prolong[e], group - 2 * core))
            q_high[span(e), :] = high
            q_low[span(e), :] = low
            parts = [placed(prolong[e], group - 2 * t) for t in range(GROUPS // 2)]
            restrict_rows.append(jnp.concatenate(parts, axis=1))
        high, low = halves(jnp.concatenate(restrict_rows, axis=0).T)
        rt_high[...] = high
        rt_low[...] = low

    side_ref[...] = pair[:, WIDE:] + pair_other[:, WIDE:]
    own = halves(pair[:, :WIDE] + pair_other[:, :WIDE])
    half_ref[...] = product(own, (q_high[...], q_low[...]))
    total = product(own, halves(field[...]))
    image_ref[:, :COLS] = total[:, :COLS] - right[...]
    image_ref[:, COLS:] = total[:, COLS:]


def own_step(agg_of, prolong, message, right, pair, pair_other):
    steps = 2
    whole = lambda *dims: pl.BlockSpec(dims, lambda i: (0,) * len(dims))
    part = lambda width: pl.BlockSpec((WIDE // steps, width), lambda i: (i, 0))
    return pl.pallas_call(
        own_kernel,
        grid=(steps,),
        in_specs=[SMEM, whole(*prolong.shape), whole(WIDE, 2 * COLS), part(COLS)] + [part(2 * WIDE)] * 2,
        out_specs=[part(WIDE), part(PAIR), part(2 * COLS)] + [whole(COARSE, WIDE)] * 2,
        out_shape=[
            shape(WIDE, WIDE),
            shape(WIDE, PAIR),
            shape(WIDE, 2 * COLS),
            shape(COARSE, WIDE, dtype=BF16),
            shape(COARSE, WIDE, dtype=BF16),
        ],
        scratch_shapes=[pltpu.VMEM((WIDE, PAIR), BF16)] * 2,
        compiler_params=params(),
        name="own_step",
    )(agg_of, prolong, message, right, pair, pair_other)


def image_kernel(own_image, side, received, received_other, message, keep_ref, send_ref, high_ref, low_ref):
    core = lax.axis_index("sub") & 1
    field = halves(message[:WIDE, :])
    rows = WIDE // 2
    for group in range(2):
        part = span(group, rows)
        extra = jnp.where(core == group, received[...], received_other[...])
        high, low = halves(side[part, :] + extra)
        high_ref[part, :] = high
        low_ref[part, :] = low
        total = own_image[part, :] + product((high, low), field)
        keep_ref[part, :] = total[:, :COLS]
        send_ref[part, :] = total[:, COLS:]


def image(own_image, side, received, received_other, message):
    return pl.pallas_call(
        image_kernel,
        in_specs=[VMEM] * 5,
        out_specs=[VMEM] * 4,
        out_shape=[shape(WIDE, COLS)] * 2 + [shape(WIDE, WIDE, dtype=BF16)] * 2,
        compiler_params=params(),
        name="image",
    )(own_image, side, received, received_other, message)


def ghost_kernel(agg_of, d_high, d_low, own_half, mine, other, rt_high, rt_low, parts_ref, coarse_ref, q_high, q_low):
    _, near, far = neighbours()
    sub = lax.axis_index("sub")
    core = sub & 1
    start = jnp.where(((sub >> 1) & 1) == 0, near, far) * ROWS
    for r in range(ROWS):
        columns = span(r % HALF_ROWS)
        piece = jnp.where(core == r // HALF_ROWS, mine[:, columns], other[:, columns])
        high, low = halves(placed(piece, agg_of[start + r] - 2 * core))
        q_high[span(r), :] = high
        q_low[span(r), :] = low
    parts_ref[:, :PAIR] = own_half[...]
    parts_ref[:, PAIR:] = product((d_high[...], d_low[...]), (q_high[...], q_low[...]))
    coarse_ref[...] = product((rt_high[...], rt_low[...]), halves(parts_ref[...]))


def ghost_step(agg_of, d_high, d_low, own_half, mine, other, rt_high, rt_low):
    return pl.pallas_call(
        ghost_kernel,
        in_specs=[SMEM] + [VMEM] * 7,
        out_specs=[VMEM] * 2,
        out_shape=[shape(WIDE, 2 * PAIR), shape(COARSE, 2 * PAIR)],
        scratch_shapes=[pltpu.VMEM((WIDE, PAIR), BF16)] * 2,
        compiler_params=params(),
        name="ghost_step",
    )(agg_of, d_high, d_low, own_half, mine, other, rt_high, rt_low)


def scaled_by_weight(agg_of, value):
    start = lax.axis_index("slab") * ROWS
    pieces = []
    for a in range(GROUPS):
        members = jnp.zeros((), jnp.int32)
        for e in range(ROWS):
            members += jnp.where(agg_of[start + e] == a, 1, 0)
        piece = value[span(a), :]
        pieces.append(piece * (COARSE_WEIGHT / jnp.full(piece.shape, members.astype(F32))))
    return jnp.concatenate(pieces, axis=0)


def summed_regions(mine, received):
    is_near = ((lax.axis_index("sub") >> 1) & 1) == 0
    own = mine[:, :PAIR] + received[:, :PAIR]
    near = jnp.where(is_near, mine[:, PAIR:], received[:, PAIR:])
    far = jnp.where(is_near, received[:, PAIR:], mine[:, PAIR:])
    return jnp.concatenate([near, own, far], axis=1)


def coarse_kernel(mine, received, coarse_ref, high_ref, low_ref):
    coarse = summed_regions(mine[...], received[...])
    coarse_ref[...] = coarse
    high_ref[...], low_ref[...] = halves(coarse)


def coarse_half(mine, received):
    return pl.pallas_call(
        coarse_kernel,
        in_specs=[VMEM] * 2,
        out_specs=[VMEM] * 3,
        out_shape=[shape(COARSE, 3 * PAIR)] + [shape(COARSE, 3 * PAIR, dtype=BF16)] * 2,
        compiler_params=params(),
        name="coarse_half",
    )(mine, received)


def share_kernel(mine, other, op_ref, high_ref, low_ref, natural):
    high_ref[...], low_ref[...] = halves(other[...])
    sub = lax.axis_index("sub")
    odd = lax.axis_index("slab") & 1
    is_first = (sub & 1) == 0
    first = jnp.where(is_first, mine[...], other[...])
    second = jnp.where(is_first, other[...], mine[...])
    places = (2 * (1 - odd), 1, 2 * odd)
    for region, place in enumerate(places):
        value = jnp.concatenate([first[:, span(region, PAIR)], second[:, span(region, PAIR)]], axis=1)
        natural[:, aligned(place, COARSE)] = value
    share = op_ref.shape[1]
    for k in range(BANDS // share):

        @pl.when(sub == k)
        def _():
            for a in range(GROUPS):
                for q in range(share):
                    op_ref[a, q] = natural[span(a), span(k * share + q)]


def coarse_share(mine, other):
    return pl.pallas_call(
        share_kernel,
        in_specs=[VMEM] * 2,
        out_specs=[VMEM] * 3,
        out_shape=[shape(GROUPS, BANDS // SUBS, DOF, DOF)] + [shape(COARSE, 3 * PAIR, dtype=BF16)] * 2,
        scratch_shapes=[pltpu.VMEM((COARSE, 3 * COARSE), F32)],
        compiler_params=params(),
        name="coarse_share",
    )(mine, other)


def lift_kernel(agg_of, mine, received, smoother, prolong, w_ref):
    start = lax.axis_index("slab") * ROWS
    core = lax.axis_index("sub") & 1
    for e in range(ROWS):
        g_half = summed_regions(mine[span(e), :], received[span(e), :])
        w_ref[span(e), :] = -product(halves(smoother[e]), halves(g_half))
        w_ref[span(e), span(1, PAIR)] += placed(prolong[e], agg_of[start + e] - 2 * core)


def lift_half(agg_of, mine, received, smoother, prolong):
    return pl.pallas_call(
        lift_kernel,
        in_specs=[SMEM] + [VMEM] * 4,
        out_specs=VMEM,
        out_shape=shape(WIDE, 3 * PAIR),
        compiler_params=params(),
        name="lift_half",
    )(agg_of, mine, received, smoother, prolong)


def residual_kernel(agg_of, keep, received, rt_high, rt_low, residual_ref, first_ref):
    residual = -(keep[...] + received[...])
    residual_ref[...] = residual
    first_ref[...] = scaled_by_weight(agg_of, narrow_product((rt_high[...], rt_low[...]), residual))


def residual_step(agg_of, keep, received, rt_high, rt_low):
    return pl.pallas_call(
        residual_kernel,
        in_specs=[SMEM] + [VMEM] * 4,
        out_specs=[VMEM] * 2,
        out_shape=[shape(WIDE, COLS), shape(COARSE, COLS)],
        compiler_params=params(),
        name="residual_step",
    )(agg_of, keep, received, rt_high, rt_low)


def base_kernel(smoother, message, residual, base_ref):
    for e in range(ROWS):
        smoothed = narrow_product(halves(smoother[e]), residual[span(e), :])
        base_ref[span(e), :] = message[span(e), :COLS] + smoothed


def base_step(smoother, message, residual):
    return pl.pallas_call(
        base_kernel,
        in_specs=[VMEM] * 3,
        out_specs=VMEM,
        out_shape=shape(WIDE, COLS),
        compiler_params=params(),
        name="base_step",
    )(smoother, message, residual)


def core_parts(*fields):
    core = lax.axis_index("sub") & 1
    for which in (core, 1 - core):
        yield jnp.concatenate([field[aligned(which, PAIR), :] for field in fields], axis=0)


def sweep_kernel(agg_of, *refs):
    operators, (first, far, near, own, next_ref) = refs[:-5], refs[-5:]
    mine = (operators[0][...], operators[1][...])
    other = halves(operators[2][...]) if len(operators) == 3 else (operators[2][...], operators[3][...])
    total = None
    for operator, field in zip((mine, other), core_parts(near, own, far)):
        part = narrow_product(operator, field)
        total = part if total is None else total + part
    next_ref[...] = own[...] + first[...] - scaled_by_weight(agg_of, total)


def sweep(agg_of, operators, first, near, own, far):
    return pl.pallas_call(
        sweep_kernel,
        in_specs=[SMEM] + [VMEM] * (len(operators) + 4),
        out_specs=VMEM,
        out_shape=shape(COARSE, COLS),
        compiler_params=params(),
        name="sweep",
    )(agg_of, *operators, first, far, near, own)


def lifted_kernel(mine, other, base, own, base_ref, high_ref, low_ref):
    total = base[...]
    for place, (operator, field) in enumerate(zip((mine, other), core_parts(own))):
        total += narrow_product(halves(operator[:, span(1, PAIR)]), field)
        for t, region in enumerate((0, 2)):
            high, low = halves(operator[:, span(region, PAIR)])
            high_ref[:, span(2 * place + t, PAIR)] = high
            low_ref[:, span(2 * place + t, PAIR)] = low
    base_ref[...] = total


def lifted(mine, other, base, own):
    return pl.pallas_call(
        lifted_kernel,
        in_specs=[VMEM] * 4,
        out_specs=[VMEM] * 3,
        out_shape=[shape(WIDE, COLS)] + [shape(WIDE, 2 * COARSE, dtype=BF16)] * 2,
        compiler_params=params(),
        name="lifted",
    )(mine, other, base, own)


def last_kernel(w_high, w_low, base, far, near, out_ref):
    field = jnp.concatenate(list(core_parts(near, far)), axis=0)
    out_ref[...] = base[...] + narrow_product((w_high[...], w_low[...]), field)


def last_step(w_high, w_low, base, near, far):
    return pl.pallas_call(
        last_kernel,
        in_specs=[VMEM] * 5,
        out_specs=VMEM,
        out_shape=shape(WIDE, COLS),
        compiler_params=params(),
        name="last_step",
    )(w_high, w_low, base, far, near)


def swaps(size, start):
    pairs = [(i, i + 1) for i in range(start, size - 1, 2)]
    return pairs + [(j, i) for i, j in pairs]


def from_neighbours(value):
    size = lax.axis_size("slab")
    near = lax.ppermute(value, "slab", swaps(size, 0))
    far = lax.ppermute(value, "slab", swaps(size, 1))
    return far, near


def from_side(value):
    size, subs = lax.axis_size("slab"), lax.axis_size("sub")
    pairs = [
        (i * subs + k, j * subs + k) for k in range(subs) for i, j in swaps(size, (k >> 1) & 1)
    ]
    return lax.ppermute(value, ("slab", "sub"), pairs)


def swapped(value, bit):
    size = lax.axis_size("sub")
    return lax.ppermute(value, "sub", [(i, i ^ bit) for i in range(size)])


def per_device(fine_blocks, prolong, smoother, right_side, agg_of, col_slot, send_rows, send_count):
    pair, mine, theirs, message, right = start_step(
        col_slot, send_rows, send_count, fine_blocks, smoother, right_side, prolong
    )
    side_message = from_side(message)
    theirs = swapped(theirs, 1)
    received = swapped(mine + theirs, 2)
    pair, theirs = lax.optimization_barrier((pair, theirs))
    side, own_half, own_image, rt_high, rt_low = own_step(agg_of, prolong, message, right, pair, swapped(pair, 1))
    received, side = lax.optimization_barrier((received, side))
    keep, send, d_high, d_low = image(own_image, side, received, swapped(received, 1), side_message)
    image_received = swapped(send, 2)
    ghosts = side_message[WIDE:]
    parts, coarse = ghost_step(agg_of, d_high, d_low, own_half, ghosts, swapped(ghosts, 1), rt_high, rt_low)
    coarse_received = swapped(coarse, 2)
    residual, first = residual_step(agg_of, keep, image_received, rt_high, rt_low)
    base = base_step(smoother, message, residual)
    far, near = from_neighbours(first)
    parts, coarse_received = lax.optimization_barrier((parts, coarse_received))
    parts_received = swapped(parts, 2)
    coarse, mine_high, mine_low = coarse_half(coarse, coarse_received)
    far, near, coarse = lax.optimization_barrier((far, near, coarse))
    coarse_other = swapped(coarse, 1)
    correction = sweep(agg_of, (mine_high, mine_low, coarse_other), first, near, first, far)
    coarse_op, other_high, other_low = coarse_share(coarse, coarse_other)
    lift = lift_half(agg_of, parts, parts_received, smoother, prolong)
    for index in range(1, COARSE_SWEEPS - 1):
        far, near = from_neighbours(correction)
        if index == 1:
            shadowed = (far, near, lift, other_high, other_low)
            far, near, lift, other_high, other_low = lax.optimization_barrier(shadowed)
        operators = (mine_high, mine_low, other_high, other_low)
        correction = sweep(agg_of, operators, first, near, correction, far)
    lift_other = swapped(lift, 1)
    far, near = from_neighbours(correction)
    base, w_high, w_low = lifted(lift, lift_other, base, correction)
    solution = last_step(w_high, w_low, base, near, far)
    return coarse_op, solution.reshape(ROWS, DOF, COLS)


def solution(mesh):
    placed_args = (
        P("slab", "sub", None, None),
        P("slab", None, None),
        P("slab", None, None),
        P("slab", None, None),
        P(),
        P("slab", "sub"),
        P(),
        P(),
    )
    return jax.shard_map(
        per_device,
        mesh=mesh,
        in_specs=placed_args,
        out_specs=(P("slab", "sub", None, None), P("slab", None, "sub")),
        check_vma=False,
    )
```

```python
import jax
import jax.numpy as jnp
from jax import lax
from jax.experimental import pallas as pl
from jax.experimental.pallas import tpu as pltpu
from jax.sharding import PartitionSpec as P

COARSE_SWEEPS = 3
COARSE_WEIGHT = 0.25
F32 = jnp.float32
BF16 = jnp.bfloat16
VMEM = pl.BlockSpec(memory_space=pltpu.VMEM)
SMEM = pl.BlockSpec(memory_space=pltpu.SMEM)
HBM = pl.BlockSpec(memory_space=pltpu.HBM)
ROWS = 8
GHOSTS = 8
SLOTS = ROWS + 2 * GHOSTS
GROUPS = 4
BANDS = 3 * GROUPS
DOF = 64
COLS = 128
SUBS = 4
HALF_ROWS = ROWS // 2
WIDE = ROWS * DOF
PAIR = 2 * DOF
COARSE = GROUPS * DOF


def params(limit=24):
    return pltpu.CompilerParams(vmem_limit_bytes=limit << 20)


def shape(*dims, dtype=F32):
    return jax.ShapeDtypeStruct(dims, dtype)


def halves(value):
    high = value.astype(BF16)
    return high, (value - high.astype(F32)).astype(BF16)


def mm(a, b):
    return jnp.dot(a, b, preferred_element_type=F32)


def product(left, right):
    left_high, left_low = left
    right_high, right_low = right
    return mm(left_high, right_high) + (mm(left_high, right_low) + mm(left_low, right_high))


def narrow_product(left, value):
    left_high, left_low = left
    high, low = halves(value)
    width = value.shape[1]
    both = mm(left_high, jnp.concatenate([high, low], axis=1))
    return both[:, :width] + (both[:, width:] + mm(left_low, high))


def span(index, size=DOF):
    return slice(index * size, (index + 1) * size)


def aligned(index, size):
    return pl.ds(pl.multiple_of(index * size, size), size)


def neighbours():
    slab, size = lax.axis_index("slab"), lax.axis_size("slab")
    odd = slab & 1
    near = jnp.minimum(slab ^ 1, size - 1)
    far = jnp.where(odd == 1, jnp.minimum(slab + 1, size - 1), jnp.maximum(slab - 1, 0))
    return slab, near, far


def start_kernel(
    col_hbm, rows_hbm, counts_hbm, blocks_hbm, smoother_hbm, right_hbm, prolong_hbm,
    pair_ref, mine_ref, theirs_ref, message_ref, right_ref,
    col_slot, rows, counts, blocks, smoother, right, prolong, sems, block_sems, *parts
):
    slab, size, sub = lax.axis_index("slab"), lax.axis_size("slab"), lax.axis_index("sub")
    below = jnp.maximum(slab - 1, 0)
    above = jnp.minimum(slab + 1, size - 1)
    core = sub & 1
    chip = (sub >> 1) & 1
    sources = [
        (smoother_hbm, smoother),
        (right_hbm.at[:, :, aligned(sub, COLS)], right.at[0]),
        (right_hbm.at[:, :, aligned(sub ^ 2, COLS)], right.at[1]),
        (prolong_hbm.at[pl.ds(core * HALF_ROWS, HALF_ROWS)], prolong),
        (col_hbm, col_slot),
        (rows_hbm.at[below, sub], rows.at[0]),
        (rows_hbm.at[above, sub], rows.at[1]),
        (counts_hbm.at[sub], counts),
    ]
    copies = [pltpu.make_async_copy(s, d, sems.at[i]) for i, (s, d) in enumerate(sources)]
    block_copies = [
        pltpu.make_async_copy(blocks_hbm.at[e], blocks.at[e], block_sems.at[e]) for e in range(ROWS)
    ]
    for copy in copies + block_copies:
        copy.start()
    for copy in copies:
        copy.wait()

    for e in range(ROWS):
        right_ref[span(e), :] = right[0, e]
        wide = jnp.concatenate([right[0, e], right[1, e]], axis=1)
        message_ref[span(e), :] = product(halves(smoother[e]), halves(wide))
    message_ref[span(ROWS), :] = jnp.concatenate([prolong[i] for i in range(HALF_ROWS)], axis=1)

    lower_count = jnp.where(slab > 0, counts[1, below], 0)
    upper_count = jnp.where(slab < size - 1, counts[0, above], 0)
    lower_region = 1 + (1 - (slab & 1) ^ chip)
    lower_start = lower_region * ROWS
    upper_start = (3 - lower_region) * ROWS
    upper_lanes = lax.broadcasted_iota(jnp.int32, (DOF, PAIR), 1) >= DOF
    for group in range(ROWS // HALF_ROWS):
        for position, part in enumerate(parts):
            part[...] = jnp.zeros_like(part)
            block_copies[group * HALF_ROWS + position].wait()
        for j in range(blocks.shape[1]):
            for position, part in enumerate(parts):
                e = group * HALF_ROWS + position
                slot = col_slot[e, j]
                is_own = slot < ROWS
                is_upper = slot >= ROWS + GHOSTS
                side = jnp.where(is_upper, 1, 0)
                place = jnp.where(is_own, 0, slot - ROWS - side * GHOSTS)
                listed = rows[side, 1 - side, place] + jnp.where(is_upper, upper_start, lower_start)
                column = jnp.where(is_own, slot, listed)
                count = jnp.where(is_upper, upper_count, lower_count)
                live = jnp.where(is_own | (place < count), 1.0, 0.0)
                odd_column = column & 1
                lower_scale = jnp.where(odd_column == 0, live, 0.0)
                upper_scale = jnp.where(odd_column == 1, live, 0.0)
                block = blocks[e, j]
                doubled = jnp.concatenate([block, block], axis=1)
                part[:, aligned(column >> 1, PAIR)] += doubled * jnp.where(upper_lanes, upper_scale, lower_scale)
        for position, part in enumerate(parts):
            pair_ref[span(group * HALF_ROWS + position), :] = part[:, : 2 * WIDE]

        @pl.when(core == group)
        def _():
            for position, part in enumerate(parts):
                mine_ref[span(position), :] = part[:, 2 * WIDE :]

        @pl.when(core != group)
        def _():
            for position, part in enumerate(parts):
                theirs_ref[span(position), :] = part[:, 2 * WIDE :]


def start_step(col_slot, send_rows, send_count, blocks, smoother, right_side, prolong):
    counts = jnp.transpose(send_count, (1, 2, 0))
    arrays = (col_slot, send_rows, counts, blocks, smoother, right_side, prolong)
    return pl.pallas_call(
        start_kernel,
        in_specs=[HBM] * 7,
        out_specs=[VMEM] * 5,
        out_shape=[
            shape(WIDE, 2 * WIDE),
            shape(WIDE // 2, WIDE),
            shape(WIDE // 2, WIDE),
            shape(WIDE + DOF, 2 * COLS),
            shape(WIDE, COLS),
        ],
        scratch_shapes=[
            pltpu.SMEM(col_slot.shape, jnp.int32),
            pltpu.SMEM((2, 2, GHOSTS), jnp.int32),
            pltpu.SMEM((2, send_count.shape[0]), jnp.int32),
            pltpu.VMEM(blocks.shape, F32),
            pltpu.VMEM(smoother.shape, F32),
            pltpu.VMEM((2, ROWS, DOF, COLS), F32),
            pltpu.VMEM((HALF_ROWS, DOF, DOF), F32),
            pltpu.SemaphoreType.DMA((8,)),
            pltpu.SemaphoreType.DMA((ROWS,)),
        ]
        + [pltpu.VMEM((DOF, 3 * WIDE), F32)] * HALF_ROWS,
        compiler_params=params(),
        name="start_step",
    )(*(pltpu.with_memory_space_constraint(a, pltpu.HBM) for a in arrays))


def placed(piece, index):
    upper = lax.broadcasted_iota(jnp.int32, (DOF, PAIR), 1) >= DOF
    doubled = jnp.concatenate([piece, piece], axis=1)
    lower_scale = jnp.where(index == 0, 1.0, 0.0)
    upper_scale = jnp.where(index == 1, 1.0, 0.0)
    return doubled * jnp.where(upper, upper_scale, lower_scale)


def own_kernel(
    agg_of, prolong, field, right, pair, pair_other,
    side_ref, half_ref, coarse_ref, image_ref, weight_ref, rt_high, rt_low, q_high, q_low
):
    start = lax.axis_index("slab") * ROWS
    core = lax.axis_index("sub") & 1

    @pl.when(pl.program_id(0) == 0)
    def _():
        for a in range(GROUPS):
            members = jnp.zeros((), jnp.int32)
            for e in range(ROWS):
                members += jnp.where(agg_of[start + e] == a, 1, 0)
            weight_ref[span(a), :] = COARSE_WEIGHT / jnp.full((DOF, COLS), members.astype(F32))
        restrict_rows = []
        for e in range(ROWS):
            group = agg_of[start + e]
            high, low = halves(placed(prolong[e], group - 2 * core))
            q_high[span(e), :] = high
            q_low[span(e), :] = low
            parts = [placed(prolong[e], group - 2 * t) for t in range(GROUPS // 2)]
            restrict_rows.append(jnp.concatenate(parts, axis=1))
        high, low = halves(jnp.concatenate(restrict_rows, axis=0).T)
        rt_high[...] = high
        rt_low[...] = low
        coarse_ref[...] = jnp.zeros_like(coarse_ref)

    side_ref[...] = pair[:, WIDE:] + pair_other[:, WIDE:]
    own = halves(pair[:, :WIDE] + pair_other[:, :WIDE])
    half = product(own, (q_high[...], q_low[...]))
    half_ref[...] = half
    lanes = aligned(pl.program_id(0), half.shape[0])
    coarse_ref[...] += narrow_product((rt_high[:, lanes], rt_low[:, lanes]), half)
    total = product(own, halves(field[...]))
    image_ref[:, :COLS] = total[:, :COLS] - right[...]
    image_ref[:, COLS:] = total[:, COLS:]


def own_step(agg_of, prolong, message, right, pair, pair_other):
    steps = 2
    whole = lambda *dims: pl.BlockSpec(dims, lambda i: (0,) * len(dims))
    part = lambda width: pl.BlockSpec((WIDE // steps, width), lambda i: (i, 0))
    return pl.pallas_call(
        own_kernel,
        grid=(steps,),
        in_specs=[SMEM, whole(*prolong.shape), whole(WIDE, 2 * COLS), part(COLS)] + [part(2 * WIDE)] * 2,
        out_specs=[part(WIDE), part(PAIR), whole(COARSE, PAIR), part(2 * COLS), whole(COARSE, COLS)] + [whole(COARSE, WIDE)] * 2,
        out_shape=[
            shape(WIDE, WIDE),
            shape(WIDE, PAIR),
            shape(COARSE, PAIR),
            shape(WIDE, 2 * COLS),
            shape(COARSE, COLS),
            shape(COARSE, WIDE, dtype=BF16),
            shape(COARSE, WIDE, dtype=BF16),
        ],
        scratch_shapes=[pltpu.VMEM((WIDE, PAIR), BF16)] * 2,
        compiler_params=params(),
        name="own_step",
    )(agg_of, prolong, message, right, pair, pair_other)


def image_kernel(own_image, side, received, received_other, message, keep_ref, send_ref, high_ref, low_ref):
    core = lax.axis_index("sub") & 1
    field = halves(message[:WIDE, :])
    rows = WIDE // 2
    for group in range(2):
        part = span(group, rows)
        extra = jnp.where(core == group, received[...], received_other[...])
        high, low = halves(side[part, :] + extra)
        high_ref[part, :] = high
        low_ref[part, :] = low
        total = own_image[part, :] + product((high, low), field)
        keep_ref[part, :] = total[:, :COLS]
        send_ref[part, :] = total[:, COLS:]


def image(own_image, side, received, received_other, message):
    return pl.pallas_call(
        image_kernel,
        in_specs=[VMEM] * 5,
        out_specs=[VMEM] * 4,
        out_shape=[shape(WIDE, COLS)] * 2 + [shape(WIDE, WIDE, dtype=BF16)] * 2,
        compiler_params=params(),
        name="image",
    )(own_image, side, received, received_other, message)


def ghost_kernel(agg_of, d_high, d_low, mine, other, half_ref, q_high, q_low):
    _, near, far = neighbours()
    sub = lax.axis_index("sub")
    core = sub & 1
    start = jnp.where(((sub >> 1) & 1) == 0, near, far) * ROWS
    for r in range(ROWS):
        columns = span(r % HALF_ROWS)
        piece = jnp.where(core == r // HALF_ROWS, mine[:, columns], other[:, columns])
        high, low = halves(placed(piece, agg_of[start + r] - 2 * core))
        q_high[span(r), :] = high
        q_low[span(r), :] = low
    half_ref[...] = product((d_high[...], d_low[...]), (q_high[...], q_low[...]))


def ghost_step(agg_of, d_high, d_low, mine, other):
    return pl.pallas_call(
        ghost_kernel,
        in_specs=[SMEM] + [VMEM] * 4,
        out_specs=VMEM,
        out_shape=shape(WIDE, PAIR),
        scratch_shapes=[pltpu.VMEM((WIDE, PAIR), BF16)] * 2,
        compiler_params=params(),
        name="ghost_step",
    )(agg_of, d_high, d_low, mine, other)


def near_and_far(mine, received):
    is_near = ((lax.axis_index("sub") >> 1) & 1) == 0
    return jnp.where(is_near, mine, received), jnp.where(is_near, received, mine)


def coarse_kernel(own, own_received, side, side_received, rt_high, rt_low, *refs):
    regions, (high_ref, low_ref) = refs[:3], refs[3:]
    sides = jnp.concatenate(near_and_far(side[...], side_received[...]), axis=1)
    sides = product((rt_high[...], rt_low[...]), halves(sides))
    values = (sides[:, :PAIR], own[...] + own_received[...], sides[:, PAIR:])
    for region, (ref, value) in enumerate(zip(regions, values)):
        ref[...] = value
        high, low = halves(value)
        high_ref[:, span(region, PAIR)] = high
        low_ref[:, span(region, PAIR)] = low


def coarse_half(own, own_received, side, side_received, rt_high, rt_low):
    return pl.pallas_call(
        coarse_kernel,
        in_specs=[VMEM] * 6,
        out_specs=[VMEM] * 5,
        out_shape=[shape(COARSE, PAIR)] * 3 + [shape(COARSE, 3 * PAIR, dtype=BF16)] * 2,
        compiler_params=params(),
        name="coarse_half",
    )(own, own_received, side, side_received, rt_high, rt_low)


def share_kernel(*refs):
    mine, other, (op_ref, high_ref, low_ref, natural) = refs[:3], refs[3:6], refs[6:]
    sub = lax.axis_index("sub")
    odd = lax.axis_index("slab") & 1
    is_first = (sub & 1) == 0
    places = (2 * (1 - odd), 1, 2 * odd)
    for region, place in enumerate(places):
        own_value, other_value = mine[region][...], other[region][...]
        first = jnp.where(is_first, own_value, other_value)
        second = jnp.where(is_first, other_value, own_value)
        natural[:, aligned(place, COARSE)] = jnp.concatenate([first, second], axis=1)
        high, low = halves(other_value)
        high_ref[:, span(region, PAIR)] = high
        low_ref[:, span(region, PAIR)] = low
    share = op_ref.shape[1]
    for k in range(BANDS // share):

        @pl.when(sub == k)
        def _():
            for a in range(GROUPS):
                for q in range(share):
                    op_ref[a, q] = natural[span(a), span(k * share + q)]


def coarse_share(mine, other):
    return pl.pallas_call(
        share_kernel,
        in_specs=[VMEM] * 6,
        out_specs=[VMEM] * 3,
        out_shape=[shape(GROUPS, BANDS // SUBS, DOF, DOF)] + [shape(COARSE, 3 * PAIR, dtype=BF16)] * 2,
        scratch_shapes=[pltpu.VMEM((COARSE, 3 * COARSE), F32)],
        compiler_params=params(),
        name="coarse_share",
    )(*mine, *other)


def lift_kernel(agg_of, own, own_received, side, side_received, smoother, prolong, w_ref):
    start = lax.axis_index("slab") * ROWS
    core = lax.axis_index("sub") & 1
    for e in range(ROWS):
        rows = span(e)
        near, far = near_and_far(side[rows, :], side_received[rows, :])
        g_half = jnp.concatenate([near, own[rows, :] + own_received[rows, :], far], axis=1)
        w_ref[rows, :] = -product(halves(smoother[e]), halves(g_half))
        w_ref[rows, span(1, PAIR)] += placed(prolong[e], agg_of[start + e] - 2 * core)


def lift_half(agg_of, own, own_received, side, side_received, smoother, prolong):
    return pl.pallas_call(
        lift_kernel,
        in_specs=[SMEM] + [VMEM] * 6,
        out_specs=VMEM,
        out_shape=shape(WIDE, 3 * PAIR),
        compiler_params=params(),
        name="lift_half",
    )(agg_of, own, own_received, side, side_received, smoother, prolong)


def residual_kernel(keep, received, weight, rt_high, rt_low, residual_ref, first_ref):
    residual = -(keep[...] + received[...])
    residual_ref[...] = residual
    first_ref[...] = weight[...] * narrow_product((rt_high[...], rt_low[...]), residual)


def residual_step(keep, received, weight, rt_high, rt_low):
    return pl.pallas_call(
        residual_kernel,
        in_specs=[VMEM] * 5,
        out_specs=[VMEM] * 2,
        out_shape=[shape(WIDE, COLS), shape(COARSE, COLS)],
        compiler_params=params(),
        name="residual_step",
    )(keep, received, weight, rt_high, rt_low)


def base_kernel(smoother, message, residual, base_ref):
    for e in range(ROWS):
        smoothed = narrow_product(halves(smoother[e]), residual[span(e), :])
        base_ref[span(e), :] = message[span(e), :COLS] + smoothed


def base_step(smoother, message, residual):
    return pl.pallas_call(
        base_kernel,
        in_specs=[VMEM] * 3,
        out_specs=VMEM,
        out_shape=shape(WIDE, COLS),
        compiler_params=params(),
        name="base_step",
    )(smoother, message, residual)


def core_parts(*fields):
    core = lax.axis_index("sub") & 1
    for which in (core, 1 - core):
        yield jnp.concatenate([field[aligned(which, PAIR), :] for field in fields], axis=0)


def sweep_kernel(*refs):
    operators, (first, weight, near, own, far, next_ref) = refs[:-6], refs[-6:]
    mine = (operators[0][...], operators[1][...])
    if len(operators) == 5:
        other = halves(jnp.concatenate([region[...] for region in operators[2:]], axis=1))
    else:
        other = (operators[2][...], operators[3][...])
    total = None
    for operator, field in zip((mine, other), core_parts(near, own, far)):
        part = narrow_product(operator, field)
        total = part if total is None else total + part
    next_ref[...] = own[...] + first[...] - weight[...] * total


def sweep(operators, first, weight, near, own, far):
    return pl.pallas_call(
        sweep_kernel,
        in_specs=[VMEM] * (len(operators) + 5),
        out_specs=VMEM,
        out_shape=shape(COARSE, COLS),
        compiler_params=params(),
        name="sweep",
    )(*operators, first, weight, near, own, far)


def lifted_kernel(mine, other, base, own, base_ref, high_ref, low_ref):
    total = base[...]
    for place, (operator, field) in enumerate(zip((mine, other), core_parts(own))):
        total += narrow_product(halves(operator[:, span(1, PAIR)]), field)
        for t, region in enumerate((0, 2)):
            high, low = halves(operator[:, span(region, PAIR)])
            high_ref[:, span(2 * place + t, PAIR)] = high
            low_ref[:, span(2 * place + t, PAIR)] = low
    base_ref[...] = total


def lifted(mine, other, base, own):
    return pl.pallas_call(
        lifted_kernel,
        in_specs=[VMEM] * 4,
        out_specs=[VMEM] * 3,
        out_shape=[shape(WIDE, COLS)] + [shape(WIDE, 2 * COARSE, dtype=BF16)] * 2,
        compiler_params=params(),
        name="lifted",
    )(mine, other, base, own)


def last_kernel(w_high, w_low, base, near, far, out_ref):
    field = jnp.concatenate(list(core_parts(near, far)), axis=0)
    out_ref[...] = base[...] + narrow_product((w_high[...], w_low[...]), field)


def last_step(w_high, w_low, base, near, far):
    return pl.pallas_call(
        last_kernel,
        in_specs=[VMEM] * 5,
        out_specs=VMEM,
        out_shape=shape(WIDE, COLS),
        compiler_params=params(),
        name="last_step",
    )(w_high, w_low, base, near, far)


def swaps(size, start):
    pairs = [(i, i + 1) for i in range(start, size - 1, 2)]
    return pairs + [(j, i) for i, j in pairs]


def from_neighbours(value):
    size = lax.axis_size("slab")
    near = lax.ppermute(value, "slab", swaps(size, 0))
    far = lax.ppermute(value, "slab", swaps(size, 1))
    return near, far


def from_side(value):
    size, subs = lax.axis_size("slab"), lax.axis_size("sub")
    pairs = [
        (i * subs + k, j * subs + k) for k in range(subs) for i, j in swaps(size, (k >> 1) & 1)
    ]
    return lax.ppermute(value, ("slab", "sub"), pairs)


def swapped(value, bit):
    size = lax.axis_size("sub")
    return lax.ppermute(value, "sub", [(i, i ^ bit) for i in range(size)])


def per_device(fine_blocks, prolong, smoother, right_side, agg_of, col_slot, send_rows, send_count):
    pair, mine, theirs, message, right = start_step(
        col_slot, send_rows, send_count, fine_blocks, smoother, right_side, prolong
    )
    side_message = from_side(message)
    theirs = swapped(theirs, 1)
    received = swapped(mine + theirs, 2)
    pair, theirs = lax.optimization_barrier((pair, theirs))
    side, own_half, own_coarse, own_image, weight, rt_high, rt_low = own_step(
        agg_of, prolong, message, right, pair, swapped(pair, 1)
    )
    received, side, own_coarse = lax.optimization_barrier((received, side, own_coarse))
    own_coarse_received = swapped(own_coarse, 2)
    keep, send, d_high, d_low = image(own_image, side, received, swapped(received, 1), side_message)
    image_received = swapped(send, 2)
    ghosts = side_message[WIDE:]
    ghosts, own_coarse_received = lax.optimization_barrier((ghosts, own_coarse_received))
    side_half = ghost_step(agg_of, d_high, d_low, ghosts, swapped(ghosts, 1))
    side_received = swapped(side_half, 2)
    residual, first = residual_step(keep, image_received, weight, rt_high, rt_low)
    base = base_step(smoother, message, residual)
    near, far = from_neighbours(first)
    own_half, side_received = lax.optimization_barrier((own_half, side_received))
    own_received = swapped(own_half, 2)
    *coarse, mine_high, mine_low = coarse_half(
        own_coarse, own_coarse_received, side_half, side_received, rt_high, rt_low
    )
    coarse_other = [swapped(region, 1) for region in coarse]
    near, far, coarse_other = lax.optimization_barrier((near, far, coarse_other))
    correction = sweep((mine_high, mine_low, *coarse_other), first, weight, near, first, far)
    coarse_op, other_high, other_low = coarse_share(coarse, coarse_other)
    lift = lift_half(agg_of, own_half, own_received, side_half, side_received, smoother, prolong)
    for index in range(1, COARSE_SWEEPS - 1):
        near, far = from_neighbours(correction)
        if index == 1:
            shadowed = (near, far, lift, other_high, other_low)
            near, far, lift, other_high, other_low = lax.optimization_barrier(shadowed)
        operators = (mine_high, mine_low, other_high, other_low)
        correction = sweep(operators, first, weight, near, correction, far)
    lift_other = swapped(lift, 1)
    near, far = from_neighbours(correction)
    base, w_high, w_low = lifted(lift, lift_other, base, correction)
    solution = last_step(w_high, w_low, base, near, far)
    return coarse_op, solution.reshape(ROWS, DOF, COLS)


def solution(mesh):
    placed_args = (
        P("slab", "sub", None, None),
        P("slab", None, None),
        P("slab", None, None),
        P("slab", None, None),
        P(),
        P("slab", "sub"),
        P(),
        P(),
    )
    return jax.shard_map(
        per_device,
        mesh=mesh,
        in_specs=placed_args,
        out_specs=(P("slab", "sub", None, None), P("slab", None, "sub")),
        check_vma=False,
    )
```

```python
import jax
import jax.numpy as jnp
from jax import lax
from jax.experimental import pallas as pl
from jax.experimental.pallas import tpu as pltpu
from jax.sharding import PartitionSpec as P

COARSE_SWEEPS = 3
COARSE_WEIGHT = 0.25
F32 = jnp.float32
BF16 = jnp.bfloat16
VMEM = pl.BlockSpec(memory_space=pltpu.VMEM)
SMEM = pl.BlockSpec(memory_space=pltpu.SMEM)
HBM = pl.BlockSpec(memory_space=pltpu.HBM)
ROWS = 8
GHOSTS = 8
SLOTS = ROWS + 2 * GHOSTS
GROUPS = 4
BANDS = 3 * GROUPS
DOF = 64
COLS = 128
SUBS = 4
HALF_ROWS = ROWS // 2
WIDE = ROWS * DOF
PAIR = 2 * DOF
COARSE = GROUPS * DOF


def params(limit=24):
    return pltpu.CompilerParams(vmem_limit_bytes=limit << 20)


def shape(*dims, dtype=F32):
    return jax.ShapeDtypeStruct(dims, dtype)


def halves(value):
    high = value.astype(BF16)
    return high, (value - high.astype(F32)).astype(BF16)


def mm(a, b):
    return jnp.dot(a, b, preferred_element_type=F32)


def product(left, right):
    left_high, left_low = left
    right_high, right_low = right
    return mm(left_high, right_high) + (mm(left_high, right_low) + mm(left_low, right_high))


def narrow_product(left, value):
    left_high, left_low = left
    high, low = halves(value)
    width = value.shape[1]
    both = mm(left_high, jnp.concatenate([high, low], axis=1))
    return both[:, :width] + (both[:, width:] + mm(left_low, high))


def span(index, size=DOF):
    return slice(index * size, (index + 1) * size)


def aligned(index, size):
    return pl.ds(pl.multiple_of(index * size, size), size)


def neighbours():
    slab, size = lax.axis_index("slab"), lax.axis_size("slab")
    odd = slab & 1
    near = jnp.minimum(slab ^ 1, size - 1)
    far = jnp.where(odd == 1, jnp.minimum(slab + 1, size - 1), jnp.maximum(slab - 1, 0))
    return slab, near, far


def start_kernel(
    col_hbm, rows_hbm, counts_hbm, blocks_hbm, smoother_hbm, right_hbm, prolong_hbm,
    pair_ref, mine_ref, theirs_ref, message_ref, right_ref,
    col_slot, rows, counts, blocks, smoother, right, prolong, sems, block_sems, *parts
):
    slab, size, sub = lax.axis_index("slab"), lax.axis_size("slab"), lax.axis_index("sub")
    below = jnp.maximum(slab - 1, 0)
    above = jnp.minimum(slab + 1, size - 1)
    core = sub & 1
    chip = (sub >> 1) & 1
    sources = [
        (smoother_hbm, smoother),
        (right_hbm.at[:, :, aligned(sub, COLS)], right.at[0]),
        (right_hbm.at[:, :, aligned(sub ^ 2, COLS)], right.at[1]),
        (prolong_hbm.at[pl.ds(core * HALF_ROWS, HALF_ROWS)], prolong),
        (col_hbm, col_slot),
        (rows_hbm.at[below, sub], rows.at[0]),
        (rows_hbm.at[above, sub], rows.at[1]),
        (counts_hbm.at[sub], counts),
    ]
    copies = [pltpu.make_async_copy(s, d, sems.at[i]) for i, (s, d) in enumerate(sources)]
    block_copies = [
        pltpu.make_async_copy(blocks_hbm.at[e], blocks.at[e], block_sems.at[e]) for e in range(ROWS)
    ]
    for copy in copies + block_copies:
        copy.start()
    for copy in copies:
        copy.wait()

    for e in range(ROWS):
        right_ref[span(e), :] = right[0, e]
        wide = jnp.concatenate([right[0, e], right[1, e]], axis=1)
        message_ref[span(e), :] = product(halves(smoother[e]), halves(wide))
    message_ref[span(ROWS), :] = jnp.concatenate([prolong[i] for i in range(HALF_ROWS)], axis=1)

    lower_count = jnp.where(slab > 0, counts[1, below], 0)
    upper_count = jnp.where(slab < size - 1, counts[0, above], 0)
    lower_region = 1 + (1 - (slab & 1) ^ chip)
    lower_start = lower_region * ROWS
    upper_start = (3 - lower_region) * ROWS
    upper_lanes = lax.broadcasted_iota(jnp.int32, (DOF, PAIR), 1) >= DOF
    for group in range(ROWS // HALF_ROWS):
        for position, part in enumerate(parts):
            part[...] = jnp.zeros_like(part)
            block_copies[group * HALF_ROWS + position].wait()
        for j in range(blocks.shape[1]):
            for position, part in enumerate(parts):
                e = group * HALF_ROWS + position
                slot = col_slot[e, j]
                is_own = slot < ROWS
                is_upper = slot >= ROWS + GHOSTS
                side = jnp.where(is_upper, 1, 0)
                place = jnp.where(is_own, 0, slot - ROWS - side * GHOSTS)
                listed = rows[side, 1 - side, place] + jnp.where(is_upper, upper_start, lower_start)
                column = jnp.where(is_own, slot, listed)
                count = jnp.where(is_upper, upper_count, lower_count)
                live = jnp.where(is_own | (place < count), 1.0, 0.0)
                odd_column = column & 1
                lower_scale = jnp.where(odd_column == 0, live, 0.0)
                upper_scale = jnp.where(odd_column == 1, live, 0.0)
                block = blocks[e, j]
                doubled = jnp.concatenate([block, block], axis=1)
                part[:, aligned(column >> 1, PAIR)] += doubled * jnp.where(upper_lanes, upper_scale, lower_scale)
        for position, part in enumerate(parts):
            pair_ref[span(group * HALF_ROWS + position), :] = part[:, : 2 * WIDE]

        @pl.when(core == group)
        def _():
            for position, part in enumerate(parts):
                mine_ref[span(position), :] = part[:, 2 * WIDE :]

        @pl.when(core != group)
        def _():
            for position, part in enumerate(parts):
                theirs_ref[span(position), :] = part[:, 2 * WIDE :]


def start_step(col_slot, send_rows, send_count, blocks, smoother, right_side, prolong):
    counts = jnp.transpose(send_count, (1, 2, 0))
    arrays = (col_slot, send_rows, counts, blocks, smoother, right_side, prolong)
    return pl.pallas_call(
        start_kernel,
        in_specs=[HBM] * 7,
        out_specs=[VMEM] * 5,
        out_shape=[
            shape(WIDE, 2 * WIDE),
            shape(WIDE // 2, WIDE),
            shape(WIDE // 2, WIDE),
            shape(WIDE + DOF, 2 * COLS),
            shape(WIDE, COLS),
        ],
        scratch_shapes=[
            pltpu.SMEM(col_slot.shape, jnp.int32),
            pltpu.SMEM((2, 2, GHOSTS), jnp.int32),
            pltpu.SMEM((2, send_count.shape[0]), jnp.int32),
            pltpu.VMEM(blocks.shape, F32),
            pltpu.VMEM(smoother.shape, F32),
            pltpu.VMEM((2, ROWS, DOF, COLS), F32),
            pltpu.VMEM((HALF_ROWS, DOF, DOF), F32),
            pltpu.SemaphoreType.DMA((8,)),
            pltpu.SemaphoreType.DMA((ROWS,)),
        ]
        + [pltpu.VMEM((DOF, 3 * WIDE), F32)] * HALF_ROWS,
        compiler_params=params(),
        name="start_step",
    )(*(pltpu.with_memory_space_constraint(a, pltpu.HBM) for a in arrays))


def placed(piece, index):
    upper = lax.broadcasted_iota(jnp.int32, (DOF, PAIR), 1) >= DOF
    doubled = jnp.concatenate([piece, piece], axis=1)
    lower_scale = jnp.where(index == 0, 1.0, 0.0)
    upper_scale = jnp.where(index == 1, 1.0, 0.0)
    return doubled * jnp.where(upper, upper_scale, lower_scale)


def own_kernel(
    agg_of, prolong, field, right, pair, pair_other,
    side_ref, half_ref, coarse_ref, image_ref, weight_ref, rt_high, rt_low, q_high, q_low
):
    start = lax.axis_index("slab") * ROWS
    core = lax.axis_index("sub") & 1

    @pl.when(pl.program_id(0) == 0)
    def _():
        for a in range(GROUPS):
            members = jnp.zeros((), jnp.int32)
            for e in range(ROWS):
                members += jnp.where(agg_of[start + e] == a, 1, 0)
            weight_ref[span(a), :] = COARSE_WEIGHT / jnp.full((DOF, COLS), members.astype(F32))
        restrict_rows = []
        for e in range(ROWS):
            group = agg_of[start + e]
            high, low = halves(placed(prolong[e], group - 2 * core))
            q_high[span(e), :] = high
            q_low[span(e), :] = low
            parts = [placed(prolong[e], group - 2 * t) for t in range(GROUPS // 2)]
            restrict_rows.append(jnp.concatenate(parts, axis=1))
        high, low = halves(jnp.concatenate(restrict_rows, axis=0).T)
        rt_high[...] = high
        rt_low[...] = low
        coarse_ref[...] = jnp.zeros_like(coarse_ref)

    side_ref[...] = pair[:, WIDE:] + pair_other[:, WIDE:]
    own = halves(pair[:, :WIDE] + pair_other[:, :WIDE])
    half = product(own, (q_high[...], q_low[...]))
    half_ref[...] = half
    lanes = aligned(pl.program_id(0), half.shape[0])
    coarse_ref[...] += narrow_product((rt_high[:, lanes], rt_low[:, lanes]), half)
    total = product(own, halves(field[...]))
    image_ref[:, :COLS] = total[:, :COLS] - right[...]
    image_ref[:, COLS:] = total[:, COLS:]


def own_step(agg_of, prolong, message, right, pair, pair_other):
    steps = 2
    whole = lambda *dims: pl.BlockSpec(dims, lambda i: (0,) * len(dims))
    part = lambda width: pl.BlockSpec((WIDE // steps, width), lambda i: (i, 0))
    return pl.pallas_call(
        own_kernel,
        grid=(steps,),
        in_specs=[SMEM, whole(*prolong.shape), whole(WIDE, 2 * COLS), part(COLS)] + [part(2 * WIDE)] * 2,
        out_specs=[part(WIDE), part(PAIR), whole(COARSE, PAIR), part(2 * COLS), whole(COARSE, COLS)] + [whole(COARSE, WIDE)] * 2,
        out_shape=[
            shape(WIDE, WIDE),
            shape(WIDE, PAIR),
            shape(COARSE, PAIR),
            shape(WIDE, 2 * COLS),
            shape(COARSE, COLS),
            shape(COARSE, WIDE, dtype=BF16),
            shape(COARSE, WIDE, dtype=BF16),
        ],
        scratch_shapes=[pltpu.VMEM((WIDE, PAIR), BF16)] * 2,
        compiler_params=params(),
        name="own_step",
    )(agg_of, prolong, message, right, pair, pair_other)


def image_kernel(
    own_image, side, received, received_other, message, rt_high, rt_low,
    keep_ref, send_ref, rhs_keep_ref, rhs_send_ref, high_ref, low_ref
):
    core = lax.axis_index("sub") & 1
    field = halves(message[:WIDE, :])
    rows = WIDE // 2
    rhs = None
    for group in range(2):
        part = span(group, rows)
        extra = jnp.where(core == group, received[...], received_other[...])
        high, low = halves(side[part, :] + extra)
        high_ref[part, :] = high
        low_ref[part, :] = low
        total = own_image[part, :] + product((high, low), field)
        keep_ref[part, :] = total[:, :COLS]
        send_ref[part, :] = total[:, COLS:]
        term = product((rt_high[:, part], rt_low[:, part]), halves(total))
        rhs = term if rhs is None else rhs + term
    rhs_keep_ref[...] = rhs[:, :COLS]
    rhs_send_ref[...] = rhs[:, COLS:]


def image(own_image, side, received, received_other, message, rt_high, rt_low):
    return pl.pallas_call(
        image_kernel,
        in_specs=[VMEM] * 7,
        out_specs=[VMEM] * 6,
        out_shape=[shape(WIDE, COLS)] * 2 + [shape(COARSE, COLS)] * 2 + [shape(WIDE, WIDE, dtype=BF16)] * 2,
        compiler_params=params(),
        name="image",
    )(own_image, side, received, received_other, message, rt_high, rt_low)


def ghost_kernel(agg_of, d_high, d_low, mine, other, upper_ref, lower_ref, q_high, q_low):
    _, near, far = neighbours()
    sub = lax.axis_index("sub")
    core = sub & 1
    start = jnp.where(((sub >> 1) & 1) == 0, near, far) * ROWS
    for r in range(ROWS):
        columns = span(r % HALF_ROWS)
        piece = jnp.where(core == r // HALF_ROWS, mine[:, columns], other[:, columns])
        high, low = halves(placed(piece, agg_of[start + r] - 2 * core))
        q_high[span(r), :] = high
        q_low[span(r), :] = low
    for group, ref in enumerate((upper_ref, lower_ref)):
        part = span(group, WIDE // 2)
        ref[...] = product((d_high[part, :], d_low[part, :]), (q_high[...], q_low[...]))


def ghost_step(agg_of, d_high, d_low, mine, other):
    return pl.pallas_call(
        ghost_kernel,
        in_specs=[SMEM] + [VMEM] * 4,
        out_specs=[VMEM] * 2,
        out_shape=[shape(WIDE // 2, PAIR)] * 2,
        scratch_shapes=[pltpu.VMEM((WIDE, PAIR), BF16)] * 2,
        compiler_params=params(),
        name="ghost_step",
    )(agg_of, d_high, d_low, mine, other)


def near_and_far(mine, received):
    is_near = ((lax.axis_index("sub") >> 1) & 1) == 0
    return jnp.where(is_near, mine, received), jnp.where(is_near, received, mine)


def coarse_kernel(own, own_received, upper, lower, upper_received, lower_received, rt_high, rt_low, *refs):
    regions, (high_ref, low_ref) = refs[:3], refs[3:]
    side = jnp.concatenate([upper[...], lower[...]], axis=0)
    side_received = jnp.concatenate([upper_received[...], lower_received[...]], axis=0)
    sides = jnp.concatenate(near_and_far(side, side_received), axis=1)
    sides = product((rt_high[...], rt_low[...]), halves(sides))
    values = (sides[:, :PAIR], own[...] + own_received[...], sides[:, PAIR:])
    for region, (ref, value) in enumerate(zip(regions, values)):
        ref[...] = value
        high, low = halves(value)
        high_ref[:, span(region, PAIR)] = high
        low_ref[:, span(region, PAIR)] = low


def coarse_half(own, own_received, side, side_received, rt_high, rt_low):
    return pl.pallas_call(
        coarse_kernel,
        in_specs=[VMEM] * 8,
        out_specs=[VMEM] * 5,
        out_shape=[shape(COARSE, PAIR)] * 3 + [shape(COARSE, 3 * PAIR, dtype=BF16)] * 2,
        compiler_params=params(),
        name="coarse_half",
    )(own, own_received, *side, *side_received, rt_high, rt_low)


def share_kernel(*refs):
    mine, other, (op_ref, high_ref, low_ref, natural) = refs[:3], refs[3:6], refs[6:]
    sub = lax.axis_index("sub")
    odd = lax.axis_index("slab") & 1
    is_first = (sub & 1) == 0
    places = (2 * (1 - odd), 1, 2 * odd)
    for region, place in enumerate(places):
        own_value, other_value = mine[region][...], other[region][...]
        first = jnp.where(is_first, own_value, other_value)
        second = jnp.where(is_first, other_value, own_value)
        natural[:, aligned(place, COARSE)] = jnp.concatenate([first, second], axis=1)
        high, low = halves(other_value)
        high_ref[:, span(region, PAIR)] = high
        low_ref[:, span(region, PAIR)] = low
    share = op_ref.shape[1]
    for k in range(BANDS // share):

        @pl.when(sub == k)
        def _():
            for a in range(GROUPS):
                for q in range(share):
                    op_ref[a, q] = natural[span(a), span(k * share + q)]


def coarse_share(mine, other):
    return pl.pallas_call(
        share_kernel,
        in_specs=[VMEM] * 6,
        out_specs=[VMEM] * 3,
        out_shape=[shape(GROUPS, BANDS // SUBS, DOF, DOF)] + [shape(COARSE, 3 * PAIR, dtype=BF16)] * 2,
        scratch_shapes=[pltpu.VMEM((COARSE, 3 * COARSE), F32)],
        compiler_params=params(),
        name="coarse_share",
    )(*mine, *other)


def lift_kernel(agg_of, own, own_received, upper, lower, upper_received, lower_received, smoother, prolong, w_ref):
    start = lax.axis_index("slab") * ROWS
    core = lax.axis_index("sub") & 1
    for e in range(ROWS):
        rows = span(e)
        side, side_received = ((upper, upper_received), (lower, lower_received))[e // HALF_ROWS]
        near, far = near_and_far(side[span(e % HALF_ROWS), :], side_received[span(e % HALF_ROWS), :])
        g_half = jnp.concatenate([near, own[rows, :] + own_received[rows, :], far], axis=1)
        w_ref[rows, :] = -product(halves(smoother[e]), halves(g_half))
        w_ref[rows, span(1, PAIR)] += placed(prolong[e], agg_of[start + e] - 2 * core)


def lift_half(agg_of, own, own_received, side, side_received, smoother, prolong):
    return pl.pallas_call(
        lift_kernel,
        in_specs=[SMEM] + [VMEM] * 8,
        out_specs=VMEM,
        out_shape=shape(WIDE, 3 * PAIR),
        compiler_params=params(),
        name="lift_half",
    )(agg_of, own, own_received, *side, *side_received, smoother, prolong)


def first_kernel(keep, received, weight, first_ref):
    first_ref[...] = -weight[...] * (keep[...] + received[...])


def first_correction(keep, received, weight):
    return pl.pallas_call(
        first_kernel,
        in_specs=[VMEM] * 3,
        out_specs=VMEM,
        out_shape=shape(COARSE, COLS),
        compiler_params=params(),
        name="first_correction",
    )(keep, received, weight)


def base_kernel(smoother, message, keep, received, base_ref):
    for e in range(ROWS):
        residual = -(keep[span(e), :] + received[span(e), :])
        base_ref[span(e), :] = message[span(e), :COLS] + narrow_product(halves(smoother[e]), residual)


def base_step(smoother, message, keep, received):
    return pl.pallas_call(
        base_kernel,
        in_specs=[VMEM] * 4,
        out_specs=VMEM,
        out_shape=shape(WIDE, COLS),
        compiler_params=params(),
        name="base_step",
    )(smoother, message, keep, received)


def core_parts(*fields):
    core = lax.axis_index("sub") & 1
    for which in (core, 1 - core):
        yield jnp.concatenate([field[aligned(which, PAIR), :] for field in fields], axis=0)


def sweep_kernel(*refs):
    operators, (first, weight, near, own, far, next_ref) = refs[:-6], refs[-6:]
    mine = (operators[0][...], operators[1][...])
    if len(operators) == 5:
        other = halves(jnp.concatenate([region[...] for region in operators[2:]], axis=1))
    else:
        other = (operators[2][...], operators[3][...])
    total = None
    for operator, field in zip((mine, other), core_parts(near, own, far)):
        part = narrow_product(operator, field)
        total = part if total is None else total + part
    next_ref[...] = own[...] + first[...] - weight[...] * total


def sweep(operators, first, weight, near, own, far):
    return pl.pallas_call(
        sweep_kernel,
        in_specs=[VMEM] * (len(operators) + 5),
        out_specs=VMEM,
        out_shape=shape(COARSE, COLS),
        compiler_params=params(),
        name="sweep",
    )(*operators, first, weight, near, own, far)


def lifted_kernel(mine, other, base, own, base_ref, high_ref, low_ref):
    total = base[...]
    for place, (operator, field) in enumerate(zip((mine, other), core_parts(own))):
        total += narrow_product(halves(operator[:, span(1, PAIR)]), field)
        for t, region in enumerate((0, 2)):
            high, low = halves(operator[:, span(region, PAIR)])
            high_ref[:, span(2 * place + t, PAIR)] = high
            low_ref[:, span(2 * place + t, PAIR)] = low
    base_ref[...] = total


def lifted(mine, other, base, own):
    return pl.pallas_call(
        lifted_kernel,
        in_specs=[VMEM] * 4,
        out_specs=[VMEM] * 3,
        out_shape=[shape(WIDE, COLS)] + [shape(WIDE, 2 * COARSE, dtype=BF16)] * 2,
        compiler_params=params(),
        name="lifted",
    )(mine, other, base, own)


def last_kernel(w_high, w_low, base, near, far, out_ref):
    field = jnp.concatenate(list(core_parts(near, far)), axis=0)
    out_ref[...] = base[...] + narrow_product((w_high[...], w_low[...]), field)


def last_step(w_high, w_low, base, near, far):
    return pl.pallas_call(
        last_kernel,
        in_specs=[VMEM] * 5,
        out_specs=VMEM,
        out_shape=shape(WIDE, COLS),
        compiler_params=params(),
        name="last_step",
    )(w_high, w_low, base, near, far)


def swaps(size, start):
    pairs = [(i, i + 1) for i in range(start, size - 1, 2)]
    return pairs + [(j, i) for i, j in pairs]


def from_neighbours(value):
    size = lax.axis_size("slab")
    near = lax.ppermute(value, "slab", swaps(size, 0))
    far = lax.ppermute(value, "slab", swaps(size, 1))
    return near, far


def from_side(value):
    size, subs = lax.axis_size("slab"), lax.axis_size("sub")
    pairs = [
        (i * subs + k, j * subs + k) for k in range(subs) for i, j in swaps(size, (k >> 1) & 1)
    ]
    return lax.ppermute(value, ("slab", "sub"), pairs)


def swapped(value, bit):
    size = lax.axis_size("sub")
    return lax.ppermute(value, "sub", [(i, i ^ bit) for i in range(size)])


def per_device(fine_blocks, prolong, smoother, right_side, agg_of, col_slot, send_rows, send_count):
    pair, mine, theirs, message, right = start_step(
        col_slot, send_rows, send_count, fine_blocks, smoother, right_side, prolong
    )
    side_message = from_side(message)
    theirs = swapped(theirs, 1)
    received = swapped(mine + theirs, 2)
    pair, theirs = lax.optimization_barrier((pair, theirs))
    side, own_half, own_coarse, own_image, weight, rt_high, rt_low = own_step(
        agg_of, prolong, message, right, pair, swapped(pair, 1)
    )
    received, side, own_coarse = lax.optimization_barrier((received, side, own_coarse))
    own_coarse_received = swapped(own_coarse, 2)
    keep, send, rhs_keep, rhs_send, d_high, d_low = image(
        own_image, side, received, swapped(received, 1), side_message, rt_high, rt_low
    )
    rhs_received = swapped(rhs_send, 2)
    ghosts = side_message[WIDE:]
    ghosts, own_coarse_received = lax.optimization_barrier((ghosts, own_coarse_received))
    side_half = ghost_step(agg_of, d_high, d_low, ghosts, swapped(ghosts, 1))
    side_received = [swapped(part, 2) for part in side_half]
    first = first_correction(rhs_keep, rhs_received, weight)
    near, far = from_neighbours(first)
    own_half, side_received = lax.optimization_barrier((own_half, side_received))
    own_received = swapped(own_half, 2)
    send, side_received = lax.optimization_barrier((send, side_received))
    base = base_step(smoother, message, keep, swapped(send, 2))
    *coarse, mine_high, mine_low = coarse_half(
        own_coarse, own_coarse_received, side_half, side_received, rt_high, rt_low
    )
    coarse_other = [swapped(region, 1) for region in coarse]
    near, far, coarse_other = lax.optimization_barrier((near, far, coarse_other))
    correction = sweep((mine_high, mine_low, *coarse_other), first, weight, near, first, far)
    coarse_op, other_high, other_low = coarse_share(coarse, coarse_other)
    lift = lift_half(agg_of, own_half, own_received, side_half, side_received, smoother, prolong)
    for index in range(1, COARSE_SWEEPS - 1):
        near, far = from_neighbours(correction)
        if index == 1:
            shadowed = (near, far, lift, other_high, other_low)
            near, far, lift, other_high, other_low = lax.optimization_barrier(shadowed)
        operators = (mine_high, mine_low, other_high, other_low)
        correction = sweep(operators, first, weight, near, correction, far)
    lift_other = swapped(lift, 1)
    near, far = from_neighbours(correction)
    base, w_high, w_low = lifted(lift, lift_other, base, correction)
    solution = last_step(w_high, w_low, base, near, far)
    return coarse_op, solution.reshape(ROWS, DOF, COLS)


def solution(mesh):
    placed_args = (
        P("slab", "sub", None, None),
        P("slab", None, None),
        P("slab", None, None),
        P("slab", None, None),
        P(),
        P("slab", "sub"),
        P(),
        P(),
    )
    return jax.shard_map(
        per_device,
        mesh=mesh,
        in_specs=placed_args,
        out_specs=(P("slab", "sub", None, None), P("slab", None, "sub")),
        check_vma=False,
    )
```

```python
import jax
import jax.numpy as jnp
from jax import lax
from jax.experimental import pallas as pl
from jax.experimental.pallas import tpu as pltpu
from jax.sharding import PartitionSpec as P

COARSE_SWEEPS = 3
COARSE_WEIGHT = 0.25
F32 = jnp.float32
BF16 = jnp.bfloat16
VMEM = pl.BlockSpec(memory_space=pltpu.VMEM)
SMEM = pl.BlockSpec(memory_space=pltpu.SMEM)
HBM = pl.BlockSpec(memory_space=pltpu.HBM)
ROWS = 8
GHOSTS = 8
SLOTS = ROWS + 2 * GHOSTS
GROUPS = 4
BANDS = 3 * GROUPS
DOF = 64
COLS = 128
SUBS = 4
HALF_ROWS = ROWS // 2
WIDE = ROWS * DOF
PAIR = 2 * DOF
COARSE = GROUPS * DOF


def params(limit=24):
    return pltpu.CompilerParams(vmem_limit_bytes=limit << 20)


def shape(*dims, dtype=F32):
    return jax.ShapeDtypeStruct(dims, dtype)


def halves(value):
    high = value.astype(BF16)
    return high, (value - high.astype(F32)).astype(BF16)


def mm(a, b):
    return jnp.dot(a, b, preferred_element_type=F32)


def product(left, right):
    left_high, left_low = left
    right_high, right_low = right
    return mm(left_high, right_high) + (mm(left_high, right_low) + mm(left_low, right_high))


def narrow_product(left, value):
    left_high, left_low = left
    high, low = halves(value)
    width = value.shape[1]
    both = mm(left_high, jnp.concatenate([high, low], axis=1))
    return both[:, :width] + (both[:, width:] + mm(left_low, high))


def span(index, size=DOF):
    return slice(index * size, (index + 1) * size)


def aligned(index, size):
    return pl.ds(pl.multiple_of(index * size, size), size)


def neighbours():
    slab, size = lax.axis_index("slab"), lax.axis_size("slab")
    odd = slab & 1
    near = jnp.minimum(slab ^ 1, size - 1)
    far = jnp.where(odd == 1, jnp.minimum(slab + 1, size - 1), jnp.maximum(slab - 1, 0))
    return slab, near, far


def start_kernel(
    col_hbm, rows_hbm, counts_hbm, blocks_hbm, smoother_hbm, right_hbm, prolong_hbm,
    pair_ref, mine_ref, theirs_ref, message_ref, right_ref,
    col_slot, rows, counts, blocks, smoother, right, prolong, sems, block_sems, *parts
):
    slab, size, sub = lax.axis_index("slab"), lax.axis_size("slab"), lax.axis_index("sub")
    below = jnp.maximum(slab - 1, 0)
    above = jnp.minimum(slab + 1, size - 1)
    core = sub & 1
    chip = (sub >> 1) & 1
    sources = [
        (smoother_hbm, smoother),
        (right_hbm.at[:, :, aligned(sub, COLS)], right.at[0]),
        (right_hbm.at[:, :, aligned(sub ^ 2, COLS)], right.at[1]),
        (prolong_hbm.at[pl.ds(core * HALF_ROWS, HALF_ROWS)], prolong),
        (col_hbm, col_slot),
        (rows_hbm.at[below, sub], rows.at[0]),
        (rows_hbm.at[above, sub], rows.at[1]),
        (counts_hbm.at[sub], counts),
    ]
    copies = [pltpu.make_async_copy(s, d, sems.at[i]) for i, (s, d) in enumerate(sources)]
    block_copies = [
        pltpu.make_async_copy(blocks_hbm.at[e], blocks.at[e], block_sems.at[e]) for e in range(ROWS)
    ]
    for copy in copies + block_copies:
        copy.start()
    for copy in copies:
        copy.wait()

    for e in range(ROWS):
        right_ref[span(e), :] = right[0, e]
        wide = jnp.concatenate([right[0, e], right[1, e]], axis=1)
        message_ref[span(e), :] = product(halves(smoother[e]), halves(wide))
    message_ref[span(ROWS), :] = jnp.concatenate([prolong[i] for i in range(HALF_ROWS)], axis=1)

    lower_count = jnp.where(slab > 0, counts[1, below], 0)
    upper_count = jnp.where(slab < size - 1, counts[0, above], 0)
    lower_region = 1 + (1 - (slab & 1) ^ chip)
    lower_start = lower_region * ROWS
    upper_start = (3 - lower_region) * ROWS
    upper_lanes = lax.broadcasted_iota(jnp.int32, (DOF, PAIR), 1) >= DOF
    for group in range(ROWS // HALF_ROWS):
        for position, part in enumerate(parts):
            part[...] = jnp.zeros_like(part)
            block_copies[group * HALF_ROWS + position].wait()
        for j in range(blocks.shape[1]):
            for position, part in enumerate(parts):
                e = group * HALF_ROWS + position
                slot = col_slot[e, j]
                is_own = slot < ROWS
                is_upper = slot >= ROWS + GHOSTS
                side = jnp.where(is_upper, 1, 0)
                place = jnp.where(is_own, 0, slot - ROWS - side * GHOSTS)
                listed = rows[side, 1 - side, place] + jnp.where(is_upper, upper_start, lower_start)
                column = jnp.where(is_own, slot, listed)
                count = jnp.where(is_upper, upper_count, lower_count)
                live = jnp.where(is_own | (place < count), 1.0, 0.0)
                odd_column = column & 1
                lower_scale = jnp.where(odd_column == 0, live, 0.0)
                upper_scale = jnp.where(odd_column == 1, live, 0.0)
                block = blocks[e, j]
                doubled = jnp.concatenate([block, block], axis=1)
                part[:, aligned(column >> 1, PAIR)] += doubled * jnp.where(upper_lanes, upper_scale, lower_scale)
        for position, part in enumerate(parts):
            pair_ref[span(group * HALF_ROWS + position), :] = part[:, : 2 * WIDE]

        @pl.when(core == group)
        def _():
            for position, part in enumerate(parts):
                mine_ref[span(position), :] = part[:, 2 * WIDE :]

        @pl.when(core != group)
        def _():
            for position, part in enumerate(parts):
                theirs_ref[span(position), :] = part[:, 2 * WIDE :]


def start_step(col_slot, send_rows, send_count, blocks, smoother, right_side, prolong):
    counts = jnp.transpose(send_count, (1, 2, 0))
    arrays = (col_slot, send_rows, counts, blocks, smoother, right_side, prolong)
    return pl.pallas_call(
        start_kernel,
        in_specs=[HBM] * 7,
        out_specs=[VMEM] * 5,
        out_shape=[
            shape(WIDE, 2 * WIDE),
            shape(WIDE // 2, WIDE),
            shape(WIDE // 2, WIDE),
            shape(WIDE + DOF, 2 * COLS),
            shape(WIDE, COLS),
        ],
        scratch_shapes=[
            pltpu.SMEM(col_slot.shape, jnp.int32),
            pltpu.SMEM((2, 2, GHOSTS), jnp.int32),
            pltpu.SMEM((2, send_count.shape[0]), jnp.int32),
            pltpu.VMEM(blocks.shape, F32),
            pltpu.VMEM(smoother.shape, F32),
            pltpu.VMEM((2, ROWS, DOF, COLS), F32),
            pltpu.VMEM((HALF_ROWS, DOF, DOF), F32),
            pltpu.SemaphoreType.DMA((8,)),
            pltpu.SemaphoreType.DMA((ROWS,)),
        ]
        + [pltpu.VMEM((DOF, 3 * WIDE), F32)] * HALF_ROWS,
        compiler_params=params(),
        name="start_step",
    )(*(pltpu.with_memory_space_constraint(a, pltpu.HBM) for a in arrays))


def placed(piece, index):
    upper = lax.broadcasted_iota(jnp.int32, (DOF, PAIR), 1) >= DOF
    doubled = jnp.concatenate([piece, piece], axis=1)
    lower_scale = jnp.where(index == 0, 1.0, 0.0)
    upper_scale = jnp.where(index == 1, 1.0, 0.0)
    return doubled * jnp.where(upper, upper_scale, lower_scale)


def own_kernel(
    agg_of, prolong, field, right, pair, pair_other,
    side_ref, half_ref, image_ref, weight_ref, rt_high, rt_low, q_high, q_low
):
    start = lax.axis_index("slab") * ROWS
    core = lax.axis_index("sub") & 1

    @pl.when(pl.program_id(0) == 0)
    def _():
        for a in range(GROUPS):
            members = jnp.zeros((), jnp.int32)
            for e in range(ROWS):
                members += jnp.where(agg_of[start + e] == a, 1, 0)
            weight_ref[span(a), :] = COARSE_WEIGHT / jnp.full((DOF, COLS), members.astype(F32))
        restrict_rows = []
        for e in range(ROWS):
            group = agg_of[start + e]
            high, low = halves(placed(prolong[e], group - 2 * core))
            q_high[span(e), :] = high
            q_low[span(e), :] = low
            parts = [placed(prolong[e], group - 2 * t) for t in range(GROUPS // 2)]
            restrict_rows.append(jnp.concatenate(parts, axis=1))
        high, low = halves(jnp.concatenate(restrict_rows, axis=0).T)
        rt_high[...] = high
        rt_low[...] = low

    side_ref[...] = pair[:, WIDE:] + pair_other[:, WIDE:]
    own = halves(pair[:, :WIDE] + pair_other[:, :WIDE])
    half_ref[...] = product(own, (q_high[...], q_low[...]))
    total = product(own, halves(field[...]))
    image_ref[:, :COLS] = total[:, :COLS] - right[...]
    image_ref[:, COLS:] = total[:, COLS:]


def own_step(agg_of, prolong, message, right, pair, pair_other):
    steps = 2
    whole = lambda *dims: pl.BlockSpec(dims, lambda i: (0,) * len(dims))
    part = lambda width: pl.BlockSpec((WIDE // steps, width), lambda i: (i, 0))
    return pl.pallas_call(
        own_kernel,
        grid=(steps,),
        in_specs=[SMEM, whole(*prolong.shape), whole(WIDE, 2 * COLS), part(COLS)] + [part(2 * WIDE)] * 2,
        out_specs=[part(WIDE), part(PAIR), part(2 * COLS), whole(COARSE, COLS)] + [whole(COARSE, WIDE)] * 2,
        out_shape=[
            shape(WIDE, WIDE),
            shape(WIDE, PAIR),
            shape(WIDE, 2 * COLS),
            shape(COARSE, COLS),
            shape(COARSE, WIDE, dtype=BF16),
            shape(COARSE, WIDE, dtype=BF16),
        ],
        scratch_shapes=[pltpu.VMEM((WIDE, PAIR), BF16)] * 2,
        compiler_params=params(),
        name="own_step",
    )(agg_of, prolong, message, right, pair, pair_other)


def image_kernel(
    own_image, side, received, received_other, message, rt_high, rt_low,
    keep_ref, send_ref, rhs_keep_ref, rhs_send_ref, high_ref, low_ref
):
    core = lax.axis_index("sub") & 1
    field = halves(message[:WIDE, :])
    rows = WIDE // 2
    rhs = None
    for group in range(2):
        part = span(group, rows)
        extra = jnp.where(core == group, received[...], received_other[...])
        high, low = halves(side[part, :] + extra)
        high_ref[part, :] = high
        low_ref[part, :] = low
        total = own_image[part, :] + product((high, low), field)
        keep_ref[part, :] = total[:, :COLS]
        send_ref[part, :] = total[:, COLS:]
        term = product((rt_high[:, part], rt_low[:, part]), halves(total))
        rhs = term if rhs is None else rhs + term
    rhs_keep_ref[...] = rhs[:, :COLS]
    rhs_send_ref[...] = rhs[:, COLS:]


def image(own_image, side, received, received_other, message, rt_high, rt_low):
    return pl.pallas_call(
        image_kernel,
        in_specs=[VMEM] * 7,
        out_specs=[VMEM] * 6,
        out_shape=[shape(WIDE, COLS)] * 2 + [shape(COARSE, COLS)] * 2 + [shape(WIDE, WIDE, dtype=BF16)] * 2,
        compiler_params=params(),
        name="image",
    )(own_image, side, received, received_other, message, rt_high, rt_low)


def ghost_kernel(agg_of, d_high, d_low, mine, other, upper_ref, lower_ref, q_high, q_low):
    _, near, far = neighbours()
    sub = lax.axis_index("sub")
    core = sub & 1
    start = jnp.where(((sub >> 1) & 1) == 0, near, far) * ROWS
    for r in range(ROWS):
        columns = span(r % HALF_ROWS)
        piece = jnp.where(core == r // HALF_ROWS, mine[:, columns], other[:, columns])
        high, low = halves(placed(piece, agg_of[start + r] - 2 * core))
        q_high[span(r), :] = high
        q_low[span(r), :] = low
    for group, ref in enumerate((upper_ref, lower_ref)):
        part = span(group, WIDE // 2)
        ref[...] = product((d_high[part, :], d_low[part, :]), (q_high[...], q_low[...]))


def ghost_step(agg_of, d_high, d_low, mine, other):
    return pl.pallas_call(
        ghost_kernel,
        in_specs=[SMEM] + [VMEM] * 4,
        out_specs=[VMEM] * 2,
        out_shape=[shape(WIDE // 2, PAIR)] * 2,
        scratch_shapes=[pltpu.VMEM((WIDE, PAIR), BF16)] * 2,
        compiler_params=params(),
        name="ghost_step",
    )(agg_of, d_high, d_low, mine, other)


def near_and_far(mine, received):
    is_near = ((lax.axis_index("sub") >> 1) & 1) == 0
    return jnp.where(is_near, mine, received), jnp.where(is_near, received, mine)


def coarse_kernel(own, own_received, upper, lower, upper_received, lower_received, rt_high, rt_low, *refs):
    regions, (high_ref, low_ref) = refs[:3], refs[3:]
    side = jnp.concatenate([upper[...], lower[...]], axis=0)
    side_received = jnp.concatenate([upper_received[...], lower_received[...]], axis=0)
    sides = jnp.concatenate(near_and_far(side, side_received), axis=1)
    sides = product((rt_high[...], rt_low[...]), halves(sides))
    centre = narrow_product((rt_high[...], rt_low[...]), own[...] + own_received[...])
    values = (sides[:, :PAIR], centre, sides[:, PAIR:])
    for region, (ref, value) in enumerate(zip(regions, values)):
        ref[...] = value
        high, low = halves(value)
        high_ref[:, span(region, PAIR)] = high
        low_ref[:, span(region, PAIR)] = low


def coarse_half(own, own_received, side, side_received, rt_high, rt_low):
    return pl.pallas_call(
        coarse_kernel,
        in_specs=[VMEM] * 8,
        out_specs=[VMEM] * 5,
        out_shape=[shape(COARSE, PAIR)] * 3 + [shape(COARSE, 3 * PAIR, dtype=BF16)] * 2,
        compiler_params=params(),
        name="coarse_half",
    )(own, own_received, *side, *side_received, rt_high, rt_low)


def share_kernel(*refs):
    mine, other, (op_ref, high_ref, low_ref, natural) = refs[:3], refs[3:6], refs[6:]
    sub = lax.axis_index("sub")
    odd = lax.axis_index("slab") & 1
    is_first = (sub & 1) == 0
    places = (2 * (1 - odd), 1, 2 * odd)
    for region, place in enumerate(places):
        own_value, other_value = mine[region][...], other[region][...]
        first = jnp.where(is_first, own_value, other_value)
        second = jnp.where(is_first, other_value, own_value)
        natural[:, aligned(place, COARSE)] = jnp.concatenate([first, second], axis=1)
        high, low = halves(other_value)
        high_ref[:, span(region, PAIR)] = high
        low_ref[:, span(region, PAIR)] = low
    share = op_ref.shape[1]
    for k in range(BANDS // share):

        @pl.when(sub == k)
        def _():
            for a in range(GROUPS):
                for q in range(share):
                    op_ref[a, q] = natural[span(a), span(k * share + q)]


def coarse_share(mine, other):
    return pl.pallas_call(
        share_kernel,
        in_specs=[VMEM] * 6,
        out_specs=[VMEM] * 3,
        out_shape=[shape(GROUPS, BANDS // SUBS, DOF, DOF)] + [shape(COARSE, 3 * PAIR, dtype=BF16)] * 2,
        scratch_shapes=[pltpu.VMEM((COARSE, 3 * COARSE), F32)],
        compiler_params=params(),
        name="coarse_share",
    )(*mine, *other)


def lift_kernel(agg_of, own, own_received, upper, lower, upper_received, lower_received, smoother, prolong, w_ref):
    start = lax.axis_index("slab") * ROWS
    core = lax.axis_index("sub") & 1
    for e in range(ROWS):
        rows = span(e)
        side, side_received = ((upper, upper_received), (lower, lower_received))[e // HALF_ROWS]
        near, far = near_and_far(side[span(e % HALF_ROWS), :], side_received[span(e % HALF_ROWS), :])
        g_half = jnp.concatenate([near, own[rows, :] + own_received[rows, :], far], axis=1)
        w_ref[rows, :] = -product(halves(smoother[e]), halves(g_half))
        w_ref[rows, span(1, PAIR)] += placed(prolong[e], agg_of[start + e] - 2 * core)


def lift_half(agg_of, own, own_received, side, side_received, smoother, prolong):
    return pl.pallas_call(
        lift_kernel,
        in_specs=[SMEM] + [VMEM] * 8,
        out_specs=VMEM,
        out_shape=shape(WIDE, 3 * PAIR),
        compiler_params=params(),
        name="lift_half",
    )(agg_of, own, own_received, *side, *side_received, smoother, prolong)


def first_kernel(keep, received, weight, first_ref):
    first_ref[...] = -weight[...] * (keep[...] + received[...])


def first_correction(keep, received, weight):
    return pl.pallas_call(
        first_kernel,
        in_specs=[VMEM] * 3,
        out_specs=VMEM,
        out_shape=shape(COARSE, COLS),
        compiler_params=params(),
        name="first_correction",
    )(keep, received, weight)


def base_kernel(smoother, message, keep, received, base_ref):
    for e in range(ROWS):
        residual = -(keep[span(e), :] + received[span(e), :])
        base_ref[span(e), :] = message[span(e), :COLS] + narrow_product(halves(smoother[e]), residual)


def base_step(smoother, message, keep, received):
    return pl.pallas_call(
        base_kernel,
        in_specs=[VMEM] * 4,
        out_specs=VMEM,
        out_shape=shape(WIDE, COLS),
        compiler_params=params(),
        name="base_step",
    )(smoother, message, keep, received)


def core_parts(*fields):
    core = lax.axis_index("sub") & 1
    for which in (core, 1 - core):
        yield jnp.concatenate([field[aligned(which, PAIR), :] for field in fields], axis=0)


def sweep_kernel(*refs):
    operators, (first, weight, near, own, far, next_ref) = refs[:-6], refs[-6:]
    mine = (operators[0][...], operators[1][...])
    if len(operators) == 5:
        other = halves(jnp.concatenate([region[...] for region in operators[2:]], axis=1))
    else:
        other = (operators[2][...], operators[3][...])
    total = None
    for operator, field in zip((mine, other), core_parts(near, own, far)):
        part = narrow_product(operator, field)
        total = part if total is None else total + part
    next_ref[...] = own[...] + first[...] - weight[...] * total


def sweep(operators, first, weight, near, own, far):
    return pl.pallas_call(
        sweep_kernel,
        in_specs=[VMEM] * (len(operators) + 5),
        out_specs=VMEM,
        out_shape=shape(COARSE, COLS),
        compiler_params=params(),
        name="sweep",
    )(*operators, first, weight, near, own, far)


def lifted_kernel(mine, other, base, own, base_ref, high_ref, low_ref):
    total = base[...]
    for place, (operator, field) in enumerate(zip((mine, other), core_parts(own))):
        total += narrow_product(halves(operator[:, span(1, PAIR)]), field)
        for t, region in enumerate((0, 2)):
            high, low = halves(operator[:, span(region, PAIR)])
            high_ref[:, span(2 * place + t, PAIR)] = high
            low_ref[:, span(2 * place + t, PAIR)] = low
    base_ref[...] = total


def lifted(mine, other, base, own):
    return pl.pallas_call(
        lifted_kernel,
        in_specs=[VMEM] * 4,
        out_specs=[VMEM] * 3,
        out_shape=[shape(WIDE, COLS)] + [shape(WIDE, 2 * COARSE, dtype=BF16)] * 2,
        compiler_params=params(),
        name="lifted",
    )(mine, other, base, own)


def last_kernel(w_high, w_low, base, near, far, out_ref):
    field = jnp.concatenate(list(core_parts(near, far)), axis=0)
    out_ref[...] = base[...] + narrow_product((w_high[...], w_low[...]), field)


def last_step(w_high, w_low, base, near, far):
    return pl.pallas_call(
        last_kernel,
        in_specs=[VMEM] * 5,
        out_specs=VMEM,
        out_shape=shape(WIDE, COLS),
        compiler_params=params(),
        name="last_step",
    )(w_high, w_low, base, near, far)


def swaps(size, start):
    pairs = [(i, i + 1) for i in range(start, size - 1, 2)]
    return pairs + [(j, i) for i, j in pairs]


def from_neighbours(value):
    size = lax.axis_size("slab")
    near = lax.ppermute(value, "slab", swaps(size, 0))
    far = lax.ppermute(value, "slab", swaps(size, 1))
    return near, far


def from_side(value):
    size, subs = lax.axis_size("slab"), lax.axis_size("sub")
    pairs = [
        (i * subs + k, j * subs + k) for k in range(subs) for i, j in swaps(size, (k >> 1) & 1)
    ]
    return lax.ppermute(value, ("slab", "sub"), pairs)


def swapped(value, bit):
    size = lax.axis_size("sub")
    return lax.ppermute(value, "sub", [(i, i ^ bit) for i in range(size)])


def per_device(fine_blocks, prolong, smoother, right_side, agg_of, col_slot, send_rows, send_count):
    pair, mine, theirs, message, right = start_step(
        col_slot, send_rows, send_count, fine_blocks, smoother, right_side, prolong
    )
    side_message = from_side(message)
    theirs = swapped(theirs, 1)
    received = swapped(mine + theirs, 2)
    pair, theirs = lax.optimization_barrier((pair, theirs))
    side, own_half, own_image, weight, rt_high, rt_low = own_step(
        agg_of, prolong, message, right, pair, swapped(pair, 1)
    )
    received, side, own_half = lax.optimization_barrier((received, side, own_half))
    own_received = swapped(own_half, 2)
    keep, send, rhs_keep, rhs_send, d_high, d_low = image(
        own_image, side, received, swapped(received, 1), side_message, rt_high, rt_low
    )
    rhs_received = swapped(rhs_send, 2)
    ghosts = side_message[WIDE:]
    side_half = ghost_step(agg_of, d_high, d_low, ghosts, swapped(ghosts, 1))
    side_received = [swapped(part, 2) for part in side_half]
    first = first_correction(rhs_keep, rhs_received, weight)
    near, far = from_neighbours(first)
    send, side_received = lax.optimization_barrier((send, side_received))
    base = base_step(smoother, message, keep, swapped(send, 2))
    *coarse, mine_high, mine_low = coarse_half(
        own_half, own_received, side_half, side_received, rt_high, rt_low
    )
    coarse_other = [swapped(region, 1) for region in coarse]
    near, far, coarse_other = lax.optimization_barrier((near, far, coarse_other))
    correction = sweep((mine_high, mine_low, *coarse_other), first, weight, near, first, far)
    coarse_op, other_high, other_low = coarse_share(coarse, coarse_other)
    lift = lift_half(agg_of, own_half, own_received, side_half, side_received, smoother, prolong)
    for index in range(1, COARSE_SWEEPS - 1):
        near, far = from_neighbours(correction)
        if index == 1:
            shadowed = (near, far, lift, base, other_high, other_low)
            near, far, lift, base, other_high, other_low = lax.optimization_barrier(shadowed)
        operators = (mine_high, mine_low, other_high, other_low)
        correction = sweep(operators, first, weight, near, correction, far)
    lift_other = swapped(lift, 1)
    near, far = from_neighbours(correction)
    base, w_high, w_low = lifted(lift, lift_other, base, correction)
    solution = last_step(w_high, w_low, base, near, far)
    return coarse_op, solution.reshape(ROWS, DOF, COLS)


def solution(mesh):
    placed_args = (
        P("slab", "sub", None, None),
        P("slab", None, None),
        P("slab", None, None),
        P("slab", None, None),
        P(),
        P("slab", "sub"),
        P(),
        P(),
    )
    return jax.shard_map(
        per_device,
        mesh=mesh,
        in_specs=placed_args,
        out_specs=(P("slab", "sub", None, None), P("slab", None, "sub")),
        check_vma=False,
    )
```

```python
import jax
import jax.numpy as jnp
from jax import lax
from jax.experimental import pallas as pl
from jax.experimental.pallas import tpu as pltpu
from jax.sharding import PartitionSpec as P

COARSE_SWEEPS = 3
COARSE_WEIGHT = 0.25
F32 = jnp.float32
BF16 = jnp.bfloat16
VMEM = pl.BlockSpec(memory_space=pltpu.VMEM)
SMEM = pl.BlockSpec(memory_space=pltpu.SMEM)
HBM = pl.BlockSpec(memory_space=pltpu.HBM)
ROWS = 8
GHOSTS = 8
SLOTS = ROWS + 2 * GHOSTS
GROUPS = 4
BANDS = 3 * GROUPS
DOF = 64
COLS = 128
SUBS = 4
HALF_ROWS = ROWS // 2
WIDE = ROWS * DOF
PAIR = 2 * DOF
COARSE = GROUPS * DOF


def params(limit=24):
    return pltpu.CompilerParams(vmem_limit_bytes=limit << 20)


def shape(*dims, dtype=F32):
    return jax.ShapeDtypeStruct(dims, dtype)


def halves(value):
    high = value.astype(BF16)
    return high, (value - high.astype(F32)).astype(BF16)


def mm(a, b):
    return jnp.dot(a, b, preferred_element_type=F32)


def product(left, right):
    left_high, left_low = left
    right_high, right_low = right
    return mm(left_high, right_high) + (mm(left_high, right_low) + mm(left_low, right_high))


def narrow_product(left, value):
    left_high, left_low = left
    high, low = halves(value)
    width = value.shape[1]
    both = mm(left_high, jnp.concatenate([high, low], axis=1))
    return both[:, :width] + (both[:, width:] + mm(left_low, high))


def span(index, size=DOF):
    return slice(index * size, (index + 1) * size)


def aligned(index, size):
    return pl.ds(pl.multiple_of(index * size, size), size)


def neighbours():
    slab, size = lax.axis_index("slab"), lax.axis_size("slab")
    odd = slab & 1
    near = jnp.minimum(slab ^ 1, size - 1)
    far = jnp.where(odd == 1, jnp.minimum(slab + 1, size - 1), jnp.maximum(slab - 1, 0))
    return slab, near, far


def start_kernel(
    col_hbm, rows_hbm, counts_hbm, blocks_hbm, smoother_hbm, right_hbm, prolong_hbm,
    pair_ref, mine_ref, theirs_ref, message_ref, right_ref,
    col_slot, rows, counts, blocks, smoother, right, prolong, sems, block_sems, *parts
):
    slab, size, sub = lax.axis_index("slab"), lax.axis_size("slab"), lax.axis_index("sub")
    below = jnp.maximum(slab - 1, 0)
    above = jnp.minimum(slab + 1, size - 1)
    core = sub & 1
    chip = (sub >> 1) & 1
    sources = [
        (smoother_hbm, smoother),
        (right_hbm.at[:, :, aligned(sub, COLS)], right.at[0]),
        (right_hbm.at[:, :, aligned(sub ^ 2, COLS)], right.at[1]),
        (prolong_hbm.at[pl.ds(core * HALF_ROWS, HALF_ROWS)], prolong),
        (col_hbm, col_slot),
        (rows_hbm.at[below, sub], rows.at[0]),
        (rows_hbm.at[above, sub], rows.at[1]),
        (counts_hbm.at[sub], counts),
    ]
    copies = [pltpu.make_async_copy(s, d, sems.at[i]) for i, (s, d) in enumerate(sources)]
    block_copies = [
        pltpu.make_async_copy(blocks_hbm.at[e], blocks.at[e], block_sems.at[e]) for e in range(ROWS)
    ]
    for copy in copies + block_copies:
        copy.start()
    for copy in copies:
        copy.wait()

    for e in range(ROWS):
        right_ref[span(e), :] = right[0, e]
        wide = jnp.concatenate([right[0, e], right[1, e]], axis=1)
        message_ref[span(e), :] = product(halves(smoother[e]), halves(wide))
    message_ref[span(ROWS), :] = jnp.concatenate([prolong[i] for i in range(HALF_ROWS)], axis=1)

    lower_count = jnp.where(slab > 0, counts[1, below], 0)
    upper_count = jnp.where(slab < size - 1, counts[0, above], 0)
    lower_region = 1 + (1 - (slab & 1) ^ chip)
    lower_start = lower_region * ROWS
    upper_start = (3 - lower_region) * ROWS
    upper_lanes = lax.broadcasted_iota(jnp.int32, (DOF, PAIR), 1) >= DOF
    for group in range(ROWS // HALF_ROWS):
        for position, part in enumerate(parts):
            part[...] = jnp.zeros_like(part)
            block_copies[group * HALF_ROWS + position].wait()
        for j in range(blocks.shape[1]):
            for position, part in enumerate(parts):
                e = group * HALF_ROWS + position
                slot = col_slot[e, j]
                is_own = slot < ROWS
                is_upper = slot >= ROWS + GHOSTS
                side = jnp.where(is_upper, 1, 0)
                place = jnp.where(is_own, 0, slot - ROWS - side * GHOSTS)
                listed = rows[side, 1 - side, place] + jnp.where(is_upper, upper_start, lower_start)
                column = jnp.where(is_own, slot, listed)
                count = jnp.where(is_upper, upper_count, lower_count)
                live = jnp.where(is_own | (place < count), 1.0, 0.0)
                odd_column = column & 1
                lower_scale = jnp.where(odd_column == 0, live, 0.0)
                upper_scale = jnp.where(odd_column == 1, live, 0.0)
                block = blocks[e, j]
                doubled = jnp.concatenate([block, block], axis=1)
                part[:, aligned(column >> 1, PAIR)] += doubled * jnp.where(upper_lanes, upper_scale, lower_scale)
        for position, part in enumerate(parts):
            pair_ref[span(group * HALF_ROWS + position), :] = part[:, : 2 * WIDE]

        @pl.when(core == group)
        def _():
            for position, part in enumerate(parts):
                mine_ref[span(position), :] = part[:, 2 * WIDE :]

        @pl.when(core != group)
        def _():
            for position, part in enumerate(parts):
                theirs_ref[span(position), :] = part[:, 2 * WIDE :]


def start_step(col_slot, send_rows, send_count, blocks, smoother, right_side, prolong):
    counts = jnp.transpose(send_count, (1, 2, 0))
    arrays = (col_slot, send_rows, counts, blocks, smoother, right_side, prolong)
    return pl.pallas_call(
        start_kernel,
        in_specs=[HBM] * 7,
        out_specs=[VMEM] * 5,
        out_shape=[
            shape(WIDE, 2 * WIDE),
            shape(WIDE // 2, WIDE),
            shape(WIDE // 2, WIDE),
            shape(WIDE + DOF, 2 * COLS),
            shape(WIDE, COLS),
        ],
        scratch_shapes=[
            pltpu.SMEM(col_slot.shape, jnp.int32),
            pltpu.SMEM((2, 2, GHOSTS), jnp.int32),
            pltpu.SMEM((2, send_count.shape[0]), jnp.int32),
            pltpu.VMEM(blocks.shape, F32),
            pltpu.VMEM(smoother.shape, F32),
            pltpu.VMEM((2, ROWS, DOF, COLS), F32),
            pltpu.VMEM((HALF_ROWS, DOF, DOF), F32),
            pltpu.SemaphoreType.DMA((8,)),
            pltpu.SemaphoreType.DMA((ROWS,)),
        ]
        + [pltpu.VMEM((DOF, 3 * WIDE), F32)] * HALF_ROWS,
        compiler_params=params(),
        name="start_step",
    )(*(pltpu.with_memory_space_constraint(a, pltpu.HBM) for a in arrays))


def placed(piece, index):
    upper = lax.broadcasted_iota(jnp.int32, (DOF, PAIR), 1) >= DOF
    doubled = jnp.concatenate([piece, piece], axis=1)
    lower_scale = jnp.where(index == 0, 1.0, 0.0)
    upper_scale = jnp.where(index == 1, 1.0, 0.0)
    return doubled * jnp.where(upper, upper_scale, lower_scale)


def own_kernel(
    agg_of, prolong, field, right, pair, pair_other,
    side_ref, half_ref, image_ref, weight_ref, rt_high, rt_low, q_high, q_low
):
    start = lax.axis_index("slab") * ROWS
    core = lax.axis_index("sub") & 1

    @pl.when(pl.program_id(0) == 0)
    def _():
        for a in range(GROUPS):
            members = jnp.zeros((), jnp.int32)
            for e in range(ROWS):
                members += jnp.where(agg_of[start + e] == a, 1, 0)
            weight_ref[span(a), :] = COARSE_WEIGHT / jnp.full((DOF, COLS), members.astype(F32))
        restrict_rows = []
        for e in range(ROWS):
            group = agg_of[start + e]
            high, low = halves(placed(prolong[e], group - 2 * core))
            q_high[span(e), :] = high
            q_low[span(e), :] = low
            parts = [placed(prolong[e], group - 2 * t) for t in range(GROUPS // 2)]
            restrict_rows.append(jnp.concatenate(parts, axis=1))
        high, low = halves(jnp.concatenate(restrict_rows, axis=0).T)
        rt_high[...] = high
        rt_low[...] = low

    side_ref[...] = pair[:, WIDE:] + pair_other[:, WIDE:]
    own = halves(pair[:, :WIDE] + pair_other[:, :WIDE])
    half_ref[...] = product(own, (q_high[...], q_low[...]))
    total = product(own, halves(field[...]))
    image_ref[:, :COLS] = total[:, :COLS] - right[...]
    image_ref[:, COLS:] = total[:, COLS:]


def own_step(agg_of, prolong, message, right, pair, pair_other):
    steps = 2
    whole = lambda *dims: pl.BlockSpec(dims, lambda i: (0,) * len(dims))
    part = lambda width: pl.BlockSpec((WIDE // steps, width), lambda i: (i, 0))
    return pl.pallas_call(
        own_kernel,
        grid=(steps,),
        in_specs=[SMEM, whole(*prolong.shape), whole(WIDE, 2 * COLS), part(COLS)] + [part(2 * WIDE)] * 2,
        out_specs=[part(WIDE), part(PAIR), part(2 * COLS), whole(COARSE, COLS)] + [whole(COARSE, WIDE)] * 2,
        out_shape=[
            shape(WIDE, WIDE),
            shape(WIDE, PAIR),
            shape(WIDE, 2 * COLS),
            shape(COARSE, COLS),
            shape(COARSE, WIDE, dtype=BF16),
            shape(COARSE, WIDE, dtype=BF16),
        ],
        scratch_shapes=[pltpu.VMEM((WIDE, PAIR), BF16)] * 2,
        compiler_params=params(),
        name="own_step",
    )(agg_of, prolong, message, right, pair, pair_other)


def image_kernel(
    own_image, side, received, received_other, message, rt_high, rt_low,
    keep_ref, send_ref, rhs_keep_ref, rhs_send_ref, high_ref, low_ref
):
    core = lax.axis_index("sub") & 1
    field = halves(message[:WIDE, :])
    rows = WIDE // 2
    rhs = None
    for group in range(2):
        part = span(group, rows)
        extra = jnp.where(core == group, received[...], received_other[...])
        high, low = halves(side[part, :] + extra)
        high_ref[part, :] = high
        low_ref[part, :] = low
        total = own_image[part, :] + product((high, low), field)
        keep_ref[part, :] = total[:, :COLS]
        send_ref[part, :] = total[:, COLS:]
        term = product((rt_high[:, part], rt_low[:, part]), halves(total))
        rhs = term if rhs is None else rhs + term
    rhs_keep_ref[...] = rhs[:, :COLS]
    rhs_send_ref[...] = rhs[:, COLS:]


def image(own_image, side, received, received_other, message, rt_high, rt_low):
    return pl.pallas_call(
        image_kernel,
        in_specs=[VMEM] * 7,
        out_specs=[VMEM] * 6,
        out_shape=[shape(WIDE, COLS)] * 2 + [shape(COARSE, COLS)] * 2 + [shape(WIDE, WIDE, dtype=BF16)] * 2,
        compiler_params=params(),
        name="image",
    )(own_image, side, received, received_other, message, rt_high, rt_low)


def ghost_kernel(agg_of, d_high, d_low, mine, other, upper_ref, lower_ref, q_high, q_low):
    _, near, far = neighbours()
    sub = lax.axis_index("sub")
    core = sub & 1
    start = jnp.where(((sub >> 1) & 1) == 0, near, far) * ROWS
    for r in range(ROWS):
        columns = span(r % HALF_ROWS)
        piece = jnp.where(core == r // HALF_ROWS, mine[:, columns], other[:, columns])
        high, low = halves(placed(piece, agg_of[start + r] - 2 * core))
        q_high[span(r), :] = high
        q_low[span(r), :] = low
    for group, ref in enumerate((upper_ref, lower_ref)):
        part = span(group, WIDE // 2)
        ref[...] = product((d_high[part, :], d_low[part, :]), (q_high[...], q_low[...]))


def ghost_step(agg_of, d_high, d_low, mine, other):
    return pl.pallas_call(
        ghost_kernel,
        in_specs=[SMEM] + [VMEM] * 4,
        out_specs=[VMEM] * 2,
        out_shape=[shape(WIDE // 2, PAIR)] * 2,
        scratch_shapes=[pltpu.VMEM((WIDE, PAIR), BF16)] * 2,
        compiler_params=params(),
        name="ghost_step",
    )(agg_of, d_high, d_low, mine, other)


def near_and_far(mine, received):
    is_near = ((lax.axis_index("sub") >> 1) & 1) == 0
    return jnp.where(is_near, mine, received), jnp.where(is_near, received, mine)


def coarse_kernel(own, own_received, upper, lower, upper_received, lower_received, rt_high, rt_low, *refs):
    regions, (high_ref, low_ref) = refs[:3], refs[3:]
    side = jnp.concatenate([upper[...], lower[...]], axis=0)
    side_received = jnp.concatenate([upper_received[...], lower_received[...]], axis=0)
    sides = jnp.concatenate(near_and_far(side, side_received), axis=1)
    sides = product((rt_high[...], rt_low[...]), halves(sides))
    centre = narrow_product((rt_high[...], rt_low[...]), own[...] + own_received[...])
    values = (sides[:, :PAIR], centre, sides[:, PAIR:])
    for region, (ref, value) in enumerate(zip(regions, values)):
        ref[...] = value
        high, low = halves(value)
        high_ref[:, span(region, PAIR)] = high
        low_ref[:, span(region, PAIR)] = low


def coarse_half(own, own_received, side, side_received, rt_high, rt_low):
    return pl.pallas_call(
        coarse_kernel,
        in_specs=[VMEM] * 8,
        out_specs=[VMEM] * 5,
        out_shape=[shape(COARSE, PAIR)] * 3 + [shape(COARSE, 3 * PAIR, dtype=BF16)] * 2,
        compiler_params=params(),
        name="coarse_half",
    )(own, own_received, *side, *side_received, rt_high, rt_low)


def share_kernel(*refs):
    mine, other, (op_ref, high_ref, low_ref, natural) = refs[:3], refs[3:6], refs[6:]
    sub = lax.axis_index("sub")
    odd = lax.axis_index("slab") & 1
    is_first = (sub & 1) == 0
    places = (2 * (1 - odd), 1, 2 * odd)
    for region, place in enumerate(places):
        own_value, other_value = mine[region][...], other[region][...]
        first = jnp.where(is_first, own_value, other_value)
        second = jnp.where(is_first, other_value, own_value)
        natural[:, aligned(place, COARSE)] = jnp.concatenate([first, second], axis=1)
        high, low = halves(other_value)
        high_ref[:, span(region, PAIR)] = high
        low_ref[:, span(region, PAIR)] = low
    share = op_ref.shape[1]
    for k in range(BANDS // share):

        @pl.when(sub == k)
        def _():
            for a in range(GROUPS):
                for q in range(share):
                    op_ref[a, q] = natural[span(a), span(k * share + q)]


def coarse_share(mine, other):
    return pl.pallas_call(
        share_kernel,
        in_specs=[VMEM] * 6,
        out_specs=[VMEM] * 3,
        out_shape=[shape(GROUPS, BANDS // SUBS, DOF, DOF)] + [shape(COARSE, 3 * PAIR, dtype=BF16)] * 2,
        scratch_shapes=[pltpu.VMEM((COARSE, 3 * COARSE), F32)],
        compiler_params=params(),
        name="coarse_share",
    )(*mine, *other)


def lift_kernel(agg_of, own, own_received, upper, lower, upper_received, lower_received, smoother, prolong, w_ref):
    start = lax.axis_index("slab") * ROWS
    core = lax.axis_index("sub") & 1
    for e in range(ROWS):
        rows = span(e)
        side, side_received = ((upper, upper_received), (lower, lower_received))[e // HALF_ROWS]
        near, far = near_and_far(side[span(e % HALF_ROWS), :], side_received[span(e % HALF_ROWS), :])
        g_half = jnp.concatenate([near, own[rows, :] + own_received[rows, :], far], axis=1)
        w_ref[rows, :] = -product(halves(smoother[e]), halves(g_half))
        w_ref[rows, span(1, PAIR)] += placed(prolong[e], agg_of[start + e] - 2 * core)


def lift_half(agg_of, own, own_received, side, side_received, smoother, prolong):
    return pl.pallas_call(
        lift_kernel,
        in_specs=[SMEM] + [VMEM] * 8,
        out_specs=VMEM,
        out_shape=shape(WIDE, 3 * PAIR),
        compiler_params=params(),
        name="lift_half",
    )(agg_of, own, own_received, *side, *side_received, smoother, prolong)


def first_kernel(keep, received, weight, first_ref):
    first_ref[...] = -weight[...] * (keep[...] + received[...])


def first_correction(keep, received, weight):
    return pl.pallas_call(
        first_kernel,
        in_specs=[VMEM] * 3,
        out_specs=VMEM,
        out_shape=shape(COARSE, COLS),
        compiler_params=params(),
        name="first_correction",
    )(keep, received, weight)


def base_kernel(smoother, message, keep, received, base_ref):
    for e in range(ROWS):
        residual = -(keep[span(e), :] + received[span(e), :])
        base_ref[span(e), :] = message[span(e), :COLS] + narrow_product(halves(smoother[e]), residual)


def base_step(smoother, message, keep, received):
    return pl.pallas_call(
        base_kernel,
        in_specs=[VMEM] * 4,
        out_specs=VMEM,
        out_shape=shape(WIDE, COLS),
        compiler_params=params(),
        name="base_step",
    )(smoother, message, keep, received)


def core_parts(*fields):
    core = lax.axis_index("sub") & 1
    for which in (core, 1 - core):
        yield jnp.concatenate([field[aligned(which, PAIR), :] for field in fields], axis=0)


def sweep_kernel(*refs):
    operators, (first, weight, near, own, far, next_ref) = refs[:-6], refs[-6:]
    mine = (operators[0][...], operators[1][...])
    if len(operators) == 5:
        other = halves(jnp.concatenate([region[...] for region in operators[2:]], axis=1))
    else:
        other = (operators[2][...], operators[3][...])
    total = None
    for operator, field in zip((mine, other), core_parts(near, own, far)):
        part = narrow_product(operator, field)
        total = part if total is None else total + part
    next_ref[...] = own[...] + first[...] - weight[...] * total


def sweep(operators, first, weight, near, own, far):
    return pl.pallas_call(
        sweep_kernel,
        in_specs=[VMEM] * (len(operators) + 5),
        out_specs=VMEM,
        out_shape=shape(COARSE, COLS),
        compiler_params=params(),
        name="sweep",
    )(*operators, first, weight, near, own, far)


def lifted_kernel(mine, other, base, own, base_ref, high_ref, low_ref):
    total = base[...]
    for place, (operator, field) in enumerate(zip((mine, other), core_parts(own))):
        total += narrow_product(halves(operator[:, span(1, PAIR)]), field)
        for t, region in enumerate((0, 2)):
            high, low = halves(operator[:, span(region, PAIR)])
            high_ref[:, span(2 * place + t, PAIR)] = high
            low_ref[:, span(2 * place + t, PAIR)] = low
    base_ref[...] = total


def lifted(mine, other, base, own):
    return pl.pallas_call(
        lifted_kernel,
        in_specs=[VMEM] * 4,
        out_specs=[VMEM] * 3,
        out_shape=[shape(WIDE, COLS)] + [shape(WIDE, 2 * COARSE, dtype=BF16)] * 2,
        compiler_params=params(),
        name="lifted",
    )(mine, other, base, own)


def last_kernel(w_high, w_low, base, near, far, out_hbm, out, sems):
    field = jnp.concatenate(list(core_parts(near, far)), axis=0)
    copies = []
    for group in range(2):
        part = span(group, WIDE // 2)
        out[part, :] = base[part, :] + narrow_product((w_high[part, :], w_low[part, :]), field)
        copies.append(pltpu.make_async_copy(out.at[part], out_hbm.at[part], sems.at[group]))
        copies[-1].start()
    for copy in copies:
        copy.wait()


def last_step(w_high, w_low, base, near, far):
    return pl.pallas_call(
        last_kernel,
        in_specs=[VMEM] * 5,
        out_specs=HBM,
        out_shape=shape(WIDE, COLS),
        scratch_shapes=[pltpu.VMEM((WIDE, COLS), F32), pltpu.SemaphoreType.DMA((2,))],
        compiler_params=params(),
        name="last_step",
    )(w_high, w_low, base, near, far)


def swaps(size, start):
    pairs = [(i, i + 1) for i in range(start, size - 1, 2)]
    return pairs + [(j, i) for i, j in pairs]


def from_neighbours(value):
    size = lax.axis_size("slab")
    near = lax.ppermute(value, "slab", swaps(size, 0))
    far = lax.ppermute(value, "slab", swaps(size, 1))
    return near, far


def from_side(value):
    size, subs = lax.axis_size("slab"), lax.axis_size("sub")
    pairs = [
        (i * subs + k, j * subs + k) for k in range(subs) for i, j in swaps(size, (k >> 1) & 1)
    ]
    return lax.ppermute(value, ("slab", "sub"), pairs)


def swapped(value, bit):
    size = lax.axis_size("sub")
    return lax.ppermute(value, "sub", [(i, i ^ bit) for i in range(size)])


def per_device(fine_blocks, prolong, smoother, right_side, agg_of, col_slot, send_rows, send_count):
    pair, mine, theirs, message, right = start_step(
        col_slot, send_rows, send_count, fine_blocks, smoother, right_side, prolong
    )
    side_message = from_side(message)
    theirs = swapped(theirs, 1)
    received = swapped(mine + theirs, 2)
    pair, theirs = lax.optimization_barrier((pair, theirs))
    side, own_half, own_image, weight, rt_high, rt_low = own_step(
        agg_of, prolong, message, right, pair, swapped(pair, 1)
    )
    received, side, own_half = lax.optimization_barrier((received, side, own_half))
    own_received = swapped(own_half, 2)
    keep, send, rhs_keep, rhs_send, d_high, d_low = image(
        own_image, side, received, swapped(received, 1), side_message, rt_high, rt_low
    )
    rhs_received = swapped(rhs_send, 2)
    ghosts = side_message[WIDE:]
    side_half = ghost_step(agg_of, d_high, d_low, ghosts, swapped(ghosts, 1))
    side_received = [swapped(part, 2) for part in side_half]
    first = first_correction(rhs_keep, rhs_received, weight)
    near, far = from_neighbours(first)
    send, side_received = lax.optimization_barrier((send, side_received))
    base = base_step(smoother, message, keep, swapped(send, 2))
    *coarse, mine_high, mine_low = coarse_half(
        own_half, own_received, side_half, side_received, rt_high, rt_low
    )
    coarse_other = [swapped(region, 1) for region in coarse]
    near, far, coarse_other = lax.optimization_barrier((near, far, coarse_other))
    correction = sweep((mine_high, mine_low, *coarse_other), first, weight, near, first, far)
    coarse_op, other_high, other_low = coarse_share(coarse, coarse_other)
    lift = lift_half(agg_of, own_half, own_received, side_half, side_received, smoother, prolong)
    for index in range(1, COARSE_SWEEPS - 1):
        near, far = from_neighbours(correction)
        if index == 1:
            shadowed = (near, far, lift, base, other_high, other_low)
            near, far, lift, base, other_high, other_low = lax.optimization_barrier(shadowed)
        operators = (mine_high, mine_low, other_high, other_low)
        correction = sweep(operators, first, weight, near, correction, far)
    lift_other = swapped(lift, 1)
    near, far = from_neighbours(correction)
    base, w_high, w_low = lifted(lift, lift_other, base, correction)
    solution = last_step(w_high, w_low, base, near, far)
    return coarse_op, solution.reshape(ROWS, DOF, COLS)


def solution(mesh):
    placed_args = (
        P("slab", "sub", None, None),
        P("slab", None, None),
        P("slab", None, None),
        P("slab", None, None),
        P(),
        P("slab", "sub"),
        P(),
        P(),
    )
    return jax.shard_map(
        per_device,
        mesh=mesh,
        in_specs=placed_args,
        out_specs=(P("slab", "sub", None, None), P("slab", None, "sub")),
        check_vma=False,
    )
```
